128 devices in a mesh: gx: 8 (over y, core), gy: 16 (over x, z).
Axes of the slice: x: 4, y: 4, z: 4, core: 2. Of those that a mesh axis runs over, the one named last changes fastest.
Arguments:
- coefficients: float32 [13, 56, 32768], P(None, None, ('gx', 'gy')), may hold values from -6 to 6
- jacobian: float32 [3, 3, 32768], P(None, None, ('gx', 'gy')), may hold values from -1 to 1
- face_normals: float32 [4, 3, 32768], P(None, None, ('gx', 'gy')), may hold values from -3 to 3
- wave_speed: float32 [32768], P(('gx', 'gy')), may hold values from 0.3 to 1.5
- star_mats: float32 [3, 13, 13], replicated, may hold values from -1.75 to 1.75
- deriv_mats: float32 [3, 56, 56], replicated, may hold values from -0.75 to 0.75
- stiff_mats: float32 [3, 56, 56], replicated, may hold values from -0.75 to 0.75
- source_mat: float32 [13, 13], replicated, may hold values from -4 to 4
- trace_mats: float32 [4, 21, 56], replicated, may hold values from -0.75 to 0.75
- lift_mats: float32 [4, 56, 21], replicated, may hold values from -1.25 to 1.25
- face_partner: int32 [4, 32768], P(None, ('gx', 'gy')), may hold values from -1 to 1535, as said below
- send_faces: int32 [8, 8192], P(None, ('gx', 'gy')), may hold values from 0 to 1023, as said below
- sea_face: int32 [32768], P(('gx', 'gy')), may hold values from 0 to 1023
- sea_row: int32 [32768, 1], P(('gx', 'gy')), may hold values from 0 to 15; in each aligned block of 256 rows (0 to 255, 256 to 511, ...) at most 64 rows name the same one
- sea_base: int32 [32768, 2], P(('gx', 'gy')), may hold values from 0 to 252
- interp_mat: float32 [16, 21], replicated, may hold values from -1.25 to 1.25
- water_depth: float32 [2048, 4096], P('gx', 'gy'), may hold values from 0.6 to 1.4
- momentum: float32 [2, 2048, 4096], P(None, 'gx', 'gy'), may hold values from -0.5 to 0.5
- bottom: float32 [2048, 4096], P('gx', 'gy'), may hold values from -0.3 to 0.3
Outputs:
- solid_final: float32 [13, 56, 32768], P(None, None, ('gx', 'gy'))
- ocean_final: float32 [3, 2048, 4096], P(None, 'gx', 'gy')
- bed_final: float32 [2048, 4096], P('gx', 'gy')
The draws below stay inside these ranges and needn't reach their ends.
Inputs may be any that keep to these rules, and one draw needn't show every extreme that they name: `face_partner`: for each face of a device's elements: -1 on the domain's outer boundary, a code below 1024 naming a face of the same device, or 1024 + k * 64 + s for the face paired with the neighbouring device at offset k in slot s. Pairings are symmetric; a device shares exactly 64 faces with each neighbour that exists on the device grid. `send_faces`: entry (k, s) of a device is the code f * 256 + e of its face paired in slot s with the neighbouring device at offset k; the 512 codes of a device are distinct. `sea_row`: among the rows of one device no tile row is named more than 64 times.
All inputs are finite; a program needn't handle non-finite values.
Results may differ from the reference program's by a relative error of at most 0.0001.
Values sent between devices are 32-bit elements; how exact they have to be, the bound alone decides.
A program may use at most 64 MiB of HBM per device.

```python
import math
import jax
import jax.numpy as jnp
import numpy as np
from jax import lax

FIELDS = 13
BASIS = 56
FACE_BASIS = 21
POINTS = 16
ORD = 3
STEPS_DG = 2
STEPS_OCEAN = 2
CAP = 64
E_DEV = 256
SEA = 256
TILE_X = 256
TILE_Y = 256
S_FACE = 64
E_TOTAL = 32768
NX_OCEAN = 2048
NY_OCEAN = 4096
N_GX = 8
N_GY = 16
DEVICES = 128


offset_x = [-1, -1, -1, 0, 0, 1, 1, 1]


offset_y = [-1, 0, 1, -1, 1, -1, 0, 1]


def mesh_tables(key):
    face_count = 4 * E_DEV
    shift_x = jnp.array(offset_x, jnp.int32)
    shift_y = jnp.array(offset_y, jnp.int32)

    def one_device(device):
        subkey = jax.random.fold_in(key, device)
        rank_order = jax.random.permutation(subkey, face_count).astype(jnp.int32)
        anchor = jax.random.randint(jax.random.fold_in(subkey, 1), (), 0, 8 * S_FACE)
        rank_order = (rank_order + (face_count - 1 - rank_order[anchor])) % face_count
        places = jnp.arange(face_count, dtype=jnp.int32)
        direction = jnp.minimum(places // S_FACE, 7)
        grid_row = device // N_GY + shift_x[direction]
        grid_column = device % N_GY + shift_y[direction]
        inside = (grid_row >= 0) & (grid_row < N_GX) & (grid_column >= 0) & (grid_column < N_GY)
        paired = rank_order[jnp.bitwise_xor(places, 1)]
        values = jnp.where(places < 8 * S_FACE, jnp.where(inside, face_count + places, -1), paired)
        face_codes = jnp.zeros((face_count,), jnp.int32).at[rank_order].set(values)
        return (face_codes.reshape(4, E_DEV), rank_order[:8 * S_FACE].reshape(8, S_FACE))
    face_codes, send_lists = jax.vmap(one_device)(jnp.arange(DEVICES, dtype=jnp.int32))
    partner_table = face_codes.transpose(1, 0, 2).reshape(4, DEVICES * E_DEV)
    send_table = send_lists.transpose(1, 0, 2).reshape(8, DEVICES * S_FACE)
    return (partner_table, send_table)


def draw_face_partner(key, part):
    return mesh_tables(jax.random.fold_in(key, 7))[0]


def draw_send_faces(key, part):
    return mesh_tables(jax.random.fold_in(key, 7))[1]


def with_ends(entries, stream_key, smallest, largest):
    extent = entries.shape
    index_at = [jax.random.randint(jax.random.fold_in(stream_key, axis), (), 0, extent[axis]) for axis in range(len(extent))]
    entries = entries.at[tuple(index_at)].set(smallest)
    longest = extent.index(max(extent))
    index_at[longest] = (index_at[longest] + 1) % extent[longest]
    return entries.at[tuple(index_at)].set(largest)


def levels(own_key, extent, cuts, low, largest):
    level = 1.0
    for axis_at, blocks in cuts:
        draws = jax.random.uniform(jax.random.fold_in(jax.random.fold_in(own_key, 6), axis_at), (blocks,), jnp.float32, low / len(cuts), largest / len(cuts))
        level = level * jnp.repeat(jnp.exp(draws), extent[axis_at] // blocks).reshape((-1,) + (1,) * (len(extent) - 1 - axis_at))
    return level


def deal_out(rng, own, number, rows, count, top, limit, lean):
    ranking = jax.random.permutation(rng, count)
    crowded, usual = portions_of(count, rows * top, limit, lean, True), portions_of(count, rows * top, limit, lean, False)
    places = jnp.arange(count)

    def named(sizes, turn):
        used = int((sizes > 0).sum())
        fixed = max(1, used // 4)
        passed = fixed + (places - fixed + turn * (used - fixed)) % max(1, count - fixed)
        return jnp.zeros((count,), jnp.int32).at[ranking[jnp.where(places < fixed, places, passed)]].set(jnp.asarray(sizes, jnp.int32))

    sizes = jnp.where(number % 4 == 0, named(crowded, number // 4), named(usual, number - number // 4 - 1))
    mixed = jax.random.permutation(jax.random.fold_in(own, 3), count)
    donor, taker = mixed[0:count // 2 * 2:2], mixed[1:count // 2 * 2:2]
    slack = jnp.minimum(sizes[donor] - 1, limit - sizes[taker]) // 2
    slack = jnp.where((donor == ranking[0]) | (taker == ranking[0]) | (sizes[taker] == 0), 0, jnp.maximum(slack, 0))
    passed = jax.random.randint(jax.random.fold_in(own, 4), (count // 2,), 0, 1 << 20) % (slack + 1)
    sizes = sizes.at[donor].add(-passed).at[taker].add(passed)
    items = jnp.searchsorted(jnp.cumsum(sizes), jnp.arange(rows * top), side="right").astype(jnp.int32)
    table = items.reshape(top, rows).T
    table = table[jax.random.permutation(jax.random.fold_in(own, 1), rows)]
    turn = jax.random.randint(jax.random.fold_in(own, 2), (rows, 1), 0, top)
    return jnp.take_along_axis(table, (jnp.arange(top)[None, :] + turn) % top, axis=1)


def portions_of(count, total, limit, slope, full):
    loads = [(1 << 20) // math.isqrt(rank ** slope) + 1 for rank in range(1, count + 1)]
    largest = limit if full else min(limit, max(-(-total // count), total * loads[0] // sum(loads)))
    least = 1 if total - largest >= count - 1 else 0
    counts, rest = [largest] + [least] * (count - 1), total - largest - least * (count - 1)
    while rest > 0:
        movable = [i for i in range(1, count) if counts[i] < largest] or [i for i in range(1, count) if counts[i] < limit]
        pool, left = sum([loads[i] for i in movable]), rest
        for i in movable:
            extra = min(limit - counts[i], max(1, left * loads[i] // pool), rest)
            counts[i] = counts[i] + extra
            rest = rest - extra
    return np.array(counts)


def bell_draw(key, dims, scale, bound, split=(), kind=jnp.bfloat16):
    drawn = jax.random.normal(key, dims, jnp.float32) * scale
    if len(split) > 0:
        drawn = levels(key, dims, split, -0.22, 0.18) * drawn
    return jnp.clip(drawn, min=-bound, max=bound).astype(kind)


def setup_inputs(seed: int = 0) -> dict:
    keys = jax.random.split(jax.random.key(seed), 20)
    coefficients = bell_draw(keys[0], (FIELDS, BASIS, E_TOTAL), 1.0, 6.0, ((2, 128),), jnp.float32)
    jacobian = jnp.clip(jax.random.uniform(keys[1], (3, 3, E_TOTAL), jnp.float32, -1.0, 1.0) * levels(keys[1], (3, 3, E_TOTAL), ((2, 128),), -0.4, 0.0), -1.0, 1.0)
    face_normals = bell_draw(keys[2], (4, 3, E_TOTAL), 0.5, 3.0, ((2, 128),), jnp.float32)
    wave_speed = jnp.clip(jnp.exp(math.log(1.5) - 1.60943787 * jax.random.uniform(keys[3], (E_TOTAL,), jnp.float32) ** levels(keys[3], (E_TOTAL,), ((0, 128),), -0.2, 0.2)), 0.3, 1.5)
    star_mats = bell_draw(keys[4], (3, FIELDS, FIELDS), FIELDS ** -0.5, 1.75, (), jnp.float32)
    deriv_mats = bell_draw(keys[5], (3, BASIS, BASIS), BASIS ** -0.5, 0.75, (), jnp.float32)
    stiff_mats = bell_draw(keys[6], (3, BASIS, BASIS), BASIS ** -0.5, 0.75, (), jnp.float32)
    source_mat = bell_draw(keys[7], (FIELDS, FIELDS), 0.8, 4.0, (), jnp.float32)
    trace_mats = bell_draw(keys[8], (4, FACE_BASIS, BASIS), BASIS ** -0.5, 0.75, (), jnp.float32)
    lift_mats = bell_draw(keys[9], (4, BASIS, FACE_BASIS), FACE_BASIS ** -0.5, 1.25, (), jnp.float32)
    face_partner = draw_face_partner(jax.random.fold_in(keys[19], 71), 0)
    send_faces = draw_send_faces(jax.random.fold_in(keys[19], 71), 0)
    sea_face = with_ends(jax.random.randint(keys[12], (SEA * DEVICES,), 0, 4 * E_DEV), jax.random.fold_in(keys[12], 1), 0, (4 * E_DEV) - 1).astype(jnp.int32)
    sea_row_keys = jax.random.split(jax.random.fold_in(keys[13], 1), (SEA * DEVICES) // SEA)
    sea_row_turns = jax.random.permutation(jax.random.fold_in(keys[13], 3), (SEA * DEVICES) // SEA)
    sea_row = jax.vmap(lambda own, number: deal_out(jax.random.fold_in(keys[13], 2), own, number, SEA, N_GY, 1, CAP, 2))(sea_row_keys, sea_row_turns).reshape((SEA * DEVICES, 1))
    sea_base = with_ends(jax.random.randint(keys[14], (SEA * DEVICES, 2), 0, min(TILE_X, TILE_Y) - 3), jax.random.fold_in(keys[14], 1), 0, (min(TILE_X, TILE_Y) - 3) - 1).astype(jnp.int32)
    interp_mat = bell_draw(keys[15], (POINTS, FACE_BASIS), FACE_BASIS ** -0.5, 1.25, (), jnp.float32)
    water_depth = jnp.clip(0.6 + 0.79999995 * jax.random.uniform(keys[16], (NX_OCEAN, NY_OCEAN), jnp.float32) ** levels(keys[16], (NX_OCEAN, NY_OCEAN), ((0, 8), (1, 16)), -0.2, 0.2), 0.6, 1.4)
    momentum = bell_draw(keys[17], (2, NX_OCEAN, NY_OCEAN), 0.1, 0.5, ((1, 8), (2, 16)), jnp.float32)
    bottom = jnp.clip(jax.random.uniform(keys[18], (NX_OCEAN, NY_OCEAN), jnp.float32, -0.3, 0.3) * levels(keys[18], (NX_OCEAN, NY_OCEAN), ((0, 8), (1, 16)), -0.4, 0.0), -0.3, 0.3)
    return dict(coefficients=coefficients, jacobian=jacobian, face_normals=face_normals, wave_speed=wave_speed, star_mats=star_mats, deriv_mats=deriv_mats, stiff_mats=stiff_mats, source_mat=source_mat, trace_mats=trace_mats, lift_mats=lift_mats, face_partner=face_partner, send_faces=send_faces, sea_face=sea_face, sea_row=sea_row, sea_base=sea_base, interp_mat=interp_mat, water_depth=water_depth, momentum=momentum, bottom=bottom)


highest = lax.Precision.HIGHEST
step_solid = 0.4
step_ocean = 0.2
depth_floor = 0.5
vertical_field = 6
patch_side = 4
offset_x = [-1, -1, -1, 0, 0, 1, 1, 1]
offset_y = [-1, 0, 1, -1, 1, -1, 0, 1]

def derivative(coeffs, jacobian, star_mats, deriv_mats, source_mat):
    spatial = jnp.einsum('dlk,gke->dgle', deriv_mats, coeffs, precision=highest)
    combined = jnp.einsum('dce,dgle->cgle', jacobian, spatial, precision=highest)
    mixed = jnp.einsum('cgh,chle->gle', star_mats, combined, precision=highest)
    return -mixed - jnp.einsum('gh,hle->gle', source_mat, coeffs, precision=highest)

def volume_term(integral, jacobian, star_mats, stiff_mats):
    spatial = jnp.einsum('dlk,gke->dgle', stiff_mats, integral, precision=highest)
    combined = jnp.einsum('dce,dgle->cgle', jacobian, spatial, precision=highest)
    return jnp.einsum('cgh,chle->gle', star_mats, combined, precision=highest)

def time_integral(coeffs, jacobian, star_mats, deriv_mats, source_mat):
    integral = step_solid * coeffs
    current = coeffs
    factor = step_solid
    for order in range(1, ORD):
        current = derivative(current, jacobian, star_mats, deriv_mats, source_mat)
        factor = factor * step_solid / (order + 1)
        integral = integral + factor * current
    return integral

def face_traces(integral, trace_mats):
    return jnp.einsum('fml,gle->gmfe', trace_mats, integral, precision=highest)

def face_update(coeffs, integral, jacobian, normals, speed, inner, outer, star_mats, stiff_mats, lift_mats):
    sum_term = inner + outer
    jump_term = inner - outer
    rotated = jnp.einsum('cgh,hmfe->cgmfe', star_mats, sum_term, precision=highest)
    numeric_flux = 0.5 * jnp.einsum('fce,cgmfe->gmfe', normals, rotated, precision=highest) + 0.5 * speed * jump_term
    lifted = jnp.einsum('flm,gmfe->gle', lift_mats, numeric_flux, precision=highest)
    return coeffs + volume_term(integral, jacobian, star_mats, stiff_mats) - lifted

def partner_columns(face_partner, send_faces):
    devices = N_GX * N_GY
    elements_all = devices * E_DEV
    shift_x = jnp.array(offset_x, jnp.int32)
    shift_y = jnp.array(offset_y, jnp.int32)
    face_codes = face_partner.reshape(4, devices, E_DEV)
    device_ids = jnp.arange(devices, dtype=jnp.int32)[None, :, None]
    local_column = face_codes // E_DEV * elements_all + device_ids * E_DEV + face_codes % E_DEV
    relative = jnp.maximum(face_codes - 4 * E_DEV, 0)
    direction = jnp.minimum(relative // S_FACE, 7)
    slot_index = relative % S_FACE
    neighbour = (device_ids // N_GY + shift_x[direction]) * N_GY + device_ids % N_GY + shift_y[direction]
    neighbour = jnp.clip(neighbour, 0, devices - 1)
    send_lists = send_faces.reshape(8, devices, S_FACE)
    their_code = send_lists[7 - direction, neighbour, slot_index]
    remote_column = their_code // E_DEV * elements_all + neighbour * E_DEV + their_code % E_DEV
    columns = jnp.where(face_codes < 0, 4 * elements_all, jnp.where(face_codes < 4 * E_DEV, local_column, remote_column))
    return columns.transpose(1, 0, 2)

def solid_step(coeffs, jacobian, face_normals, wave_speed, columns, star_mats, deriv_mats, stiff_mats, source_mat, trace_mats, lift_mats):
    devices = N_GX * N_GY
    width = FIELDS * FACE_BASIS
    blocks = coeffs.reshape(FIELDS, BASIS, devices, E_DEV).transpose(2, 0, 1, 3)
    jac_blocks = jacobian.reshape(3, 3, devices, E_DEV).transpose(2, 0, 1, 3)
    normal_blocks = face_normals.reshape(4, 3, devices, E_DEV).transpose(2, 0, 1, 3)
    speed_blocks = wave_speed.reshape(devices, E_DEV)

    def integrate(pair):
        integral = time_integral(pair[0], pair[1], star_mats, deriv_mats, source_mat)
        return (integral, face_traces(integral, trace_mats))
    integrals, traces = lax.map(integrate, (blocks, jac_blocks))
    table = traces.transpose(1, 2, 3, 0, 4).reshape(width, 4 * devices * E_DEV)
    table = jnp.concatenate([table, jnp.zeros((width, 1), table.dtype)], axis=1)

    def update(pack):
        block, integral, jac_block, normal_block, speed_block, column_block, inner = pack
        outer = table[:, column_block.reshape(-1)].reshape(FIELDS, FACE_BASIS, 4, E_DEV)
        return face_update(block, integral, jac_block, normal_block, speed_block, inner, outer, star_mats, stiff_mats, lift_mats)
    new_blocks = lax.map(update, (blocks, integrals, jac_blocks, normal_blocks, speed_blocks, columns, traces))
    return new_blocks.transpose(1, 2, 0, 3).reshape(FIELDS, BASIS, devices * E_DEV)

def seafloor_forcing(coeffs, sea_face, sea_row, sea_base, trace_mats, interp_mat):
    devices = N_GX * N_GY
    elements_all = devices * E_DEV
    vertical = coeffs[vertical_field]
    sea_traces = jnp.einsum('fml,le->mfe', trace_mats, vertical, precision=highest).reshape(FACE_BASIS, 4 * elements_all)
    owner = jnp.arange(SEA * devices, dtype=jnp.int32) // SEA
    column = sea_face // E_DEV * elements_all + owner * E_DEV + sea_face % E_DEV
    rates = jnp.dot(interp_mat, sea_traces[:, column], precision=highest)
    points = jnp.arange(POINTS, dtype=jnp.int32)
    cell_x = (owner // N_GY * TILE_X + sea_base[:, 0])[None, :] + (points // patch_side)[:, None]
    cell_y = (sea_row[:, 0] * TILE_Y + sea_base[:, 1])[None, :] + (points % patch_side)[:, None]
    return jnp.zeros((TILE_X * N_GX, TILE_Y * N_GY), rates.dtype).at[cell_x, cell_y].add(rates)

def ocean_update(padded):
    height, mom_x, mom_y, bed = (padded[0], padded[1], padded[2], padded[3])
    safe = jnp.maximum(height, depth_floor)
    vel_x = mom_x / safe
    vel_y = mom_y / safe
    celerity = jnp.sqrt(safe)
    speed_x = jnp.abs(vel_x) + celerity
    speed_y = jnp.abs(vel_y) + celerity
    conserved = (height, mom_x, mom_y)
    flux_x = (mom_x, mom_x * vel_x + 0.5 * height * height, mom_y * vel_x)
    flux_y = (mom_y, mom_x * vel_y, mom_y * vel_y + 0.5 * height * height)
    wave_x = jnp.maximum(speed_x[:-1, 1:-1], speed_x[1:, 1:-1])
    wave_y = jnp.maximum(speed_y[1:-1, :-1], speed_y[1:-1, 1:])
    results = []
    for index in range(3):
        state_now = conserved[index]
        face_x = 0.5 * (flux_x[index][:-1, 1:-1] + flux_x[index][1:, 1:-1]) - 0.5 * wave_x * (state_now[1:, 1:-1] - state_now[:-1, 1:-1])
        face_y = 0.5 * (flux_y[index][1:-1, :-1] + flux_y[index][1:-1, 1:]) - 0.5 * wave_y * (state_now[1:-1, 1:] - state_now[1:-1, :-1])
        results.append(state_now[1:-1, 1:-1] - step_ocean * (face_x[1:] - face_x[:-1] + face_y[:, 1:] - face_y[:, :-1]))
    inner_height = height[1:-1, 1:-1]
    slope_x = 0.5 * (bed[2:, 1:-1] - bed[:-2, 1:-1])
    slope_y = 0.5 * (bed[1:-1, 2:] - bed[1:-1, :-2])
    return (results[0], results[1] - step_ocean * inner_height * slope_x, results[2] - step_ocean * inner_height * slope_y)

def reference(coefficients, jacobian, face_normals, wave_speed, star_mats, deriv_mats, stiff_mats, source_mat, trace_mats, lift_mats, face_partner, send_faces, sea_face, sea_row, sea_base, interp_mat, water_depth, momentum, bottom):
    columns = partner_columns(face_partner, send_faces)
    state = coefficients
    for section in range(STEPS_DG):
        state = solid_step(state, jacobian, face_normals, wave_speed, columns, star_mats, deriv_mats, stiff_mats, source_mat, trace_mats, lift_mats)
    forcing = seafloor_forcing(state, sea_face, sea_row, sea_base, trace_mats, interp_mat)
    height = water_depth
    mom_x = momentum[0]
    mom_y = momentum[1]
    bed = bottom
    for section in range(STEPS_OCEAN):
        bed = bed + step_ocean * forcing
        stacked = jnp.stack([height, mom_x, mom_y, bed])
        padded = jnp.pad(stacked, ((0, 0), (1, 1), (1, 1)))
        height, mom_x, mom_y = ocean_update(padded)
    return (state, jnp.stack([height, mom_x, mom_y]), bed)
```

```python
import functools

import jax
import jax.numpy as jnp
from jax import lax
from jax.experimental import pallas as pl
from jax.experimental.pallas import tpu as pltpu
from jax.sharding import PartitionSpec as P

MESH = pl.DeviceIdType.MESH
F32 = jnp.float32
BF16 = jnp.bfloat16

FIELDS = 13
BASIS = 56
FACE_BASIS = 21
CAP = 64
ELEMENTS = 256
SIDE = 256
STEPS_DG = 2

step_solid = 0.4
step_ocean = 0.2
depth_floor = 0.5
vertical_field = 6

OFFSETS = [(-1, -1), (-1, 0), (-1, 1), (0, -1), (0, 1), (1, -1), (1, 0), (1, 1)]
ROWS = 320
HALF = ROWS // 2
EXT_X = SIDE + 16
EXT_Y = SIDE + 128


def mm(a, b):
    return jnp.dot(a, b, preferred_element_type=F32)


def mm_nt(a, b):
    return lax.dot_general(a, b, (((1,), (1,)), ((), ())), preferred_element_type=F32)


def halves(x):
    high = x.astype(BF16)
    return high, (x - high.astype(F32)).astype(BF16)


def triple(x):
    high = x.astype(BF16).astype(F32)
    return jnp.concatenate([high, x - high, high], axis=0).astype(BF16)


def one_hot(index_row, rows):
    iota = lax.broadcasted_iota(jnp.int32, (rows, index_row.shape[1]), 0)
    return jnp.where(iota == index_row, 1.0, 0.0).astype(BF16)


def low_lanes(shape):
    return lax.broadcasted_iota(jnp.int32, shape, len(shape) - 1) < 64


def swap_lanes(x):
    return pltpu.roll(x, 64, x.ndim - 1)


def solid_kernel(
    n_gx, n_gy,
    coef, jac, nrm, spd, dcat, scat, tcat, lift1, lift2, vcat, kron, partner, send, sea, sea_col,
    depth, mom, bottom,
    solid, ocean_ext, force_ext,
    ddt, integral, mixed, table, tsplit, outer, flux, volume,
    hot_send, hot_local, hot_remote, hot_slot, hot_y,
    msg, got, corner_msg, corner_got, rate_msg, rate_got,
    left_hi, left_lo, force,
    u_top, u_bot, u_strip, u_row_got, u_strip_got, u_corner_got,
    f_strip, f_row_got, f_strip_got, f_corner_got,
    face_send, face_recv, corner_send, corner_recv, rate_send, rate_recv,
    uh_send, uh_recv, fh_send, fh_recv,
):
    gx = lax.axis_index("gx")
    gy = lax.axis_index("gy")

    def at(dx, dy):
        return (lax.rem(gx + dx + n_gx, n_gx), lax.rem(gy + dy + n_gy, n_gy))

    barrier = pltpu.get_barrier_semaphore()
    peers = [at(dx, dy) for dx, dy in OFFSETS] + [at(0, off) for off in range(2, n_gy - 1)]
    for peer in peers:
        pl.semaphore_signal(barrier, inc=1, device_id=peer, device_id_type=MESH)

    def face_copy(step, k):
        return pltpu.make_async_remote_copy(
            src_ref=msg.at[step, k], dst_ref=got.at[step, 7 - k],
            send_sem=face_send.at[step, k], recv_sem=face_recv.at[step, 7 - k],
            device_id=at(*OFFSETS[k]), device_id_type=MESH)

    def face_arrival(step, k):
        return pltpu.make_async_remote_copy(
            src_ref=msg.at[step, k], dst_ref=got.at[step, k],
            send_sem=face_send.at[step, k], recv_sem=face_recv.at[step, k],
            device_id=at(*OFFSETS[k]), device_id_type=MESH)

    def row_copy(source, target, sends, recvs, off):
        there = lax.rem(gy + off, n_gy)
        return pltpu.make_async_remote_copy(
            src_ref=source.at[there], dst_ref=target.at[gy],
            send_sem=sends.at[off - 1], recv_sem=recvs.at[off - 1],
            device_id=(gx, there), device_id_type=MESH)

    def row_arrival(source, target, sends, recvs, off):
        origin = lax.rem(gy - off + n_gy, n_gy)
        return pltpu.make_async_remote_copy(
            src_ref=source.at[origin], dst_ref=target.at[origin],
            send_sem=sends.at[off - 1], recv_sem=recvs.at[off - 1],
            device_id=(gx, origin), device_id_type=MESH)

    def halo_copies(top, bot, strip, rows_got, strips_got, corners_got, sends, recvs):
        sources = [
            top.at[:, :, 0:128], top, top.at[:, :, 128:256], strip, strip,
            bot.at[:, :, 0:128], bot, bot.at[:, :, 128:256]]
        targets = [
            corners_got.at[0], rows_got.at[0], corners_got.at[1], strips_got.at[0],
            strips_got.at[1], corners_got.at[2], rows_got.at[1], corners_got.at[3]]
        return [
            pltpu.make_async_remote_copy(
                src_ref=sources[k], dst_ref=targets[k],
                send_sem=sends.at[k], recv_sem=recvs.at[k],
                device_id=at(*OFFSETS[k]), device_id_type=MESH)
            for k in range(8)]

    for field, ref in enumerate([depth, mom.at[0], mom.at[1], bottom]):
        u_top[field] = ref[0:8, :]
        u_bot[field] = ref[SIDE - 8:SIDE, :]
    pick_row = lax.broadcasted_iota(jnp.int32, (8, SIDE), 0)
    pick_col = lax.broadcasted_iota(jnp.int32, (8, SIDE), 1)
    chosen = jnp.where(pick_row < 4, pick_row, pick_row + (SIDE - 8))
    edge = jnp.where(pick_col == chosen, 1.0, 0.0).astype(BF16)

    def strip_of(x):
        high, low = halves(x)
        rest = (x - high.astype(F32) - low.astype(F32)).astype(BF16)
        return mm_nt(edge, high) + mm_nt(edge, low) + mm_nt(edge, rest)

    for field, ref in enumerate([depth, mom.at[0], mom.at[1], bottom]):
        u_strip[field] = strip_of(ref[...])

    rows = sea_col[...]
    lanes = lax.broadcasted_iota(jnp.int32, (ELEMENTS, 128), 1)
    hits = jnp.where(rows == lanes, 1.0, 0.0)
    tri_r = lax.broadcasted_iota(jnp.int32, (ELEMENTS, ELEMENTS), 0)
    tri_c = lax.broadcasted_iota(jnp.int32, (ELEMENTS, ELEMENTS), 1)
    before = mm(jnp.where(tri_c < tri_r, 1.0, 0.0).astype(BF16), hits.astype(BF16))
    slot = jnp.sum(before * hits, axis=1, keepdims=True).astype(jnp.int32)
    target = rows * CAP + slot
    cells = lax.broadcasted_iota(jnp.int32, (ELEMENTS, n_gy * CAP), 1)
    placed = jnp.where(target == cells, 1.0, 0.0).astype(BF16)
    sea_hi, sea_lo = halves(sea[...])
    where_ = mm(sea_hi, placed) + mm(sea_lo, placed)
    for pair in range(n_gy // 2):
        block = where_[:, pair * 128:(pair + 1) * 128]
        corner_msg[2 * pair] = block
        corner_msg[2 * pair + 1] = swap_lanes(block)

    pl.semaphore_wait(barrier, len(peers))
    uh = halo_copies(u_top, u_bot, u_strip, u_row_got, u_strip_got, u_corner_got, uh_send, uh_recv)
    for copy in uh:
        copy.start()
    for off in range(1, n_gy):
        row_copy(corner_msg, corner_got, corner_send, corner_recv, off).start()
    corner_got[gy] = corner_msg[gy]

    for quarter in range(4):
        index = jnp.concatenate([send[2 * quarter:2 * quarter + 1, :], send[2 * quarter + 1:2 * quarter + 2, :]], axis=1)
        hot_send[:, quarter * 128:(quarter + 1) * 128] = one_hot(index, 4 * ELEMENTS)
    for face in range(4):
        code = partner[face:face + 1, :]
        hot_local[:, face * ELEMENTS:(face + 1) * ELEMENTS] = one_hot(code, 4 * ELEMENTS)
        hot_remote[:, face * ELEMENTS:(face + 1) * ELEMENTS] = one_hot(code - 4 * ELEMENTS, 8 * 64)
    hot_slot[...] = one_hot(where_[0:1, :].astype(jnp.int32) - 1, 4 * ELEMENTS)

    def star(x, groups):
        high, low = halves(x)
        both = mm(kron[:, 0:8 * groups], high)
        return both[0:104] + both[104:208] + mm(kron[0:104, 0:8 * groups], low)

    def directional(source, weights, with_source, store):
        for h in range(FIELDS):
            q = source[h].reshape(BASIS, ELEMENTS)
            spatial = mm(weights[...], triple(q))
            parts = [spatial[d * BASIS:(d + 1) * BASIS] for d in range(3)]
            for c in range(3):
                total = jac[0, c:c + 1, :] * parts[0] + jac[1, c:c + 1, :] * parts[1] + jac[2, c:c + 1, :] * parts[2]
                mixed[:, c * FIELDS + h] = total.reshape(7, 8, ELEMENTS)
            if with_source:
                mixed[:, 3 * FIELDS + h] = source[h]
        groups = 4 * FIELDS if with_source else 3 * FIELDS
        for block in range(7):
            result = star(mixed[block, 0:groups].reshape(8 * groups, ELEMENTS), groups)
            store(block, result.reshape(FIELDS, 8, ELEMENTS))

    first_factor = step_solid * step_solid / 2
    second_factor = first_factor * step_solid / 3
    table[ROWS // 8 - 1] = jnp.zeros((8, 4 * ELEMENTS), F32)

    for step in range(STEPS_DG):
        state = coef if step == 0 else solid

        def store_first(block, value):
            ddt[:, block] = value
        directional(state, dcat, True, store_first)

        def store_second(block, value):
            integral[:, block] = step_solid * state[:, block] - first_factor * ddt[:, block] + second_factor * value
        directional(ddt, dcat, True, store_second)

        for g in range(FIELDS):
            trace = mm(tcat[...], triple(integral[g].reshape(BASIS, ELEMENTS)))
            for face in range(4):
                table[3 * g:3 * g + 3, :, face * ELEMENTS:(face + 1) * ELEMENTS] = (
                    trace[face * 24:(face + 1) * 24].reshape(3, 8, ELEMENTS))
        high, low = halves(table[...].reshape(ROWS, 4 * ELEMENTS))
        tsplit[0:ROWS] = high
        tsplit[ROWS:2 * ROWS] = low

        for half in range(2):
            picked = mm(tsplit[...], hot_send[:, half * 256:(half + 1) * 256])
            picked = picked[0:ROWS] + picked[ROWS:2 * ROWS]
            for pair in range(2):
                block = picked[:, pair * 128:(pair + 1) * 128]
                top, bot = block[0:HALF], block[HALF:ROWS]
                low_side = low_lanes((HALF, 128))
                k = 4 * half + 2 * pair
                msg[step, k] = jnp.where(low_side, top, swap_lanes(bot))
                msg[step, k + 1] = jnp.where(low_side, swap_lanes(top), bot)
                face_copy(step, k).start()
                face_copy(step, k + 1).start()

        for face in range(4):
            cols = slice(face * ELEMENTS, (face + 1) * ELEMENTS)
            local = mm(tsplit[...], hot_local[:, cols])
            outer[:, :, cols] = (local[0:ROWS] + local[ROWS:2 * ROWS]).reshape(ROWS // 8, 8, ELEMENTS)

        def store_volume(block, value):
            volume[:, block] = value
        directional(integral, scat, False, store_volume)

        if step == 0:
            for off in range(1, n_gy):
                row_arrival(corner_msg, corner_got, corner_send, corner_recv, off).wait_recv()
            down = lax.broadcasted_iota(jnp.int32, (SIDE, 128), 0)
            for pair in range(n_gy // 2):
                corner = jnp.where(low_lanes((8, 128)), corner_got[2 * pair], swap_lanes(corner_got[2 * pair + 1]))
                apart = down + 1 - corner[2:3, :].astype(jnp.int32)
                for j in range(4):
                    base = j * n_gy * CAP + pair * 128
                    hot_y[:, base:base + 128] = jnp.where(apart == j, 1.0, 0.0).astype(BF16)

        for k in range(8):
            face_arrival(step, k).wait_recv()
        low_side = low_lanes((HALF, 128))
        for pair in range(4):
            a, b = got[step, 2 * pair], got[step, 2 * pair + 1]
            top = jnp.where(low_side, a, swap_lanes(b))
            bot = jnp.where(low_side, swap_lanes(a), b)
            cols = slice(pair * 128, (pair + 1) * 128)
            high, low = halves(top)
            tsplit[0:HALF, cols] = high
            tsplit[ROWS:ROWS + HALF, cols] = low
            high, low = halves(bot)
            tsplit[HALF:ROWS, cols] = high
            tsplit[ROWS + HALF:2 * ROWS, cols] = low
        for face in range(4):
            cols = slice(face * ELEMENTS, (face + 1) * ELEMENTS)
            remote = mm(tsplit[:, 0:512], hot_remote[:, cols])
            remote = (remote[0:ROWS] + remote[ROWS:2 * ROWS]).reshape(ROWS // 8, 8, ELEMENTS)
            for block in range(3):
                ids = [3 * g + block for g in range(FIELDS)]
                inside = jnp.concatenate([table[i, :, cols] for i in ids], axis=0)
                outside = jnp.concatenate([outer[i, :, cols] + remote[i] for i in ids], axis=0)
                total = inside + outside
                stack = jnp.concatenate([(0.5 * nrm[face, c:c + 1, :]) * total for c in range(3)], axis=0)
                value = star(stack, 3 * FIELDS) + (0.5 * spd[...]) * (inside - outside)
                flux[:, face, block] = value.reshape(FIELDS, 8, ELEMENTS)
        for g in range(FIELDS):
            f = flux[g].reshape(96, ELEMENTS)
            high = f.astype(BF16).astype(F32)
            both = jnp.concatenate([high, f - high], axis=0).astype(BF16)
            lifted = mm(lift1[...], both) + mm(lift2[...], both[0:96])
            solid[g] = state[g] + volume[g] - lifted.reshape(7, 8, ELEMENTS)

    point = mm(vcat[...], triple(solid[vertical_field].reshape(BASIS, ELEMENTS)))
    points = jnp.concatenate([point[16 * f:16 * f + 16] for f in range(4)], axis=1)
    high = points.astype(BF16).astype(F32)
    both = jnp.concatenate([high, points - high], axis=0).astype(BF16)
    rates = mm(both, hot_slot[...])
    rates = rates[0:16] + rates[16:32]
    low_side = low_lanes((8, 128))
    for pair in range(n_gy // 2):
        a = rates[0:8, pair * 128:(pair + 1) * 128]
        b = rates[8:16, pair * 128:(pair + 1) * 128]
        rate_msg[2 * pair] = jnp.where(low_side, a, swap_lanes(b))
        rate_msg[2 * pair + 1] = jnp.where(low_side, swap_lanes(a), b)
    for off in range(1, n_gy):
        row_copy(rate_msg, rate_got, rate_send, rate_recv, off).start()
    rate_got[gy] = rate_msg[gy]

    up_in = gx > 0
    down_in = gx < n_gx - 1
    left_in = gy > 0
    right_in = gy < n_gy - 1

    def place(target, centre, rows_got, strips_got, corners_got, fields):
        side = low_lanes((8, 128))
        for field in range(fields):
            target[field, 8:8 + SIDE, 0:SIDE] = centre(field)
            target[field, 0:8, 0:SIDE] = jnp.where(up_in, rows_got[1, field], 0.0)
            target[field, 8 + SIDE:EXT_X, 0:SIDE] = jnp.where(down_in, rows_got[0, field], 0.0)
            strip = jnp.concatenate([
                jnp.where(right_in, strips_got[0, field], 0.0), jnp.zeros((112, SIDE), F32),
                jnp.where(left_in, strips_got[1, field], 0.0)], axis=0)
            target[field, 8:8 + SIDE, SIDE:EXT_Y] = jnp.transpose(strip)
            target[field, 0:8, SIDE:EXT_Y] = jnp.where(
                side, jnp.where(up_in & right_in, corners_got[2, field], 0.0),
                jnp.where(up_in & left_in, corners_got[3, field], 0.0))
            target[field, 8 + SIDE:EXT_X, SIDE:EXT_Y] = jnp.where(
                side, jnp.where(down_in & right_in, corners_got[0, field], 0.0),
                jnp.where(down_in & left_in, corners_got[1, field], 0.0))

    for copy in uh:
        copy.wait_recv()
    inputs = [depth, mom.at[0], mom.at[1], bottom]
    place(ocean_ext, lambda field: inputs[field][...], u_row_got, u_strip_got, u_corner_got, 4)

    for off in range(1, n_gy):
        row_arrival(rate_msg, rate_got, rate_send, rate_recv, off).wait_recv()
    down = lax.broadcasted_iota(jnp.int32, (SIDE, 128), 0)
    for pair in range(n_gy // 2):
        corner = jnp.where(low_side, corner_got[2 * pair], swap_lanes(corner_got[2 * pair + 1]))
        apart = down + 1 - corner[1:2, :].astype(jnp.int32)
        a, b = rate_got[2 * pair], rate_got[2 * pair + 1]
        first = jnp.where(low_side, a, swap_lanes(b))
        second = jnp.where(low_side, swap_lanes(a), b)
        masks = [apart == i for i in range(4)]
        for j in range(4):
            value = jnp.where(
                masks[0], first[j:j + 1], jnp.where(
                    masks[1], first[4 + j:5 + j], jnp.where(
                        masks[2], second[j:j + 1], jnp.where(masks[3], second[4 + j:5 + j], 0.0))))
            base = j * n_gy * CAP + pair * 128
            high, low = halves(value)
            left_hi[:, base:base + 128] = high
            left_lo[:, base:base + 128] = low
    field = mm_nt(left_hi[...], hot_y[...]) + mm_nt(left_lo[...], hot_y[...])
    force[0] = field
    f_strip[0] = strip_of(field)
    fh = halo_copies(
        force.at[:, 0:8], force.at[:, SIDE - 8:SIDE], f_strip,
        f_row_got, f_strip_got, f_corner_got, fh_send, fh_recv)
    for copy in fh:
        copy.start()
    for copy in fh:
        copy.wait_recv()
    place(force_ext, lambda _: field, f_row_got, f_strip_got, f_corner_got, 1)

    for copy in uh + fh:
        copy.wait_send()
    for off in range(1, n_gy):
        row_copy(corner_msg, corner_got, corner_send, corner_recv, off).wait_send()
        row_copy(rate_msg, rate_got, rate_send, rate_recv, off).wait_send()
    for step in range(STEPS_DG):
        for k in range(8):
            face_copy(step, k).wait_send()


def ocean_kernel(n_gx, n_gy, ext, force, ocean, bed, work):
    gx = lax.axis_index("gx")
    gy = lax.axis_index("gy")
    slab = 32

    def update(height, mom_x, mom_y, b):
        safe = jnp.maximum(height, depth_floor)
        inv = 1.0 / safe
        vel_x = mom_x * inv
        vel_y = mom_y * inv
        celerity = jnp.sqrt(safe)
        cross = mom_x * vel_y
        press = 0.5 * height * height
        n = height.shape[0]
        m = height.shape[1]
        fluxes = (
            (0, n, (mom_x, mom_x * vel_x + press, cross), jnp.abs(vel_x) + celerity),
            (1, m, (mom_y, cross, mom_y * vel_y + press), jnp.abs(vel_y) + celerity))
        state = (height, mom_x, mom_y)
        change = [0.0, 0.0, 0.0]
        for axis, size, flux, speed in fluxes:
            wave = jnp.maximum(speed, pltpu.roll(speed, size - 1, axis))
            for i in range(3):
                face = (flux[i] + pltpu.roll(flux[i], size - 1, axis)) - wave * (
                    pltpu.roll(state[i], size - 1, axis) - state[i])
                change[i] = change[i] + (face - pltpu.roll(face, 1, axis))
        half = 0.5 * step_ocean
        slope_x = pltpu.roll(b, n - 1, 0) - pltpu.roll(b, 1, 0)
        slope_y = pltpu.roll(b, m - 1, 1) - pltpu.roll(b, 1, 1)
        return (
            height - half * change[0],
            mom_x - half * (change[1] + height * slope_x),
            mom_y - half * (change[2] + height * slope_y))

    def first(begin, rows, inner_from, inner_to):
        part = pl.ds(begin, rows)
        b = ext[3, part, :] + step_ocean * force[0, part, :]
        result = update(ext[0, part, :], ext[1, part, :], ext[2, part, :], b)
        x = begin + lax.broadcasted_iota(jnp.int32, (rows, EXT_Y), 0)
        y = lax.broadcasted_iota(jnp.int32, (rows, EXT_Y), 1)
        out = ((x < 8) & (gx == 0)) | ((x >= 8 + SIDE) & (gx == n_gx - 1))
        out = out | ((y >= SIDE) & (y < SIDE + 64) & (gy == n_gy - 1)) | ((y >= SIDE + 64) & (gy == 0))
        for i in range(3):
            work[i, pl.ds(begin + inner_from, inner_to - inner_from), :] = jnp.where(
                out, 0.0, result[i])[inner_from:inner_to]

    @pl.loop(0, SIDE // slab)
    def _(s):
        first(pl.multiple_of(s * slab, 8), slab + 16, 8, slab + 8)
    first(0, 16, 0, 8)
    first(EXT_X - 16, 16, 8, 16)

    @pl.loop(0, SIDE // slab)
    def _(s):
        begin = pl.multiple_of(s * slab, 8)
        part = pl.ds(begin, slab + 16)
        b = ext[3, part, :] + (2 * step_ocean) * force[0, part, :]
        result = update(work[0, part, :], work[1, part, :], work[2, part, :], b)
        for i in range(3):
            ocean[i, pl.ds(begin, slab), :] = result[i][8:slab + 8, 0:SIDE]
        bed[pl.ds(begin, slab), :] = b[8:slab + 8, 0:SIDE]


def weight_triple(w):
    high = lax.reduce_precision(w, 8, 7)
    return jnp.concatenate([high, high, w - high], axis=1).astype(BF16)


def per_device(
    n_gx, n_gy,
    coefficients, jacobian, face_normals, wave_speed, star_mats, deriv_mats, stiff_mats, source_mat,
    trace_mats, lift_mats, face_partner, send_faces, sea_face, sea_row, sea_base, interp_mat,
    water_depth, momentum, bottom,
):
    pad = ((0, 0), (0, 24 - FACE_BASIS), (0, 0))
    dcat = weight_triple(deriv_mats.reshape(3 * BASIS, BASIS))
    scat = weight_triple(stiff_mats.reshape(3 * BASIS, BASIS))
    tcat = weight_triple(jnp.pad(trace_mats, pad).reshape(96, BASIS))
    lift = jnp.pad(lift_mats.transpose(0, 2, 1), pad).transpose(2, 0, 1).reshape(BASIS, 96)
    lift_high = lax.reduce_precision(lift, 8, 7)
    lift1 = jnp.concatenate([lift_high, lift_high], axis=1).astype(BF16)
    lift2 = (lift - lift_high).astype(BF16)
    vmat = jnp.einsum("pm,fml->fpl", interp_mat, trace_mats, precision=lax.Precision.HIGHEST)
    vcat = weight_triple(vmat.reshape(64, BASIS))
    stars = jnp.concatenate([star_mats, source_mat[None]], axis=0)
    eye = jnp.eye(8, dtype=F32)
    kron = (stars.transpose(1, 0, 2)[:, None, :, :, None] * eye[None, :, None, None, :]).reshape(104, 416)
    kron_high = lax.reduce_precision(kron, 8, 7)
    kron = jnp.concatenate([kron_high, kron - kron_high], axis=0).astype(BF16)
    sea = jnp.concatenate([
        sea_face[None], sea_base.T, jnp.zeros((5, sea_face.shape[0]), jnp.int32)], axis=0).astype(F32) + 1.0

    vm = pl.BlockSpec(memory_space=pltpu.VMEM)
    slots = n_gy * CAP
    scratch = [
        pltpu.VMEM((FIELDS, 7, 8, ELEMENTS), F32),
        pltpu.VMEM((FIELDS, 7, 8, ELEMENTS), F32),
        pltpu.VMEM((7, 4 * FIELDS, 8, ELEMENTS), F32),
        pltpu.VMEM((ROWS // 8, 8, 4 * ELEMENTS), F32),
        pltpu.VMEM((2 * ROWS, 4 * ELEMENTS), BF16),
        pltpu.VMEM((ROWS // 8, 8, 4 * ELEMENTS), F32),
        pltpu.VMEM((FIELDS, 4, 3, 8, ELEMENTS), F32),
        pltpu.VMEM((FIELDS, 7, 8, ELEMENTS), F32),
        pltpu.VMEM((4 * ELEMENTS, 512), BF16),
        pltpu.VMEM((4 * ELEMENTS, 4 * ELEMENTS), BF16),
        pltpu.VMEM((512, 4 * ELEMENTS), BF16),
        pltpu.VMEM((4 * ELEMENTS, slots), BF16),
        pltpu.VMEM((SIDE, 4 * slots), BF16),
        pltpu.VMEM((STEPS_DG, 8, HALF, 128), F32),
        pltpu.VMEM((STEPS_DG, 8, HALF, 128), F32),
        pltpu.VMEM((n_gy, 8, 128), F32),
        pltpu.VMEM((n_gy, 8, 128), F32),
        pltpu.VMEM((n_gy, 8, 128), F32),
        pltpu.VMEM((n_gy, 8, 128), F32),
        pltpu.VMEM((SIDE, 4 * slots), BF16),
        pltpu.VMEM((SIDE, 4 * slots), BF16),
        pltpu.VMEM((1, SIDE, SIDE), F32),
        pltpu.VMEM((4, 8, SIDE), F32),
        pltpu.VMEM((4, 8, SIDE), F32),
        pltpu.VMEM((4, 8, SIDE), F32),
        pltpu.VMEM((2, 4, 8, SIDE), F32),
        pltpu.VMEM((2, 4, 8, SIDE), F32),
        pltpu.VMEM((4, 4, 8, 128), F32),
        pltpu.VMEM((1, 8, SIDE), F32),
        pltpu.VMEM((2, 1, 8, SIDE), F32),
        pltpu.VMEM((2, 1, 8, SIDE), F32),
        pltpu.VMEM((4, 1, 8, 128), F32),
        pltpu.SemaphoreType.DMA((STEPS_DG, 8)),
        pltpu.SemaphoreType.DMA((STEPS_DG, 8)),
        pltpu.SemaphoreType.DMA((n_gy - 1,)),
        pltpu.SemaphoreType.DMA((n_gy - 1,)),
        pltpu.SemaphoreType.DMA((n_gy - 1,)),
        pltpu.SemaphoreType.DMA((n_gy - 1,)),
        pltpu.SemaphoreType.DMA((8,)),
        pltpu.SemaphoreType.DMA((8,)),
        pltpu.SemaphoreType.DMA((8,)),
        pltpu.SemaphoreType.DMA((8,)),
    ]
    solid, ext, force = pl.pallas_call(
        functools.partial(solid_kernel, n_gx, n_gy),
        out_shape=(
            jax.ShapeDtypeStruct((FIELDS, 7, 8, ELEMENTS), F32),
            jax.ShapeDtypeStruct((4, EXT_X, EXT_Y), F32),
            jax.ShapeDtypeStruct((1, EXT_X, EXT_Y), F32)),
        in_specs=[vm] * 18,
        out_specs=(vm, vm, vm),
        scratch_shapes=scratch,
        compiler_params=pltpu.CompilerParams(
            collective_id=0, has_side_effects=True, vmem_limit_bytes=60 * 1024 * 1024),
        name="solid",
    )(
        coefficients.reshape(FIELDS, 7, 8, ELEMENTS), jacobian, face_normals, wave_speed.reshape(1, ELEMENTS),
        dcat, scat, tcat, lift1, lift2, vcat, kron, face_partner, send_faces, sea, sea_row,
        water_depth, momentum, bottom)
    ocean, bed = pl.pallas_call(
        functools.partial(ocean_kernel, n_gx, n_gy),
        out_shape=(
            jax.ShapeDtypeStruct((3, SIDE, SIDE), F32),
            jax.ShapeDtypeStruct((SIDE, SIDE), F32)),
        in_specs=[vm, vm],
        out_specs=(vm, vm),
        scratch_shapes=[pltpu.VMEM((3, EXT_X, EXT_Y), F32)],
        name="ocean",
    )(ext, force)
    return solid.reshape(FIELDS, BASIS, ELEMENTS), ocean, bed


def solution(mesh):
    in_specs = (
        P(None, None, ("gx", "gy")),
        P(None, None, ("gx", "gy")),
        P(None, None, ("gx", "gy")),
        P(("gx", "gy")),
        P(),
        P(),
        P(),
        P(),
        P(),
        P(),
        P(None, ("gx", "gy")),
        P(None, ("gx", "gy")),
        P(("gx", "gy")),
        P(("gx", "gy"), None),
        P(("gx", "gy"), None),
        P(),
        P("gx", "gy"),
        P(None, "gx", "gy"),
        P("gx", "gy"),
    )
    out_specs = (P(None, None, ("gx", "gy")), P(None, "gx", "gy"), P("gx", "gy"))
    return jax.shard_map(
        functools.partial(per_device, mesh.shape["gx"], mesh.shape["gy"]),
        mesh=mesh, in_specs=in_specs, out_specs=out_specs, check_vma=False,
    )
```

```python
import functools

import jax
import jax.numpy as jnp
from jax import lax
from jax.experimental import pallas as pl
from jax.experimental.pallas import tpu as pltpu
from jax.sharding import PartitionSpec as P

MESH = pl.DeviceIdType.MESH
F32 = jnp.float32
BF16 = jnp.bfloat16

FIELDS = 13
BASIS = 56
FACE_BASIS = 21
CAP = 64
ELEMENTS = 256
SIDE = 256
STEPS_DG = 2

step_solid = 0.4
step_ocean = 0.2
depth_floor = 0.5
vertical_field = 6

OFFSETS = [(-1, -1), (-1, 0), (-1, 1), (0, -1), (0, 1), (1, -1), (1, 0), (1, 1)]
ROWS = 320
HALF = ROWS // 2
EXT_X = SIDE + 16
EXT_Y = SIDE + 128


def mm(a, b):
    return jnp.dot(a, b, preferred_element_type=F32)


def mm_nt(a, b):
    return lax.dot_general(a, b, (((1,), (1,)), ((), ())), preferred_element_type=F32)


def halves(x):
    high = x.astype(BF16)
    return high, (x - high.astype(F32)).astype(BF16)


def triple(x):
    high = x.astype(BF16).astype(F32)
    return jnp.concatenate([high, x - high, high], axis=0).astype(BF16)


def one_hot(index_row, rows):
    iota = lax.broadcasted_iota(jnp.int32, (rows, index_row.shape[1]), 0)
    return jnp.where(iota == index_row, 1.0, 0.0).astype(BF16)


def low_lanes(shape):
    return lax.broadcasted_iota(jnp.int32, shape, len(shape) - 1) < 64


def swap_lanes(x):
    return pltpu.roll(x, 64, x.ndim - 1)


def iota2(shape, axis):
    return lax.broadcasted_iota(jnp.int32, shape, axis)


def bits(condition):
    return jnp.where(condition, 1.0, 0.0).astype(BF16)


def lane_triple(w):
    high, low = halves(w)
    k, n = iota2((BASIS, 3 * BASIS), 0), iota2((BASIS, 3 * BASIS), 1)
    return (mm(high, bits((n == k) | (n == k + BASIS))) + mm(low, bits(n == k + 2 * BASIS))).astype(BF16)


def shallow_update(height, mom_x, mom_y, b, extra=None):
    safe = jnp.maximum(height, depth_floor)
    inv = 1.0 / safe
    vel_x = mom_x * inv
    vel_y = mom_y * inv
    celerity = jnp.sqrt(safe)
    cross = mom_x * vel_y
    press = 0.5 * height * height
    n, m = height.shape
    fluxes = (
        (0, n, (mom_x, mom_x * vel_x + press, cross), jnp.abs(vel_x) + celerity),
        (1, m, (mom_y, cross, mom_y * vel_y + press), jnp.abs(vel_y) + celerity))
    state = (height, mom_x, mom_y)
    change = [0.0, 0.0, 0.0]
    for axis, size, flux, speed in fluxes:
        wave = jnp.maximum(speed, pltpu.roll(speed, size - 1, axis))
        for i in range(3):
            face = (flux[i] + pltpu.roll(flux[i], size - 1, axis)) - wave * (
                pltpu.roll(state[i], size - 1, axis) - state[i])
            change[i] = change[i] + (face - pltpu.roll(face, 1, axis))
    half = 0.5 * step_ocean
    slope_x, slope_y = slopes(b)
    return (
        height - half * change[0],
        mom_x - half * (change[1] + height * slope_x),
        mom_y - half * (change[2] + height * slope_y))


def slopes(b):
    n, m = b.shape
    return (
        pltpu.roll(b, n - 1, 0) - pltpu.roll(b, 1, 0),
        pltpu.roll(b, m - 1, 1) - pltpu.roll(b, 1, 1))


def solid_kernel(
    n_gx, n_gy,
    coef, jac, nrm, spd, deriv, stiff, trace_in, lift_in, interp, stars, source, partner, send,
    sea_face, sea_row, sea_base, depth, mom, bottom,
    solid_out, wave, force_ext,
    solid, sea0, tpad, lpad, ipad, spad, dcat, scat, tcat, vcat, lift1, lift2, kron, rotate1, rotate2,
    ddt, integral, mixed, table, tsplit, outer, flux, volume,
    hot_send, hot_local, hot_remote, hot_slot, hot_x, hot_y,
    msg, got, corner_msg, corner_got, rate_msg, rate_got,
    left_hi, left_lo,
    u_top, u_bot, u_strip, u_row_got, u_strip_got, u_corner_got,
    f_top, f_bot, f_strip, f_row_got, f_strip_got, f_corner_got,
    load_sem, store_sem,
    face_send, face_recv, corner_send, corner_recv, rate_send, rate_recv,
    uh_send, uh_recv, fh_send, fh_recv,
):
    gx = lax.axis_index("gx")
    gy = lax.axis_index("gy")
    slots = n_gy * CAP

    def at(dx, dy):
        return (lax.rem(gx + dx + n_gx, n_gx), lax.rem(gy + dy + n_gy, n_gy))

    barrier = pltpu.get_barrier_semaphore()
    peers = [at(dx, dy) for dx, dy in OFFSETS] + [at(0, off) for off in range(2, n_gy - 1)]
    for peer in peers:
        pl.semaphore_signal(barrier, inc=1, device_id=peer, device_id_type=MESH)

    loads = [
        pltpu.make_async_copy(depth, sea0.at[0], load_sem.at[0]),
        pltpu.make_async_copy(mom, sea0.at[1:3], load_sem.at[1]),
        pltpu.make_async_copy(bottom, sea0.at[3], load_sem.at[2])]
    for copy in loads:
        copy.start()

    def face_copy(step, k):
        return pltpu.make_async_remote_copy(
            src_ref=msg.at[step, k], dst_ref=got.at[step, 7 - k],
            send_sem=face_send.at[step, k], recv_sem=face_recv.at[step, 7 - k],
            device_id=at(*OFFSETS[k]), device_id_type=MESH)

    def face_arrival(step, k):
        return pltpu.make_async_remote_copy(
            src_ref=msg.at[step, k], dst_ref=got.at[step, k],
            send_sem=face_send.at[step, k], recv_sem=face_recv.at[step, k],
            device_id=at(*OFFSETS[k]), device_id_type=MESH)

    def row_copy(source_ref, target_ref, sends, recvs, off):
        there = lax.rem(gy + off, n_gy)
        return pltpu.make_async_remote_copy(
            src_ref=source_ref.at[there], dst_ref=target_ref.at[gy],
            send_sem=sends.at[off - 1], recv_sem=recvs.at[off - 1],
            device_id=(gx, there), device_id_type=MESH)

    def row_arrival(source_ref, target_ref, sends, recvs, off):
        origin = lax.rem(gy - off + n_gy, n_gy)
        return pltpu.make_async_remote_copy(
            src_ref=source_ref.at[origin], dst_ref=target_ref.at[origin],
            send_sem=sends.at[off - 1], recv_sem=recvs.at[off - 1],
            device_id=(gx, origin), device_id_type=MESH)

    def halo_copies(top, bot, strip, rows_got, strips_got, corners_got, sends, recvs):
        sources = [
            top.at[:, :, 0:128], top, top.at[:, :, 128:256], strip, strip,
            bot.at[:, :, 0:128], bot, bot.at[:, :, 128:256]]
        targets = [
            corners_got.at[0], rows_got.at[0], corners_got.at[1], strips_got.at[0],
            strips_got.at[1], corners_got.at[2], rows_got.at[1], corners_got.at[3]]
        return [
            pltpu.make_async_remote_copy(
                src_ref=sources[k], dst_ref=targets[k],
                send_sem=sends.at[k], recv_sem=recvs.at[k],
                device_id=at(*OFFSETS[k]), device_id_type=MESH)
            for k in range(8)]

    dcat[...] = lane_triple(deriv[...].reshape(3 * BASIS, BASIS))
    scat[...] = lane_triple(stiff[...].reshape(3 * BASIS, BASIS))
    tpad[...] = jnp.zeros(tpad.shape, F32)
    lpad[...] = jnp.zeros(lpad.shape, F32)
    ipad[...] = jnp.zeros(ipad.shape, F32)
    spad[...] = jnp.zeros(spad.shape, F32)
    ipad[:, 0:FACE_BASIS] = interp[...]
    for face in range(4):
        tpad[face, 0:FACE_BASIS, :] = trace_in[face]
        lpad[face, :, 0:FACE_BASIS] = lift_in[face]
    for c in range(3):
        spad[c, 0:FIELDS, 0:FIELDS] = stars[c]
    spad[3, 0:FIELDS, 0:FIELDS] = source[...]
    tcat[...] = lane_triple(tpad[...].reshape(96, BASIS))

    repeat = bits(jnp.right_shift(iota2((104, 16), 0), 3) == iota2((104, 16), 1))
    tall = [[mm(repeat, part).astype(BF16) for part in halves(spad[c])] for c in range(4)]

    def spread(part, columns, starts):
        total = jnp.zeros((104, columns), F32)
        k = iota2((16, columns), 0)
        n = jnp.right_shift(iota2((16, columns), 1), 3)
        for c, start in starts:
            total = total + mm(tall[c][part], bits((n == k + start) & (k < FIELDS)))
        same = jnp.bitwise_and(iota2((104, columns), 0), 7) == jnp.bitwise_and(iota2((104, columns), 1), 7)
        return jnp.where(same, total, 0.0)

    every = [(c, c * FIELDS) for c in range(4)]
    kron[...] = jnp.concatenate([spread(0, 416, every), spread(1, 416, every)], axis=0).astype(BF16)

    def one_hot_face_sends():
        for pair in range(4):
            index = jnp.concatenate([send[2 * pair:2 * pair + 1, :], send[2 * pair + 1:2 * pair + 2, :]], axis=1)
            hot_send[:, pair * 128:(pair + 1) * 128] = one_hot(index, 4 * ELEMENTS)

    def star(x, groups):
        high, low = halves(x)
        both = mm(kron[:, 0:8 * groups], high)
        return both[0:104] + both[104:208] + mm(kron[0:104, 0:8 * groups], low)

    def directional(source_ref, weights, with_source, store):
        for h in range(FIELDS):
            q = source_ref[h].reshape(BASIS, ELEMENTS)
            spatial = mm(weights[...], triple(q))
            parts = [spatial[d * BASIS:(d + 1) * BASIS] for d in range(3)]
            for c in range(3):
                total = jac[0, c:c + 1, :] * parts[0] + jac[1, c:c + 1, :] * parts[1] + jac[2, c:c + 1, :] * parts[2]
                mixed[:, c * FIELDS + h] = total.reshape(7, 8, ELEMENTS)
            if with_source:
                mixed[:, 3 * FIELDS + h] = source_ref[h]
        groups = 4 * FIELDS if with_source else 3 * FIELDS
        for block in range(7):
            result = star(mixed[block, 0:groups].reshape(8 * groups, ELEMENTS), groups)
            store(block, result.reshape(FIELDS, 8, ELEMENTS))

    def later_matrices():
        rotate1[...] = jnp.concatenate(
            [spread(0, 208, [(c, 0), (c, FIELDS)]) for c in range(3)], axis=0).astype(BF16)
        rotate2[...] = jnp.concatenate([spread(1, 104, [(c, 0)]) for c in range(3)], axis=0).astype(BF16)
        first = jnp.zeros((BASIS, 192), F32)
        second = jnp.zeros((BASIS, 96), F32)
        for face in range(4):
            high, low = halves(lpad[face])
            k, n = iota2((24, 192), 0) + 24 * face, iota2((24, 192), 1)
            first = first + mm(high, bits((n == k) | (n == k + 96)))
            second = second + mm(low, bits(iota2((24, 96), 1) == iota2((24, 96), 0) + 24 * face))
        lift1[...] = first.astype(BF16)
        lift2[...] = second.astype(BF16)
        i_high, i_low = halves(ipad[...])
        points = []
        for face in range(4):
            t_high, t_low = halves(tpad[face])
            points.append(mm(i_high, t_high) + mm(i_high, t_low) + mm(i_low, t_high))
        vcat[...] = lane_triple(jnp.concatenate(points, axis=0))

    pick_row = iota2((8, SIDE), 0)
    edge = bits(iota2((8, SIDE), 1) == jnp.where(pick_row < 4, pick_row, pick_row + (SIDE - 8)))

    def strip_of(x):
        high, low = halves(x)
        rest = (x - high.astype(F32) - low.astype(F32)).astype(BF16)
        return mm_nt(edge, high) + mm_nt(edge, low) + mm_nt(edge, rest)

    uh = halo_copies(u_top, u_bot, u_strip, u_row_got, u_strip_got, u_corner_got, uh_send, uh_recv)

    def send_inputs():
        for copy in loads:
            copy.wait()
        for field in range(4):
            u_top[field] = sea0[field, 0:8, :]
            u_bot[field] = sea0[field, SIDE - 8:SIDE, :]
            u_strip[field] = strip_of(sea0[field])
        rows = sea_row[...]
        hits = jnp.where(iota2((n_gy, ELEMENTS), 0) == rows, 1.0, 0.0)
        tri = bits(iota2((ELEMENTS, ELEMENTS), 0) < iota2((ELEMENTS, ELEMENTS), 1))
        before = mm(hits.astype(BF16), tri)
        slot = jnp.sum(before * hits, axis=0, keepdims=True).astype(jnp.int32)
        placed = one_hot(rows * CAP + slot, slots)
        line = iota2((8, ELEMENTS), 0)
        values = jnp.where(line == 0, sea_face[...], jnp.where(
            line == 1, sea_base[0:1, :], sea_base[1:2, :])).astype(F32) + 1.0
        high, low = halves(values)
        found = mm_nt(high, placed) + mm_nt(low, placed)
        for pair in range(n_gy // 2):
            block = found[:, pair * 128:(pair + 1) * 128]
            corner_msg[2 * pair] = block
            corner_msg[2 * pair + 1] = swap_lanes(block)
        for copy in uh:
            copy.start()
        for off in range(1, n_gy):
            row_copy(corner_msg, corner_got, corner_send, corner_recv, off).start()
        corner_got[gy] = corner_msg[gy]
        return found[0:1, :].astype(jnp.int32) - 1

    side8 = low_lanes((8, 128))

    def position_tables():
        for off in range(1, n_gy):
            row_arrival(corner_msg, corner_got, corner_send, corner_recv, off).wait_recv()
        down = iota2((SIDE, 128), 0)
        for pair in range(n_gy // 2):
            corner = jnp.where(side8, corner_got[2 * pair], swap_lanes(corner_got[2 * pair + 1])).astype(jnp.int32)
            apart_x = down + 1 - corner[1:2, :]
            apart_y = down + 1 - corner[2:3, :]
            for j in range(4):
                base = j * slots + pair * 128
                hot_x[:, base:base + 128] = bits(apart_x == j)
                hot_y[:, base:base + 128] = bits(apart_y == j)

    up_in = gx > 0
    down_in = gx < n_gx - 1
    left_in = gy > 0
    right_in = gy < n_gy - 1

    def place_halo(target, rows_got, strips_got, corners_got, field):
        target[0:8, 0:SIDE] = jnp.where(up_in, rows_got[1, field], 0.0)
        target[8 + SIDE:EXT_X, 0:SIDE] = jnp.where(down_in, rows_got[0, field], 0.0)
        strip = jnp.concatenate([
            jnp.where(right_in, strips_got[0, field], 0.0), jnp.zeros((112, SIDE), F32),
            jnp.where(left_in, strips_got[1, field], 0.0)], axis=0)
        target[8:8 + SIDE, SIDE:EXT_Y] = jnp.transpose(strip)
        target[0:8, SIDE:EXT_Y] = jnp.where(
            side8, jnp.where(up_in & right_in, corners_got[2, field], 0.0),
            jnp.where(up_in & left_in, corners_got[3, field], 0.0))
        target[8 + SIDE:EXT_X, SIDE:EXT_Y] = jnp.where(
            side8, jnp.where(down_in & right_in, corners_got[0, field], 0.0),
            jnp.where(down_in & left_in, corners_got[1, field], 0.0))

    def ocean_first_step():
        for copy in uh:
            copy.wait_recv()
        for field in range(4):
            wave[field, 8:8 + SIDE, 0:SIDE] = sea0[field]
            place_halo(wave.at[field], u_row_got, u_strip_got, u_corner_got, field)

        def part(begin, rows, inner_from, inner_to):
            span = pl.ds(begin, rows)
            result = shallow_update(wave[0, span, :], wave[1, span, :], wave[2, span, :], wave[3, span, :])
            x = begin + iota2((rows, EXT_Y), 0)
            y = iota2((rows, EXT_Y), 1)
            out = ((x < 8) & (gx == 0)) | ((x >= 8 + SIDE) & (gx == n_gx - 1))
            out = out | ((y >= SIDE) & (y < SIDE + 64) & (gy == n_gy - 1)) | ((y >= SIDE + 64) & (gy == 0))
            for i in range(3):
                wave[4 + i, pl.ds(begin + inner_from, inner_to - inner_from), :] = jnp.where(
                    out, 0.0, result[i])[inner_from:inner_to]

        @pl.loop(0, SIDE // SLAB)
        def _(s):
            part(pl.multiple_of(s * SLAB, 8), SLAB + 16, 8, SLAB + 8)
        part(0, 16, 0, 8)
        part(EXT_X - 16, 16, 8, 16)

    first_factor = step_solid * step_solid / 2
    second_factor = first_factor * step_solid / 3
    table[ROWS // 8 - 1] = jnp.zeros((8, 4 * ELEMENTS), F32)

    for step in range(STEPS_DG):
        state = coef if step == 0 else solid

        def store_first(block, value):
            ddt[:, block] = value
        directional(state, dcat, True, store_first)

        def store_second(block, value):
            integral[:, block] = step_solid * state[:, block] - first_factor * ddt[:, block] + second_factor * value
        directional(ddt, dcat, True, store_second)

        if step == 0:
            one_hot_face_sends()
        for g in range(FIELDS):
            trace = mm(tcat[...], triple(integral[g].reshape(BASIS, ELEMENTS)))
            for face in range(4):
                table[3 * g:3 * g + 3, :, face * ELEMENTS:(face + 1) * ELEMENTS] = (
                    trace[face * 24:(face + 1) * 24].reshape(3, 8, ELEMENTS))
        high, low = halves(table[...].reshape(ROWS, 4 * ELEMENTS))
        tsplit[0:ROWS] = high
        tsplit[ROWS:2 * ROWS] = low

        low_side = low_lanes((HALF, 128))
        for half in range(2):
            picked = mm(tsplit[...], hot_send[:, half * 256:(half + 1) * 256])
            picked = picked[0:ROWS] + picked[ROWS:2 * ROWS]
            for pair in range(2):
                block = picked[:, pair * 128:(pair + 1) * 128]
                top, bot = block[0:HALF], block[HALF:ROWS]
                k = 4 * half + 2 * pair
                msg[step, k] = jnp.where(low_side, top, swap_lanes(bot))
                msg[step, k + 1] = jnp.where(low_side, swap_lanes(top), bot)
            if step == 0 and half == 0:
                pl.semaphore_wait(barrier, len(peers))
            for k in range(4 * half, 4 * half + 4):
                face_copy(step, k).start()

        if step == 0:
            slot_code = send_inputs()
            for face in range(4):
                code = partner[face:face + 1, :]
                cols = slice(face * ELEMENTS, (face + 1) * ELEMENTS)
                hot_local[:, cols] = one_hot(code, 4 * ELEMENTS)
                hot_remote[:, cols] = one_hot(code - 4 * ELEMENTS, 8 * 64)
            later_matrices()
        else:
            hot_slot[...] = one_hot(slot_code, 4 * ELEMENTS)
        for face in range(4):
            cols = slice(face * ELEMENTS, (face + 1) * ELEMENTS)
            local = mm(tsplit[...], hot_local[:, cols])
            outer[:, :, cols] = (local[0:ROWS] + local[ROWS:2 * ROWS]).reshape(ROWS // 8, 8, ELEMENTS)

        def store_volume(block, value):
            volume[:, block] = value
        directional(integral, scat, False, store_volume)
        if step == 1:
            position_tables()

        for k in range(8):
            face_arrival(step, k).wait_recv()
        for pair in range(4):
            a, b = got[step, 2 * pair], got[step, 2 * pair + 1]
            top = jnp.where(low_side, a, swap_lanes(b))
            bot = jnp.where(low_side, swap_lanes(a), b)
            cols = slice(pair * 128, (pair + 1) * 128)
            high, low = halves(top)
            tsplit[0:HALF, cols] = high
            tsplit[ROWS:ROWS + HALF, cols] = low
            high, low = halves(bot)
            tsplit[HALF:ROWS, cols] = high
            tsplit[ROWS + HALF:2 * ROWS, cols] = low
        for face in range(4):
            cols = slice(face * ELEMENTS, (face + 1) * ELEMENTS)
            remote = mm(tsplit[:, 0:512], hot_remote[:, cols])
            remote = (remote[0:ROWS] + remote[ROWS:2 * ROWS]).reshape(ROWS // 8, 8, ELEMENTS)
            for block in range(3):
                ids = [3 * g + block for g in range(FIELDS)]
                inside = jnp.concatenate([table[i, :, cols] for i in ids], axis=0)
                outside = jnp.concatenate([outer[i, :, cols] + remote[i] for i in ids], axis=0)
                total = inside + outside
                high = total.astype(BF16).astype(F32)
                both = jnp.concatenate([high, total - high], axis=0).astype(BF16)
                turned = mm(rotate1[...], both) + mm(rotate2[...], both[0:104])
                value = (0.5 * spd[...]) * (inside - outside)
                for c in range(3):
                    value = value + (0.5 * nrm[c, face:face + 1, :]) * turned[104 * c:104 * c + 104]
                flux[:, face, block] = value.reshape(FIELDS, 8, ELEMENTS)
        for g in range(FIELDS):
            f = flux[g].reshape(96, ELEMENTS)
            high = f.astype(BF16).astype(F32)
            both = jnp.concatenate([high, f - high], axis=0).astype(BF16)
            lifted = mm(lift1[...], both) + mm(lift2[...], both[0:96])
            solid[g] = state[g] + volume[g] - lifted.reshape(7, 8, ELEMENTS)

    point = mm(vcat[...], triple(solid[vertical_field].reshape(BASIS, ELEMENTS)))
    points = jnp.concatenate([point[16 * f:16 * f + 16] for f in range(4)], axis=1)
    high = points.astype(BF16).astype(F32)
    both = jnp.concatenate([high, points - high], axis=0).astype(BF16)
    rates = mm(both, hot_slot[...])
    rates = rates[0:16] + rates[16:32]
    for pair in range(n_gy // 2):
        a = rates[0:8, pair * 128:(pair + 1) * 128]
        b = rates[8:16, pair * 128:(pair + 1) * 128]
        rate_msg[2 * pair] = jnp.where(side8, a, swap_lanes(b))
        rate_msg[2 * pair + 1] = jnp.where(side8, swap_lanes(a), b)
    for off in range(1, n_gy):
        row_copy(rate_msg, rate_got, rate_send, rate_recv, off).start()
    rate_got[gy] = rate_msg[gy]
    saved = pltpu.make_async_copy(solid, solid_out, store_sem.at[0])
    saved.start()

    ocean_first_step()

    for off in range(1, n_gy):
        row_arrival(rate_msg, rate_got, rate_send, rate_recv, off).wait_recv()
    edge_row = jnp.where(iota2((16, 128), 0) < 8, iota2((16, 128), 0), iota2((16, 128), 0) + (SIDE - 16))
    edge_col = jnp.where(iota2((8, 128), 0) < 4, iota2((8, 128), 0), iota2((8, 128), 0) + (SIDE - 8))
    pairs = []
    for pair in range(n_gy // 2):
        corner = jnp.where(side8, corner_got[2 * pair], swap_lanes(corner_got[2 * pair + 1])).astype(jnp.int32)
        a, b = rate_got[2 * pair], rate_got[2 * pair + 1]
        first = jnp.where(side8, a, swap_lanes(b))
        second = jnp.where(side8, swap_lanes(a), b)
        rate = [[first[j:j + 1] for j in range(4)], [first[4 + j:5 + j] for j in range(4)],
                [second[j:j + 1] for j in range(4)], [second[4 + j:5 + j] for j in range(4)]]
        pairs.append((corner, rate))

    def chosen(masks, values):
        return jnp.where(masks[0], values[0], jnp.where(masks[1], values[1], jnp.where(
            masks[2], values[2], jnp.where(masks[3], values[3], 0.0))))

    row_parts = [[None] * len(pairs) for _ in range(4)]
    col_parts = [[None] * len(pairs) for _ in range(4)]
    for index, (corner, rate) in enumerate(pairs):
        apart_x = edge_row + 1 - corner[1:2, :]
        apart_y = edge_col + 1 - corner[2:3, :]
        masks_x = [apart_x == i for i in range(4)]
        masks_y = [apart_y == i for i in range(4)]
        for j in range(4):
            row_parts[j][index] = chosen(masks_x, [rate[i][j] for i in range(4)])
            col_parts[j][index] = chosen(masks_y, [rate[j][i] for i in range(4)])

    def summed(parts, table_ref):
        whole = jnp.concatenate([x for row in parts for x in row], axis=1)
        high = whole.astype(BF16).astype(F32)
        stacked = jnp.concatenate([high, whole - high], axis=0).astype(BF16)
        result = mm_nt(stacked, table_ref[...])
        return result[0:whole.shape[0]] + result[whole.shape[0]:]

    edge_rows = summed(row_parts, hot_y)
    f_top[0] = edge_rows[0:8]
    f_bot[0] = edge_rows[8:16]
    f_strip[0] = summed(col_parts, hot_x)
    fh = halo_copies(f_top, f_bot, f_strip, f_row_got, f_strip_got, f_corner_got, fh_send, fh_recv)
    for copy in fh:
        copy.start()

    down = iota2((SIDE, 128), 0)
    for index, (corner, rate) in enumerate(pairs):
        apart = down + 1 - corner[1:2, :]
        masks = [apart == i for i in range(4)]
        for j in range(4):
            base = j * slots + index * 128
            high, low = halves(chosen(masks, [rate[i][j] for i in range(4)]))
            left_hi[:, base:base + 128] = high
            left_lo[:, base:base + 128] = low
    force_ext[8:8 + SIDE, 0:SIDE] = mm_nt(left_hi[...], hot_y[...]) + mm_nt(left_lo[...], hot_y[...])
    for copy in fh:
        copy.wait_recv()
    place_halo(force_ext, f_row_got, f_strip_got, f_corner_got, 0)

    saved.wait()
    for copy in uh + fh:
        copy.wait_send()
    for off in range(1, n_gy):
        row_copy(corner_msg, corner_got, corner_send, corner_recv, off).wait_send()
        row_copy(rate_msg, rate_got, rate_send, rate_recv, off).wait_send()
    for step in range(STEPS_DG):
        for k in range(8):
            face_copy(step, k).wait_send()


SLAB = 32


def ocean_kernel(solid_in, wave, force, solid_out, ocean, bed, held, sems):
    fetch = pltpu.make_async_copy(solid_in, held, sems.at[0])
    fetch.start()
    store = pltpu.make_async_copy(held, solid_out, sems.at[1])

    def part(begin):
        span = pl.ds(begin, SLAB + 16)
        lift = force[span, :]
        depth = wave[0, span, :]
        slope_x, slope_y = slopes(lift)
        scale = 0.5 * step_ocean * step_ocean
        mom_x = wave[5, span, :] - scale * (depth * slope_x)
        mom_y = wave[6, span, :] - scale * (depth * slope_y)
        b = wave[3, span, :] + (2 * step_ocean) * lift
        result = shallow_update(wave[4, span, :], mom_x, mom_y, b)
        for i in range(3):
            ocean[i, pl.ds(begin, SLAB), :] = result[i][8:SLAB + 8, 0:SIDE]
        bed[pl.ds(begin, SLAB), :] = b[8:SLAB + 8, 0:SIDE]

    part(0)
    fetch.wait()
    store.start()

    @pl.loop(1, SIDE // SLAB)
    def _(s):
        part(pl.multiple_of(s * SLAB, 8))
    store.wait()


def per_device(
    n_gx, n_gy,
    coefficients, jacobian, face_normals, wave_speed, star_mats, deriv_mats, stiff_mats, source_mat,
    trace_mats, lift_mats, face_partner, send_faces, sea_face, sea_row, sea_base, interp_mat,
    water_depth, momentum, bottom,
):
    vm = pl.BlockSpec(memory_space=pltpu.VMEM)
    anywhere = pl.BlockSpec(memory_space=pl.ANY)
    slots = n_gy * CAP
    whole = (FIELDS, 7, 8, ELEMENTS)
    floats = lambda *shape: pltpu.VMEM(shape, F32)
    shorts = lambda *shape: pltpu.VMEM(shape, BF16)
    dma = pltpu.SemaphoreType.DMA
    scratch = [
        floats(*whole),
        floats(4, SIDE, SIDE),
        floats(4, 24, BASIS),
        floats(4, BASIS, 24),
        floats(16, 24),
        floats(4, 16, 16),
        shorts(168, 168),
        shorts(168, 168),
        shorts(96, 168),
        shorts(64, 168),
        shorts(56, 192),
        shorts(56, 96),
        shorts(208, 416),
        shorts(312, 208),
        shorts(312, 104),
        floats(*whole),
        floats(*whole),
        floats(7, 4 * FIELDS, 8, ELEMENTS),
        floats(ROWS // 8, 8, 4 * ELEMENTS),
        shorts(2 * ROWS, 4 * ELEMENTS),
        floats(ROWS // 8, 8, 4 * ELEMENTS),
        floats(FIELDS, 4, 3, 8, ELEMENTS),
        floats(*whole),
        shorts(4 * ELEMENTS, 512),
        shorts(4 * ELEMENTS, 4 * ELEMENTS),
        shorts(512, 4 * ELEMENTS),
        shorts(4 * ELEMENTS, slots),
        shorts(SIDE, 4 * slots),
        shorts(SIDE, 4 * slots),
        floats(STEPS_DG, 8, HALF, 128),
        floats(STEPS_DG, 8, HALF, 128),
        floats(n_gy, 8, 128),
        floats(n_gy, 8, 128),
        floats(n_gy, 8, 128),
        floats(n_gy, 8, 128),
        shorts(SIDE, 4 * slots),
        shorts(SIDE, 4 * slots),
        floats(4, 8, SIDE),
        floats(4, 8, SIDE),
        floats(4, 8, SIDE),
        floats(2, 4, 8, SIDE),
        floats(2, 4, 8, SIDE),
        floats(4, 4, 8, 128),
        floats(1, 8, SIDE),
        floats(1, 8, SIDE),
        floats(1, 8, SIDE),
        floats(2, 1, 8, SIDE),
        floats(2, 1, 8, SIDE),
        floats(4, 1, 8, 128),
        dma((3,)), dma((1,)),
        dma((STEPS_DG, 8)), dma((STEPS_DG, 8)),
        dma((n_gy - 1,)), dma((n_gy - 1,)), dma((n_gy - 1,)), dma((n_gy - 1,)),
        dma((8,)), dma((8,)), dma((8,)), dma((8,)),
    ]
    solid, wave, force = pl.pallas_call(
        functools.partial(solid_kernel, n_gx, n_gy),
        out_shape=(
            jax.ShapeDtypeStruct(whole, F32),
            jax.ShapeDtypeStruct((7, EXT_X, EXT_Y), F32),
            jax.ShapeDtypeStruct((EXT_X, EXT_Y), F32)),
        in_specs=[vm] * 16 + [anywhere] * 3,
        out_specs=(anywhere, vm, vm),
        scratch_shapes=scratch,
        compiler_params=pltpu.CompilerParams(
            collective_id=0, has_side_effects=True, vmem_limit_bytes=60 * 1024 * 1024),
        name="solid",
    )(
        coefficients.reshape(whole), jacobian, face_normals.transpose(1, 0, 2), wave_speed.reshape(1, ELEMENTS),
        deriv_mats, stiff_mats, trace_mats, lift_mats, interp_mat, star_mats, source_mat, face_partner, send_faces,
        sea_face.reshape(1, ELEMENTS), sea_row.reshape(1, ELEMENTS), sea_base.T,
        water_depth, momentum, bottom)
    solid, ocean, bed = pl.pallas_call(
        ocean_kernel,
        out_shape=(
            jax.ShapeDtypeStruct(whole, F32),
            jax.ShapeDtypeStruct((3, SIDE, SIDE), F32),
            jax.ShapeDtypeStruct((SIDE, SIDE), F32)),
        in_specs=[anywhere, vm, vm],
        out_specs=(anywhere, vm, vm),
        scratch_shapes=[floats(*whole), dma((2,))],
        name="ocean",
    )(solid, wave, force)
    return solid.reshape(FIELDS, BASIS, ELEMENTS), ocean, bed


def solution(mesh):
    in_specs = (
        P(None, None, ("gx", "gy")),
        P(None, None, ("gx", "gy")),
        P(None, None, ("gx", "gy")),
        P(("gx", "gy")),
        P(),
        P(),
        P(),
        P(),
        P(),
        P(),
        P(None, ("gx", "gy")),
        P(None, ("gx", "gy")),
        P(("gx", "gy")),
        P(("gx", "gy"), None),
        P(("gx", "gy"), None),
        P(),
        P("gx", "gy"),
        P(None, "gx", "gy"),
        P("gx", "gy"),
    )
    out_specs = (P(None, None, ("gx", "gy")), P(None, "gx", "gy"), P("gx", "gy"))
    return jax.shard_map(
        functools.partial(per_device, mesh.shape["gx"], mesh.shape["gy"]),
        mesh=mesh, in_specs=in_specs, out_specs=out_specs, check_vma=False,
    )
```

```python
import functools

import jax
import jax.numpy as jnp
from jax import lax
from jax.experimental import pallas as pl
from jax.experimental.pallas import tpu as pltpu
from jax.sharding import PartitionSpec as P

MESH = pl.DeviceIdType.MESH
F32 = jnp.float32
BF16 = jnp.bfloat16

FIELDS = 13
BASIS = 56
FACE_BASIS = 21
CAP = 64
ELEMENTS = 256
SIDE = 256
STEPS_DG = 2

step_solid = 0.4
step_ocean = 0.2
depth_floor = 0.5
vertical_field = 6

OFFSETS = [(-1, -1), (-1, 0), (-1, 1), (0, -1), (0, 1), (1, -1), (1, 0), (1, 1)]
ROWS = 320
HALF = ROWS // 2
EXT_X = SIDE + 16
EXT_Y = SIDE + 128


def mm(a, b):
    return jnp.dot(a, b, preferred_element_type=F32)


def mm_nt(a, b):
    return lax.dot_general(a, b, (((1,), (1,)), ((), ())), preferred_element_type=F32)


def halves(x):
    high = x.astype(BF16)
    return high, (x - high.astype(F32)).astype(BF16)


def triple(x):
    high = x.astype(BF16).astype(F32)
    return jnp.concatenate([high, x - high, high], axis=0).astype(BF16)


def one_hot(index_row, rows):
    width = index_row.shape[1]
    index = jnp.broadcast_to(index_row, (16, width)).astype(jnp.int16)
    iota = lax.broadcasted_iota(jnp.int32, (16, width), 0).astype(jnp.int16)
    apart = index - iota
    one, zero = jnp.ones((16, width), BF16), jnp.zeros((16, width), BF16)
    return jnp.concatenate(
        [jnp.where(apart == jnp.int16(16 * tile), one, zero) for tile in range(rows // 16)], axis=0)


def low_lanes(shape):
    return lax.broadcasted_iota(jnp.int32, shape, len(shape) - 1) < 64


def swap_lanes(x):
    return pltpu.roll(x, 64, x.ndim - 1)


def iota2(shape, axis):
    return lax.broadcasted_iota(jnp.int32, shape, axis)


def bits(condition):
    return jnp.where(condition, 1.0, 0.0).astype(BF16)


def lane_triple(w):
    high, low = halves(w)
    k, n = iota2((BASIS, 3 * BASIS), 0), iota2((BASIS, 3 * BASIS), 1)
    return (mm(high, bits((n == k) | (n == k + BASIS))) + mm(low, bits(n == k + 2 * BASIS))).astype(BF16)


def shallow_update(height, mom_x, mom_y, b, extra=None):
    safe = jnp.maximum(height, depth_floor)
    root = lax.rsqrt(safe)
    inv = root * root
    vel_x = mom_x * inv
    vel_y = mom_y * inv
    celerity = safe * root
    cross = mom_x * vel_y
    press = 0.5 * height * height
    n, m = height.shape
    fluxes = (
        (0, n, (mom_x, mom_x * vel_x + press, cross), jnp.abs(vel_x) + celerity),
        (1, m, (mom_y, cross, mom_y * vel_y + press), jnp.abs(vel_y) + celerity))
    state = (height, mom_x, mom_y)
    change = [0.0, 0.0, 0.0]
    for axis, size, flux, speed in fluxes:
        wave = jnp.maximum(speed, pltpu.roll(speed, size - 1, axis))
        for i in range(3):
            face = (flux[i] + pltpu.roll(flux[i], size - 1, axis)) - wave * (
                pltpu.roll(state[i], size - 1, axis) - state[i])
            change[i] = change[i] + (face - pltpu.roll(face, 1, axis))
    half = 0.5 * step_ocean
    slope_x, slope_y = slopes(b)
    return (
        height - half * change[0],
        mom_x - half * (change[1] + height * slope_x),
        mom_y - half * (change[2] + height * slope_y))


def slopes(b):
    n, m = b.shape
    return (
        pltpu.roll(b, n - 1, 0) - pltpu.roll(b, 1, 0),
        pltpu.roll(b, m - 1, 1) - pltpu.roll(b, 1, 1))


def solid_kernel(
    n_gx, n_gy,
    coef, jac, nrm, spd, deriv, stiff, trace_in, lift_in, interp, stars, source, partner, send,
    sea_face, sea_row, sea_base, depth, mom, bottom,
    solid_out, wave_out, force_ext,
    solid, wave, sea0, tpad, lpad, ipad, spad, dcat, scat, tcat, vcat, lift1, lift2, kron, kron_high, rotate1, rotate2,
    ddt, integral, mixed, table, tsplit, outer, flux, volume,
    hot_send, hot_local, hot_remote, hot_slot, hot_x, hot_y,
    msg, got, corner_msg, corner_got, rate_msg, rate_got,
    u_top, u_bot, u_strip, u_row_got, u_strip_got, u_corner_got,
    f_top, f_bot, f_strip, f_row_got, f_strip_got, f_corner_got,
    load_sem, store_sem,
    face_send, face_recv, corner_send, corner_recv, rate_send, rate_recv,
    uh_send, uh_recv, fh_send, fh_recv,
):
    gx = lax.axis_index("gx")
    gy = lax.axis_index("gy")
    slots = n_gy * CAP

    def at(dx, dy):
        return (lax.rem(gx + dx + n_gx, n_gx), lax.rem(gy + dy + n_gy, n_gy))

    barrier = pltpu.get_barrier_semaphore()
    peers = [at(dx, dy) for dx, dy in OFFSETS] + [at(0, off) for off in range(2, n_gy - 1)]
    for peer in peers:
        pl.semaphore_signal(barrier, inc=1, device_id=peer, device_id_type=MESH)

    loads = [
        pltpu.make_async_copy(depth, sea0.at[0], load_sem.at[0]),
        pltpu.make_async_copy(mom, sea0.at[1:3], load_sem.at[1]),
        pltpu.make_async_copy(bottom, sea0.at[3], load_sem.at[2])]
    for copy in loads:
        copy.start()

    def face_copy(step, k):
        return pltpu.make_async_remote_copy(
            src_ref=msg.at[step, k], dst_ref=got.at[step, 7 - k],
            send_sem=face_send.at[step, k], recv_sem=face_recv.at[step, 7 - k],
            device_id=at(*OFFSETS[k]), device_id_type=MESH)

    def face_arrival(step, k):
        return pltpu.make_async_remote_copy(
            src_ref=msg.at[step, k], dst_ref=got.at[step, k],
            send_sem=face_send.at[step, k], recv_sem=face_recv.at[step, k],
            device_id=at(*OFFSETS[k]), device_id_type=MESH)

    def row_copy(source_ref, target_ref, sends, recvs, off):
        there = lax.rem(gy + off, n_gy)
        return pltpu.make_async_remote_copy(
            src_ref=source_ref.at[there], dst_ref=target_ref.at[gy],
            send_sem=sends.at[off - 1], recv_sem=recvs.at[off - 1],
            device_id=(gx, there), device_id_type=MESH)

    def row_arrival(source_ref, target_ref, sends, recvs, off):
        origin = lax.rem(gy - off + n_gy, n_gy)
        return pltpu.make_async_remote_copy(
            src_ref=source_ref.at[origin], dst_ref=target_ref.at[origin],
            send_sem=sends.at[off - 1], recv_sem=recvs.at[off - 1],
            device_id=(gx, origin), device_id_type=MESH)

    def halo_copies(top, bot, strip, rows_got, strips_got, corners_got, sends, recvs):
        sources = [
            top.at[:, :, 0:128], top, top.at[:, :, 128:256], strip, strip,
            bot.at[:, :, 0:128], bot, bot.at[:, :, 128:256]]
        targets = [
            corners_got.at[0], rows_got.at[0], corners_got.at[1], strips_got.at[0],
            strips_got.at[1], corners_got.at[2], rows_got.at[1], corners_got.at[3]]
        return [
            pltpu.make_async_remote_copy(
                src_ref=sources[k], dst_ref=targets[k],
                send_sem=sends.at[k], recv_sem=recvs.at[k],
                device_id=at(*OFFSETS[k]), device_id_type=MESH)
            for k in range(8)]

    def by_block(ref):
        tiles = ref[...].reshape(3, 7, 8, BASIS)
        return jnp.concatenate([tiles[d, block] for block in range(7) for d in range(3)], axis=0)

    dcat[...] = lane_triple(by_block(deriv))
    scat[...] = lane_triple(by_block(stiff))
    tpad[...] = jnp.zeros(tpad.shape, F32)
    lpad[...] = jnp.zeros(lpad.shape, F32)
    ipad[...] = jnp.zeros(ipad.shape, F32)
    spad[...] = jnp.zeros(spad.shape, F32)
    ipad[:, 0:FACE_BASIS] = interp[...]
    for face in range(4):
        tpad[face, 0:FACE_BASIS, :] = trace_in[:, face, :]
        lpad[face, 0:FACE_BASIS, :] = lift_in[:, face, :]
    for c in range(3):
        spad[c, 0:FIELDS, 0:FIELDS] = stars[c]
    spad[3, 0:FIELDS, 0:FIELDS] = source[...]
    tcat[...] = lane_triple(tpad[...].reshape(96, BASIS))

    repeat = bits(jnp.right_shift(iota2((104, 16), 0), 3) == iota2((104, 16), 1))
    tall = [[mm(repeat, part).astype(BF16) for part in halves(spad[c])] for c in range(4)]

    def spread(part, columns, starts):
        total = jnp.zeros((104, columns), F32)
        k = iota2((16, columns), 0)
        n = jnp.right_shift(iota2((16, columns), 1), 3)
        for c, start in starts:
            total = total + mm(tall[c][part], bits((n == k + start) & (k < FIELDS)))
        same = jnp.bitwise_and(iota2((104, columns), 0), 7) == jnp.bitwise_and(iota2((104, columns), 1), 7)
        return jnp.where(same, total, 0.0)

    every = [(c, c * FIELDS) for c in range(4)]
    def woven(parts):
        return jnp.concatenate([part[8 * g:8 * g + 8] for g in range(FIELDS) for part in parts], axis=0).astype(BF16)

    kron_parts = [spread(0, 416, every), spread(1, 416, every)]
    kron[...] = woven(kron_parts)
    kron_high[...] = kron_parts[0].astype(BF16)

    def one_hot_face_sends():
        for pair in range(4):
            index = jnp.concatenate([send[2 * pair:2 * pair + 1, :], send[2 * pair + 1:2 * pair + 2, :]], axis=1)
            hot_send[:, pair * 128:(pair + 1) * 128] = one_hot(index, 4 * ELEMENTS)

    def star(x, groups):
        high, low = halves(x)
        both = mm(kron[:, 0:8 * groups], high).reshape(FIELDS, 2, 8, ELEMENTS)
        return both[:, 0] + both[:, 1] + mm(kron_high[:, 0:8 * groups], low).reshape(FIELDS, 8, ELEMENTS)

    def directional(source_ref, weights, with_source, store):
        for h in range(FIELDS):
            q = source_ref[h].reshape(BASIS, ELEMENTS)
            spatial = mm(weights[...], triple(q))
            for block in range(7):
                parts = [spatial[24 * block + 8 * d:24 * block + 8 * d + 8] for d in range(3)]
                for c in range(3):
                    mixed[block, c * FIELDS + h] = (
                        jac[0, c:c + 1, :] * parts[0] + jac[1, c:c + 1, :] * parts[1] + jac[2, c:c + 1, :] * parts[2])
            if with_source:
                mixed[:, 3 * FIELDS + h] = source_ref[h]
        groups = 4 * FIELDS if with_source else 3 * FIELDS
        for block in range(7):
            result = star(mixed[block, 0:groups].reshape(8 * groups, ELEMENTS), groups)
            store(block, result)

    def later_matrices():
        rotate1[...] = woven([spread(0, 208, [(c, 0), (c, FIELDS)]) for c in range(3)])
        rotate2[...] = woven([spread(1, 104, [(c, 0)]) for c in range(3)])
        first = jnp.zeros((BASIS, 192), F32)
        second = jnp.zeros((BASIS, 96), F32)
        for face in range(4):
            same = bits(iota2((BASIS, BASIS), 0) == iota2((BASIS, BASIS), 1))
            high, low = [mm_nt(same, part).astype(BF16) for part in halves(lpad[face])]
            k, n = iota2((24, 192), 0) + 24 * face, iota2((24, 192), 1)
            first = first + mm(high, bits((n == k) | (n == k + 96)))
            second = second + mm(low, bits(iota2((24, 96), 1) == iota2((24, 96), 0) + 24 * face))
        lift1[...] = first.astype(BF16)
        lift2[...] = second.astype(BF16)
        i_high, i_low = halves(ipad[...])
        points = []
        for face in range(4):
            t_high, t_low = halves(tpad[face])
            points.append(mm(i_high, t_high) + mm(i_high, t_low) + mm(i_low, t_high))
        vcat[...] = lane_triple(jnp.concatenate(points, axis=0))

    pick_row = iota2((8, SIDE), 0)
    edge = bits(iota2((8, SIDE), 1) == jnp.where(pick_row < 4, pick_row, pick_row + (SIDE - 8)))

    def strip_of(x):
        high, low = halves(x)
        rest = (x - high.astype(F32) - low.astype(F32)).astype(BF16)
        return mm_nt(edge, high) + mm_nt(edge, low) + mm_nt(edge, rest)

    uh = halo_copies(u_top, u_bot, u_strip, u_row_got, u_strip_got, u_corner_got, uh_send, uh_recv)

    def send_inputs():
        for copy in loads:
            copy.wait()
        for field in range(4):
            u_top[field] = sea0[field, 0:8, :]
            u_bot[field] = sea0[field, SIDE - 8:SIDE, :]
            u_strip[field] = strip_of(sea0[field])
        rows = sea_row[...]
        hits = jnp.where(iota2((n_gy, ELEMENTS), 0) == rows, 1.0, 0.0)
        tri = bits(iota2((ELEMENTS, ELEMENTS), 0) < iota2((ELEMENTS, ELEMENTS), 1))
        before = mm(hits.astype(BF16), tri)
        slot = jnp.sum(before * hits, axis=0, keepdims=True).astype(jnp.int32)
        placed = one_hot(rows * CAP + slot, slots)
        line = iota2((8, ELEMENTS), 0)
        values = jnp.where(line == 0, sea_face[...], jnp.where(
            line == 1, sea_base[0:1, :], sea_base[1:2, :])).astype(F32) + 1.0
        high, low = halves(values)
        found = mm_nt(high, placed) + mm_nt(low, placed)
        for pair in range(n_gy // 2):
            block = found[:, pair * 128:(pair + 1) * 128]
            corner_msg[2 * pair] = block
            corner_msg[2 * pair + 1] = swap_lanes(block)
        for copy in uh:
            copy.start()
        for off in range(1, n_gy):
            row_copy(corner_msg, corner_got, corner_send, corner_recv, off).start()
        corner_got[gy] = corner_msg[gy]
        return found[0:1, :].astype(jnp.int32) - 1

    side8 = low_lanes((8, 128))

    iota16 = iota2((16, 128), 0).astype(jnp.int16)
    one16, zero16 = jnp.ones((16, 128), BF16), jnp.zeros((16, 128), BF16)

    def position_tables():
        for off in range(1, n_gy):
            row_arrival(corner_msg, corner_got, corner_send, corner_recv, off).wait_recv()
        for pair in range(n_gy // 2):
            corner = jnp.where(side8, corner_got[2 * pair], swap_lanes(corner_got[2 * pair + 1])).astype(jnp.int32)
            for hot, line in ((hot_x, 1), (hot_y, 2)):
                apart = jnp.broadcast_to(corner[line:line + 1, :] - 1, (16, 128)).astype(jnp.int16) - iota16
                for tile in range(SIDE // 16):
                    for j in range(4):
                        base = pair * 512 + j * 128
                        hot[16 * tile:16 * tile + 16, base:base + 128] = jnp.where(
                            apart == jnp.int16(16 * tile - j), one16, zero16)

    up_in = gx > 0
    down_in = gx < n_gx - 1
    left_in = gy > 0
    right_in = gy < n_gy - 1

    def place_halo(target, rows_got, strips_got, corners_got, field):
        target[0:8, 0:SIDE] = jnp.where(up_in, rows_got[1, field], 0.0)
        target[8 + SIDE:EXT_X, 0:SIDE] = jnp.where(down_in, rows_got[0, field], 0.0)
        strip = jnp.concatenate([
            jnp.where(right_in, strips_got[0, field], 0.0), jnp.zeros((112, SIDE), F32),
            jnp.where(left_in, strips_got[1, field], 0.0)], axis=0)
        target[8:8 + SIDE, SIDE:EXT_Y] = jnp.transpose(strip)
        target[0:8, SIDE:EXT_Y] = jnp.where(
            side8, jnp.where(up_in & right_in, corners_got[2, field], 0.0),
            jnp.where(up_in & left_in, corners_got[3, field], 0.0))
        target[8 + SIDE:EXT_X, SIDE:EXT_Y] = jnp.where(
            side8, jnp.where(down_in & right_in, corners_got[0, field], 0.0),
            jnp.where(down_in & left_in, corners_got[1, field], 0.0))

    def ocean_first_step():
        for copy in uh:
            copy.wait_recv()
        for field in range(4):
            row = (0, 5, 6, 1)[field]
            wave[row, 8:8 + SIDE, 0:SIDE] = sea0[field]
            place_halo(wave.at[row], u_row_got, u_strip_got, u_corner_got, field)

        def part(begin, rows, inner_from, inner_to):
            span = pl.ds(begin, rows)
            result = shallow_update(wave[0, span, :], wave[5, span, :], wave[6, span, :], wave[1, span, :])
            x = begin + iota2((rows, EXT_Y), 0)
            y = iota2((rows, EXT_Y), 1)
            out = ((x < 8) & (gx == 0)) | ((x >= 8 + SIDE) & (gx == n_gx - 1))
            out = out | ((y >= SIDE) & (y < SIDE + 64) & (gy == n_gy - 1)) | ((y >= SIDE + 64) & (gy == 0))
            for i in range(3):
                wave[2 + i, pl.ds(begin + inner_from, inner_to - inner_from), :] = jnp.where(
                    out, 0.0, result[i])[inner_from:inner_to]

        @pl.loop(0, SIDE // SLAB)
        def _(s):
            part(pl.multiple_of(s * SLAB, 8), SLAB + 16, 8, SLAB + 8)
        part(0, 16, 0, 8)
        part(EXT_X - 16, 16, 8, 16)

    first_factor = step_solid * step_solid / 2
    second_factor = first_factor * step_solid / 3
    table[ROWS // 8 - 1] = jnp.zeros((8, 4 * ELEMENTS), F32)

    for step in range(STEPS_DG):
        state = coef if step == 0 else solid

        def store_first(block, value):
            ddt[:, block] = value
        directional(state, dcat, True, store_first)

        def store_second(block, value):
            integral[:, block] = step_solid * state[:, block] - first_factor * ddt[:, block] + second_factor * value
        directional(ddt, dcat, True, store_second)

        if step == 0:
            one_hot_face_sends()
        for g in range(FIELDS):
            trace = mm(tcat[...], triple(integral[g].reshape(BASIS, ELEMENTS)))
            for face in range(4):
                table[3 * g:3 * g + 3, :, face * ELEMENTS:(face + 1) * ELEMENTS] = (
                    trace[face * 24:(face + 1) * 24].reshape(3, 8, ELEMENTS))
        for tile in range(ROWS // 16):
            high, low = halves(table[2 * tile:2 * tile + 2].reshape(16, 4 * ELEMENTS))
            tsplit[32 * tile:32 * tile + 16] = high
            tsplit[32 * tile + 16:32 * tile + 32] = low

        low_side = low_lanes((HALF, 128))
        for half in range(2):
            picked = mm(tsplit[...], hot_send[:, half * 256:(half + 1) * 256])
            picked = picked.reshape(ROWS // 16, 2, 16, 256)
            picked = (picked[:, 0] + picked[:, 1]).reshape(ROWS, 256)
            for pair in range(2):
                block = picked[:, pair * 128:(pair + 1) * 128]
                top, bot = block[0:HALF], block[HALF:ROWS]
                k = 4 * half + 2 * pair
                msg[step, k] = jnp.where(low_side, top, swap_lanes(bot))
                msg[step, k + 1] = jnp.where(low_side, swap_lanes(top), bot)
            if step == 0 and half == 0:
                pl.semaphore_wait(barrier, len(peers))
            for k in range(4 * half, 4 * half + 4):
                face_copy(step, k).start()

        if step == 0:
            slot_code = send_inputs()
            for face in range(4):
                code = partner[face:face + 1, :]
                cols = slice(face * ELEMENTS, (face + 1) * ELEMENTS)
                hot_local[:, cols] = one_hot(code, 4 * ELEMENTS)
                hot_remote[:, cols] = one_hot(code - 4 * ELEMENTS, 8 * 64)
            later_matrices()
        else:
            hot_slot[...] = one_hot(slot_code, 4 * ELEMENTS)
        for face in range(4):
            cols = slice(face * ELEMENTS, (face + 1) * ELEMENTS)
            local = mm(tsplit[...], hot_local[:, cols])
            local = local.reshape(ROWS // 16, 2, 16, ELEMENTS)
            outer[:, :, cols] = (local[:, 0] + local[:, 1]).reshape(ROWS // 8, 8, ELEMENTS)

        def store_volume(block, value):
            volume[:, block] = value
        directional(integral, scat, False, store_volume)
        if step == 1:
            position_tables()

        for k in range(8):
            face_arrival(step, k).wait_recv()
        for pair in range(4):
            a, b = got[step, 2 * pair], got[step, 2 * pair + 1]
            top = jnp.where(low_side, a, swap_lanes(b))
            bot = jnp.where(low_side, swap_lanes(a), b)
            cols = slice(pair * 128, (pair + 1) * 128)
            for begin, part in ((0, top), (HALF, bot)):
                for tile in range(HALF // 16):
                    high, low = halves(part[16 * tile:16 * tile + 16])
                    row = 2 * (begin + 16 * tile)
                    tsplit[row:row + 16, cols] = high
                    tsplit[row + 16:row + 32, cols] = low
        for face in range(4):
            cols = slice(face * ELEMENTS, (face + 1) * ELEMENTS)
            remote = mm(tsplit[:, 0:512], hot_remote[:, cols])
            remote = remote.reshape(ROWS // 16, 2, 16, ELEMENTS)
            remote = (remote[:, 0] + remote[:, 1]).reshape(ROWS // 8, 8, ELEMENTS)
            for block in range(3):
                ids = [3 * g + block for g in range(FIELDS)]
                inside = jnp.concatenate([table[i, :, cols] for i in ids], axis=0)
                outside = jnp.concatenate([outer[i, :, cols] + remote[i] for i in ids], axis=0)
                total = inside + outside
                high = total.astype(BF16).astype(F32)
                both = jnp.concatenate([high, total - high], axis=0).astype(BF16)
                turned = mm(rotate1[...], both) + mm(rotate2[...], both[0:104])
                normal = [0.5 * nrm[c, face:face + 1, :] for c in range(3)]
                speed = 0.5 * spd[...]
                for g in range(FIELDS):
                    value = speed * (inside[8 * g:8 * g + 8] - outside[8 * g:8 * g + 8])
                    for c in range(3):
                        value = value + normal[c] * turned[24 * g + 8 * c:24 * g + 8 * c + 8]
                    flux[g, face, block] = value
        for g in range(FIELDS):
            f = flux[g].reshape(96, ELEMENTS)
            high = f.astype(BF16).astype(F32)
            both = jnp.concatenate([high, f - high], axis=0).astype(BF16)
            lifted = mm(lift1[...], both) + mm(lift2[...], both[0:96])
            solid[g] = state[g] + volume[g] - lifted.reshape(7, 8, ELEMENTS)

    point = mm(vcat[...], triple(solid[vertical_field].reshape(BASIS, ELEMENTS)))
    points = jnp.concatenate([point[16 * f:16 * f + 16] for f in range(4)], axis=1)
    high = points.astype(BF16).astype(F32)
    both = jnp.concatenate([high, points - high], axis=0).astype(BF16)
    rates = mm(both, hot_slot[...])
    rates = rates[0:16] + rates[16:32]
    for pair in range(n_gy // 2):
        a = rates[0:8, pair * 128:(pair + 1) * 128]
        b = rates[8:16, pair * 128:(pair + 1) * 128]
        rate_msg[2 * pair] = jnp.where(side8, a, swap_lanes(b))
        rate_msg[2 * pair + 1] = jnp.where(side8, swap_lanes(a), b)
    for off in range(1, n_gy):
        row_copy(rate_msg, rate_got, rate_send, rate_recv, off).start()
    rate_got[gy] = rate_msg[gy]
    saved = pltpu.make_async_copy(solid, solid_out, store_sem.at[0])
    saved.start()

    ocean_first_step()
    waved = pltpu.make_async_copy(wave.at[0:5], wave_out, store_sem.at[1])
    waved.start()

    for off in range(1, n_gy):
        row_arrival(rate_msg, rate_got, rate_send, rate_recv, off).wait_recv()
    edge_row = jnp.where(iota2((16, 128), 0) < 8, iota2((16, 128), 0), iota2((16, 128), 0) + (SIDE - 16))
    edge_col = jnp.where(iota2((8, 128), 0) < 4, iota2((8, 128), 0), iota2((8, 128), 0) + (SIDE - 8))
    pairs = []
    for pair in range(n_gy // 2):
        corner = jnp.where(side8, corner_got[2 * pair], swap_lanes(corner_got[2 * pair + 1])).astype(jnp.int32)
        a, b = rate_got[2 * pair], rate_got[2 * pair + 1]
        first = jnp.where(side8, a, swap_lanes(b))
        second = jnp.where(side8, swap_lanes(a), b)
        rate = [[first[j:j + 1] for j in range(4)], [first[4 + j:5 + j] for j in range(4)],
                [second[j:j + 1] for j in range(4)], [second[4 + j:5 + j] for j in range(4)]]
        pairs.append((corner, rate))

    def chosen(masks, values):
        return jnp.where(masks[0], values[0], jnp.where(masks[1], values[1], jnp.where(
            masks[2], values[2], jnp.where(masks[3], values[3], 0.0))))

    row_parts = [[None] * len(pairs) for _ in range(4)]
    col_parts = [[None] * len(pairs) for _ in range(4)]
    for index, (corner, rate) in enumerate(pairs):
        apart_x = edge_row + 1 - corner[1:2, :]
        apart_y = edge_col + 1 - corner[2:3, :]
        masks_x = [apart_x == i for i in range(4)]
        masks_y = [apart_y == i for i in range(4)]
        for j in range(4):
            row_parts[j][index] = chosen(masks_x, [rate[i][j] for i in range(4)])
            col_parts[j][index] = chosen(masks_y, [rate[j][i] for i in range(4)])

    def summed(parts, table_ref):
        whole = jnp.concatenate([row[pair] for pair in range(n_gy // 2) for row in parts], axis=1)
        high = whole.astype(BF16).astype(F32)
        stacked = jnp.concatenate([high, whole - high], axis=0).astype(BF16)
        result = mm_nt(stacked, table_ref[...])
        return result[0:whole.shape[0]] + result[whole.shape[0]:]

    edge_rows = summed(row_parts, hot_y)
    f_top[0] = edge_rows[0:8]
    f_bot[0] = edge_rows[8:16]
    f_strip[0] = summed(col_parts, hot_x)
    fh = halo_copies(f_top, f_bot, f_strip, f_row_got, f_strip_got, f_corner_got, fh_send, fh_recv)
    for copy in fh:
        copy.start()

    force_ext[8:8 + SIDE, 0:SIDE] = jnp.zeros((SIDE, SIDE), F32)

    @pl.loop(0, n_gy // 2, unroll=2)
    def _(pair):
        corner = jnp.where(side8, corner_got[2 * pair], swap_lanes(corner_got[2 * pair + 1])).astype(jnp.int32)
        a, b = rate_got[2 * pair], rate_got[2 * pair + 1]
        first = jnp.where(side8, a, swap_lanes(b))
        second = jnp.where(side8, swap_lanes(a), b)
        wide = []
        for line in [first[i:i + 1] for i in range(8)] + [second[i:i + 1] for i in range(8)]:
            wide.append(halves(jnp.broadcast_to(line, (16, 128))))
        apart = jnp.broadcast_to(corner[1:2, :] - 1, (16, 128)).astype(jnp.int16) - iota16
        columns = [[] for _ in range(4)]
        for tile in range(SIDE // 16):
            masks = [apart == jnp.int16(16 * tile - i) for i in range(4)]
            for j in range(4):
                for part in range(2):
                    value = zero16
                    for i in range(4):
                        value = jnp.where(masks[i], wide[4 * i + j][part], value)
                    columns[j].append(value)
        total = jnp.zeros((2 * SIDE, SIDE), F32)
        for half in range(2):
            table_part = hot_y[:, pl.ds(pl.multiple_of(pair * 512 + half * 256, 256), 256)]
            left = jnp.concatenate([jnp.concatenate(columns[2 * half + j], axis=0) for j in range(2)], axis=1)
            total = total + mm_nt(left, table_part)
        total = total.reshape(SIDE // 16, 2, 16, SIDE)
        total = (total[:, 0] + total[:, 1]).reshape(SIDE, SIDE)
        force_ext[8:8 + SIDE, 0:SIDE] = force_ext[8:8 + SIDE, 0:SIDE] + total

    for copy in fh:
        copy.wait_recv()
    place_halo(force_ext, f_row_got, f_strip_got, f_corner_got, 0)

    saved.wait()
    waved.wait()
    for copy in uh + fh:
        copy.wait_send()
    for off in range(1, n_gy):
        row_copy(corner_msg, corner_got, corner_send, corner_recv, off).wait_send()
        row_copy(rate_msg, rate_got, rate_send, rate_recv, off).wait_send()
    for step in range(STEPS_DG):
        for k in range(8):
            face_copy(step, k).wait_send()


SLAB = 64


def ocean_kernel(solid_in, wave_in, force_in, solid_out, ocean_out, bed_out, held, wave, force, ocean, bed, sems, out_sems):
    pieces = SIDE // SLAB
    spans = [slice(0 if piece == 0 else piece * SLAB + 16, (piece + 1) * SLAB + 16) for piece in range(pieces)]
    fetches = [
        (pltpu.make_async_copy(wave_in.at[:, span], wave.at[:, span], sems.at[0, piece]),
         pltpu.make_async_copy(force_in.at[span], force.at[span], sems.at[1, piece]))
        for piece, span in enumerate(spans)]
    for pair in fetches:
        for copy in pair:
            copy.start()
    fetch = pltpu.make_async_copy(solid_in, held, out_sems.at[2, 0])
    fetch.start()
    store = pltpu.make_async_copy(held, solid_out, out_sems.at[2, 1])
    stores = []
    for piece in range(pieces):
        for copy in fetches[piece]:
            copy.wait()
        if piece == 1:
            fetch.wait()
            store.start()
        begin = piece * SLAB
        span = slice(begin, begin + SLAB + 16)
        lift = force[span, :]
        depth = wave[0, span, :]
        slope_x, slope_y = slopes(lift)
        scale = 0.5 * step_ocean * step_ocean
        mom_x = wave[3, span, :] - scale * (depth * slope_x)
        mom_y = wave[4, span, :] - scale * (depth * slope_y)
        b = wave[1, span, :] + (2 * step_ocean) * lift
        result = shallow_update(wave[2, span, :], mom_x, mom_y, b)
        inner = slice(begin, begin + SLAB)
        for i in range(3):
            ocean[i, inner, :] = result[i][8:SLAB + 8, 0:SIDE]
        bed[inner, :] = b[8:SLAB + 8, 0:SIDE]
        stores.append(pltpu.make_async_copy(ocean.at[:, inner], ocean_out.at[:, inner], out_sems.at[0, piece]))
        stores.append(pltpu.make_async_copy(bed.at[inner], bed_out.at[inner], out_sems.at[1, piece]))
        for copy in stores[-2:]:
            copy.start()
    for copy in stores:
        copy.wait()
    store.wait()


def per_device(
    n_gx, n_gy,
    coefficients, jacobian, face_normals, wave_speed, star_mats, deriv_mats, stiff_mats, source_mat,
    trace_mats, lift_mats, face_partner, send_faces, sea_face, sea_row, sea_base, interp_mat,
    water_depth, momentum, bottom,
):
    vm = pl.BlockSpec(memory_space=pltpu.VMEM)
    anywhere = pl.BlockSpec(memory_space=pl.ANY)
    slots = n_gy * CAP
    whole = (FIELDS, 7, 8, ELEMENTS)
    floats = lambda *shape: pltpu.VMEM(shape, F32)
    shorts = lambda *shape: pltpu.VMEM(shape, BF16)
    dma = pltpu.SemaphoreType.DMA
    scratch = [
        floats(*whole),
        floats(7, EXT_X, EXT_Y),
        floats(4, SIDE, SIDE),
        floats(4, 24, BASIS),
        floats(4, 24, BASIS),
        floats(16, 24),
        floats(4, 16, 16),
        shorts(168, 168),
        shorts(168, 168),
        shorts(96, 168),
        shorts(64, 168),
        shorts(56, 192),
        shorts(56, 96),
        shorts(208, 416),
        shorts(104, 416),
        shorts(312, 208),
        shorts(312, 104),
        floats(*whole),
        floats(*whole),
        floats(7, 4 * FIELDS, 8, ELEMENTS),
        floats(ROWS // 8, 8, 4 * ELEMENTS),
        shorts(2 * ROWS, 4 * ELEMENTS),
        floats(ROWS // 8, 8, 4 * ELEMENTS),
        floats(FIELDS, 4, 3, 8, ELEMENTS),
        floats(*whole),
        shorts(4 * ELEMENTS, 512),
        shorts(4 * ELEMENTS, 4 * ELEMENTS),
        shorts(512, 4 * ELEMENTS),
        shorts(4 * ELEMENTS, slots),
        shorts(SIDE, 4 * slots),
        shorts(SIDE, 4 * slots),
        floats(STEPS_DG, 8, HALF, 128),
        floats(STEPS_DG, 8, HALF, 128),
        floats(n_gy, 8, 128),
        floats(n_gy, 8, 128),
        floats(n_gy, 8, 128),
        floats(n_gy, 8, 128),
        floats(4, 8, SIDE),
        floats(4, 8, SIDE),
        floats(4, 8, SIDE),
        floats(2, 4, 8, SIDE),
        floats(2, 4, 8, SIDE),
        floats(4, 4, 8, 128),
        floats(1, 8, SIDE),
        floats(1, 8, SIDE),
        floats(1, 8, SIDE),
        floats(2, 1, 8, SIDE),
        floats(2, 1, 8, SIDE),
        floats(4, 1, 8, 128),
        dma((3,)), dma((2,)),
        dma((STEPS_DG, 8)), dma((STEPS_DG, 8)),
        dma((n_gy - 1,)), dma((n_gy - 1,)), dma((n_gy - 1,)), dma((n_gy - 1,)),
        dma((8,)), dma((8,)), dma((8,)), dma((8,)),
    ]
    solid, wave, force = pl.pallas_call(
        functools.partial(solid_kernel, n_gx, n_gy),
        out_shape=(
            jax.ShapeDtypeStruct(whole, F32),
            jax.ShapeDtypeStruct((5, EXT_X, EXT_Y), F32),
            jax.ShapeDtypeStruct((EXT_X, EXT_Y), F32)),
        in_specs=[vm] * 16 + [anywhere] * 3,
        out_specs=(anywhere, anywhere, vm),
        scratch_shapes=scratch,
        compiler_params=pltpu.CompilerParams(
            collective_id=0, has_side_effects=True, vmem_limit_bytes=60 * 1024 * 1024),
        name="solid",
    )(
        coefficients.reshape(whole), jacobian, face_normals.transpose(1, 0, 2), wave_speed.reshape(1, ELEMENTS),
        deriv_mats, stiff_mats, trace_mats.transpose(1, 0, 2), lift_mats.transpose(2, 0, 1), interp_mat, star_mats, source_mat, face_partner, send_faces,
        sea_face.reshape(1, ELEMENTS), sea_row.reshape(1, ELEMENTS), sea_base.T,
        water_depth, momentum, bottom)
    solid, ocean, bed = pl.pallas_call(
        ocean_kernel,
        out_shape=(
            jax.ShapeDtypeStruct(whole, F32),
            jax.ShapeDtypeStruct((3, SIDE, SIDE), F32),
            jax.ShapeDtypeStruct((SIDE, SIDE), F32)),
        in_specs=[anywhere] * 3,
        out_specs=(anywhere,) * 3,
        scratch_shapes=[
            floats(*whole), floats(5, EXT_X, EXT_Y), floats(EXT_X, EXT_Y), floats(3, SIDE, SIDE), floats(SIDE, SIDE),
            dma((2, SIDE // SLAB)), dma((3, SIDE // SLAB))],
        name="ocean",
    )(solid, wave, force)
    return solid.reshape(FIELDS, BASIS, ELEMENTS), ocean, bed


def solution(mesh):
    in_specs = (
        P(None, None, ("gx", "gy")),
        P(None, None, ("gx", "gy")),
        P(None, None, ("gx", "gy")),
        P(("gx", "gy")),
        P(),
        P(),
        P(),
        P(),
        P(),
        P(),
        P(None, ("gx", "gy")),
        P(None, ("gx", "gy")),
        P(("gx", "gy")),
        P(("gx", "gy"), None),
        P(("gx", "gy"), None),
        P(),
        P("gx", "gy"),
        P(None, "gx", "gy"),
        P("gx", "gy"),
    )
    out_specs = (P(None, None, ("gx", "gy")), P(None, "gx", "gy"), P("gx", "gy"))
    return jax.shard_map(
        functools.partial(per_device, mesh.shape["gx"], mesh.shape["gy"]),
        mesh=mesh, in_specs=in_specs, out_specs=out_specs, check_vma=False,
    )
```

```python
import functools

import jax
import jax.numpy as jnp
from jax import lax
from jax.experimental import pallas as pl
from jax.experimental.pallas import tpu as pltpu
from jax.sharding import PartitionSpec as P

MESH = pl.DeviceIdType.MESH
F32 = jnp.float32
BF16 = jnp.bfloat16

FIELDS = 13
BASIS = 56
FACE_BASIS = 21
CAP = 64
ELEMENTS = 256
SIDE = 256
STEPS_DG = 2

step_solid = 0.4
step_ocean = 0.2
depth_floor = 0.5
vertical_field = 6

OFFSETS = [(-1, -1), (-1, 0), (-1, 1), (0, -1), (0, 1), (1, -1), (1, 0), (1, 1)]
ROWS = 320
HALF = ROWS // 2
EXT_X = SIDE + 16
EXT_Y = SIDE + 128


def mm(a, b):
    return jnp.dot(a, b, preferred_element_type=F32)


def mm_nt(a, b):
    return lax.dot_general(a, b, (((1,), (1,)), ((), ())), preferred_element_type=F32)


def halves(x):
    high = x.astype(BF16)
    return high, (x - high.astype(F32)).astype(BF16)


def triple(x):
    high = x.astype(BF16).astype(F32)
    return jnp.concatenate([high, x - high, high], axis=0).astype(BF16)


def one_hot(index_row, rows):
    width = index_row.shape[1]
    index = jnp.broadcast_to(index_row, (16, width)).astype(jnp.int16)
    iota = lax.broadcasted_iota(jnp.int32, (16, width), 0).astype(jnp.int16)
    apart = index - iota
    one, zero = jnp.ones((16, width), BF16), jnp.zeros((16, width), BF16)
    return jnp.concatenate(
        [jnp.where(apart == jnp.int16(16 * tile), one, zero) for tile in range(rows // 16)], axis=0)


def low_lanes(shape):
    return lax.broadcasted_iota(jnp.int32, shape, len(shape) - 1) < 64


def swap_lanes(x):
    return pltpu.roll(x, 64, x.ndim - 1)


def iota2(shape, axis):
    return lax.broadcasted_iota(jnp.int32, shape, axis)


def bits(condition):
    return jnp.where(condition, 1.0, 0.0).astype(BF16)


def lane_triple(w):
    high, low = halves(w)
    k, n = iota2((BASIS, 3 * BASIS), 0), iota2((BASIS, 3 * BASIS), 1)
    return (mm(high, bits((n == k) | (n == k + BASIS))) + mm(low, bits(n == k + 2 * BASIS))).astype(BF16)


def shallow_update(height, mom_x, mom_y, b, extra=None):
    safe = jnp.maximum(height, depth_floor)
    root = lax.rsqrt(safe)
    inv = root * root
    vel_x = mom_x * inv
    vel_y = mom_y * inv
    celerity = safe * root
    cross = mom_x * vel_y
    press = 0.5 * height * height
    n, m = height.shape
    fluxes = (
        (0, n, (mom_x, mom_x * vel_x + press, cross), jnp.abs(vel_x) + celerity),
        (1, m, (mom_y, cross, mom_y * vel_y + press), jnp.abs(vel_y) + celerity))
    state = (height, mom_x, mom_y)
    change = [0.0, 0.0, 0.0]
    for axis, size, flux, speed in fluxes:
        wave = jnp.maximum(speed, pltpu.roll(speed, size - 1, axis))
        for i in range(3):
            face = (flux[i] + pltpu.roll(flux[i], size - 1, axis)) - wave * (
                pltpu.roll(state[i], size - 1, axis) - state[i])
            change[i] = change[i] + (face - pltpu.roll(face, 1, axis))
    half = 0.5 * step_ocean
    slope_x, slope_y = slopes(b)
    return (
        height - half * change[0],
        mom_x - half * (change[1] + height * slope_x),
        mom_y - half * (change[2] + height * slope_y))


def slopes(b):
    n, m = b.shape
    return (
        pltpu.roll(b, n - 1, 0) - pltpu.roll(b, 1, 0),
        pltpu.roll(b, m - 1, 1) - pltpu.roll(b, 1, 1))


def solid_kernel(
    n_gx, n_gy,
    coef, jac, nrm, spd, deriv, stiff, trace_in, lift_in, interp, stars, source, partner, send,
    sea_face, sea_row, sea_base, depth, mom, bottom,
    solid_out, ocean_out, bed_out,
    solid, wave, force_ext, ocean, bed, sea0, tpad, lpad, ipad, spad, dcat, scat, tcat, vcat, lift1, lift2, kron, kron_high, rotate1, rotate2,
    ddt, integral, mixed, table, tsplit, outer, flux, volume,
    hot_send, hot_local, hot_remote, hot_slot, hot_x, hot_y,
    msg, got, corner_msg, corner_got, rate_msg, rate_got,
    u_top, u_bot, u_strip, u_row_got, u_strip_got, u_corner_got,
    f_top, f_bot, f_strip, f_row_got, f_strip_got, f_corner_got,
    load_sem, store_sem, ocean_sem,
    face_send, face_recv, corner_send, corner_recv, rate_send, rate_recv,
    uh_send, uh_recv, fh_send, fh_recv,
):
    gx = lax.axis_index("gx")
    gy = lax.axis_index("gy")
    slots = n_gy * CAP

    def at(dx, dy):
        return (lax.rem(gx + dx + n_gx, n_gx), lax.rem(gy + dy + n_gy, n_gy))

    barrier = pltpu.get_barrier_semaphore()
    peers = [at(dx, dy) for dx, dy in OFFSETS] + [at(0, off) for off in range(2, n_gy - 1)]
    for peer in peers:
        pl.semaphore_signal(barrier, inc=1, device_id=peer, device_id_type=MESH)

    fetched = pltpu.make_async_copy(coef, solid, load_sem.at[3])
    fetched.start()
    loads = [
        pltpu.make_async_copy(depth, sea0.at[0], load_sem.at[0]),
        pltpu.make_async_copy(mom, sea0.at[1:3], load_sem.at[1]),
        pltpu.make_async_copy(bottom, sea0.at[3], load_sem.at[2])]
    for copy in loads:
        copy.start()

    def face_copy(step, k):
        return pltpu.make_async_remote_copy(
            src_ref=msg.at[step, k], dst_ref=got.at[step, 7 - k],
            send_sem=face_send.at[step, k], recv_sem=face_recv.at[step, 7 - k],
            device_id=at(*OFFSETS[k]), device_id_type=MESH)

    def face_arrival(step, k):
        return pltpu.make_async_remote_copy(
            src_ref=msg.at[step, k], dst_ref=got.at[step, k],
            send_sem=face_send.at[step, k], recv_sem=face_recv.at[step, k],
            device_id=at(*OFFSETS[k]), device_id_type=MESH)

    def row_copy(source_ref, target_ref, sends, recvs, off):
        there = lax.rem(gy + off, n_gy)
        return pltpu.make_async_remote_copy(
            src_ref=source_ref.at[there], dst_ref=target_ref.at[gy],
            send_sem=sends.at[off - 1], recv_sem=recvs.at[off - 1],
            device_id=(gx, there), device_id_type=MESH)

    def row_arrival(source_ref, target_ref, sends, recvs, off):
        origin = lax.rem(gy - off + n_gy, n_gy)
        return pltpu.make_async_remote_copy(
            src_ref=source_ref.at[origin], dst_ref=target_ref.at[origin],
            send_sem=sends.at[off - 1], recv_sem=recvs.at[off - 1],
            device_id=(gx, origin), device_id_type=MESH)

    def halo_copies(top, bot, strip, rows_got, strips_got, corners_got, sends, recvs):
        sources = [
            top.at[:, :, 0:128], top, top.at[:, :, 128:256], strip, strip,
            bot.at[:, :, 0:128], bot, bot.at[:, :, 128:256]]
        targets = [
            corners_got.at[0], rows_got.at[0], corners_got.at[1], strips_got.at[0],
            strips_got.at[1], corners_got.at[2], rows_got.at[1], corners_got.at[3]]
        return [
            pltpu.make_async_remote_copy(
                src_ref=sources[k], dst_ref=targets[k],
                send_sem=sends.at[k], recv_sem=recvs.at[k],
                device_id=at(*OFFSETS[k]), device_id_type=MESH)
            for k in range(8)]

    def by_block(ref):
        tiles = ref[...].reshape(3, 7, 8, BASIS)
        return jnp.concatenate([tiles[d, block] for block in range(7) for d in range(3)], axis=0)

    dcat[...] = lane_triple(by_block(deriv))
    scat[...] = lane_triple(by_block(stiff))
    tpad[...] = jnp.zeros(tpad.shape, F32)
    lpad[...] = jnp.zeros(lpad.shape, F32)
    ipad[...] = jnp.zeros(ipad.shape, F32)
    spad[...] = jnp.zeros(spad.shape, F32)
    ipad[:, 0:FACE_BASIS] = interp[...]
    for face in range(4):
        tpad[face, 0:FACE_BASIS, :] = trace_in[:, face, :]
        lpad[face, 0:FACE_BASIS, :] = lift_in[:, face, :]
    for c in range(3):
        spad[c, 0:FIELDS, 0:FIELDS] = stars[c]
    spad[3, 0:FIELDS, 0:FIELDS] = source[...]
    tcat[...] = lane_triple(tpad[...].reshape(96, BASIS))

    repeat = bits(jnp.right_shift(iota2((104, 16), 0), 3) == iota2((104, 16), 1))
    tall = [[mm(repeat, part).astype(BF16) for part in halves(spad[c])] for c in range(4)]

    def spread(part, columns, starts):
        total = jnp.zeros((104, columns), F32)
        k = iota2((16, columns), 0)
        n = jnp.right_shift(iota2((16, columns), 1), 3)
        for c, start in starts:
            total = total + mm(tall[c][part], bits((n == k + start) & (k < FIELDS)))
        same = jnp.bitwise_and(iota2((104, columns), 0), 7) == jnp.bitwise_and(iota2((104, columns), 1), 7)
        return jnp.where(same, total, 0.0)

    every = [(c, c * FIELDS) for c in range(4)]
    def woven(parts):
        return jnp.concatenate([part[8 * g:8 * g + 8] for g in range(FIELDS) for part in parts], axis=0).astype(BF16)

    kron_parts = [spread(0, 416, every), spread(1, 416, every)]
    kron[...] = woven(kron_parts)
    kron_high[...] = kron_parts[0].astype(BF16)

    def one_hot_face_sends():
        for pair in range(4):
            index = jnp.concatenate([send[2 * pair:2 * pair + 1, :], send[2 * pair + 1:2 * pair + 2, :]], axis=1)
            hot_send[:, pair * 128:(pair + 1) * 128] = one_hot(index, 4 * ELEMENTS)

    def star(x, groups):
        high, low = halves(x)
        both = mm(kron[:, 0:8 * groups], high).reshape(FIELDS, 2, 8, ELEMENTS)
        return both[:, 0] + both[:, 1] + mm(kron_high[:, 0:8 * groups], low).reshape(FIELDS, 8, ELEMENTS)

    def directional(source_ref, weights, with_source, store):
        for h in range(FIELDS):
            q = source_ref[h].reshape(BASIS, ELEMENTS)
            spatial = mm(weights[...], triple(q))
            for block in range(7):
                parts = [spatial[24 * block + 8 * d:24 * block + 8 * d + 8] for d in range(3)]
                for c in range(3):
                    mixed[block, c * FIELDS + h] = (
                        jac[0, c:c + 1, :] * parts[0] + jac[1, c:c + 1, :] * parts[1] + jac[2, c:c + 1, :] * parts[2])
            if with_source:
                mixed[:, 3 * FIELDS + h] = source_ref[h]
        groups = 4 * FIELDS if with_source else 3 * FIELDS
        for block in range(7):
            result = star(mixed[block, 0:groups].reshape(8 * groups, ELEMENTS), groups)
            store(block, result)

    def later_matrices():
        rotate1[...] = woven([spread(0, 208, [(c, 0), (c, FIELDS)]) for c in range(3)])
        rotate2[...] = woven([spread(1, 104, [(c, 0)]) for c in range(3)])
        first = jnp.zeros((BASIS, 192), F32)
        second = jnp.zeros((BASIS, 96), F32)
        for face in range(4):
            same = bits(iota2((BASIS, BASIS), 0) == iota2((BASIS, BASIS), 1))
            high, low = [mm_nt(same, part).astype(BF16) for part in halves(lpad[face])]
            k, n = iota2((24, 192), 0) + 24 * face, iota2((24, 192), 1)
            first = first + mm(high, bits((n == k) | (n == k + 96)))
            second = second + mm(low, bits(iota2((24, 96), 1) == iota2((24, 96), 0) + 24 * face))
        lift1[...] = first.astype(BF16)
        lift2[...] = second.astype(BF16)
        i_high, i_low = halves(ipad[...])
        points = []
        for face in range(4):
            t_high, t_low = halves(tpad[face])
            points.append(mm(i_high, t_high) + mm(i_high, t_low) + mm(i_low, t_high))
        vcat[...] = lane_triple(jnp.concatenate(points, axis=0))

    pick_row = iota2((8, SIDE), 0)
    edge = bits(iota2((8, SIDE), 1) == jnp.where(pick_row < 4, pick_row, pick_row + (SIDE - 8)))

    def strip_of(x):
        high, low = halves(x)
        rest = (x - high.astype(F32) - low.astype(F32)).astype(BF16)
        return mm_nt(edge, high) + mm_nt(edge, low) + mm_nt(edge, rest)

    uh = halo_copies(u_top, u_bot, u_strip, u_row_got, u_strip_got, u_corner_got, uh_send, uh_recv)

    def send_inputs():
        for copy in loads:
            copy.wait()
        for field in range(4):
            u_top[field] = sea0[field, 0:8, :]
            u_bot[field] = sea0[field, SIDE - 8:SIDE, :]
            u_strip[field] = strip_of(sea0[field])
        rows = sea_row[...]
        hits = jnp.where(iota2((n_gy, ELEMENTS), 0) == rows, 1.0, 0.0)
        tri = bits(iota2((ELEMENTS, ELEMENTS), 0) < iota2((ELEMENTS, ELEMENTS), 1))
        before = mm(hits.astype(BF16), tri)
        slot = jnp.sum(before * hits, axis=0, keepdims=True).astype(jnp.int32)
        placed = one_hot(rows * CAP + slot, slots)
        line = iota2((8, ELEMENTS), 0)
        values = jnp.where(line == 0, sea_face[...], jnp.where(
            line == 1, sea_base[0:1, :], sea_base[1:2, :])).astype(F32) + 1.0
        high, low = halves(values)
        found = mm_nt(high, placed) + mm_nt(low, placed)
        for pair in range(n_gy // 2):
            block = found[:, pair * 128:(pair + 1) * 128]
            corner_msg[2 * pair] = block
            corner_msg[2 * pair + 1] = swap_lanes(block)
        for copy in uh:
            copy.start()
        for off in range(1, n_gy):
            row_copy(corner_msg, corner_got, corner_send, corner_recv, off).start()
        corner_got[gy] = corner_msg[gy]
        return found[0:1, :].astype(jnp.int32) - 1

    side8 = low_lanes((8, 128))

    iota16 = iota2((16, 128), 0).astype(jnp.int16)
    one16, zero16 = jnp.ones((16, 128), BF16), jnp.zeros((16, 128), BF16)

    def position_tables():
        for off in range(1, n_gy):
            row_arrival(corner_msg, corner_got, corner_send, corner_recv, off).wait_recv()
        for pair in range(n_gy // 2):
            corner = jnp.where(side8, corner_got[2 * pair], swap_lanes(corner_got[2 * pair + 1])).astype(jnp.int32)
            for hot, line in ((hot_x, 1), (hot_y, 2)):
                apart = jnp.broadcast_to(corner[line:line + 1, :] - 1, (16, 128)).astype(jnp.int16) - iota16
                for tile in range(SIDE // 16):
                    for j in range(4):
                        base = pair * 512 + j * 128
                        hot[16 * tile:16 * tile + 16, base:base + 128] = jnp.where(
                            apart == jnp.int16(16 * tile - j), one16, zero16)

    up_in = gx > 0
    down_in = gx < n_gx - 1
    left_in = gy > 0
    right_in = gy < n_gy - 1

    def place_halo(target, rows_got, strips_got, corners_got, field):
        target[0:8, 0:SIDE] = jnp.where(up_in, rows_got[1, field], 0.0)
        target[8 + SIDE:EXT_X, 0:SIDE] = jnp.where(down_in, rows_got[0, field], 0.0)
        strip = jnp.concatenate([
            jnp.where(right_in, strips_got[0, field], 0.0), jnp.zeros((112, SIDE), F32),
            jnp.where(left_in, strips_got[1, field], 0.0)], axis=0)
        target[8:8 + SIDE, SIDE:EXT_Y] = jnp.transpose(strip)
        target[0:8, SIDE:EXT_Y] = jnp.where(
            side8, jnp.where(up_in & right_in, corners_got[2, field], 0.0),
            jnp.where(up_in & left_in, corners_got[3, field], 0.0))
        target[8 + SIDE:EXT_X, SIDE:EXT_Y] = jnp.where(
            side8, jnp.where(down_in & right_in, corners_got[0, field], 0.0),
            jnp.where(down_in & left_in, corners_got[1, field], 0.0))

    def ocean_first_step():
        for copy in uh:
            copy.wait_recv()
        for field in range(4):
            row = (0, 5, 6, 1)[field]
            wave[row, 8:8 + SIDE, 0:SIDE] = sea0[field]
            place_halo(wave.at[row], u_row_got, u_strip_got, u_corner_got, field)

        def part(begin, rows, inner_from, inner_to):
            span = pl.ds(begin, rows)
            result = shallow_update(wave[0, span, :], wave[5, span, :], wave[6, span, :], wave[1, span, :])
            x = begin + iota2((rows, EXT_Y), 0)
            y = iota2((rows, EXT_Y), 1)
            out = ((x < 8) & (gx == 0)) | ((x >= 8 + SIDE) & (gx == n_gx - 1))
            out = out | ((y >= SIDE) & (y < SIDE + 64) & (gy == n_gy - 1)) | ((y >= SIDE + 64) & (gy == 0))
            for i in range(3):
                wave[2 + i, pl.ds(begin + inner_from, inner_to - inner_from), :] = jnp.where(
                    out, 0.0, result[i])[inner_from:inner_to]

        @pl.loop(0, SIDE // SLAB)
        def _(s):
            part(pl.multiple_of(s * SLAB, 8), SLAB + 16, 8, SLAB + 8)
        part(0, 16, 0, 8)
        part(EXT_X - 16, 16, 8, 16)

    first_factor = step_solid * step_solid / 2
    second_factor = first_factor * step_solid / 3
    table[ROWS // 8 - 1] = jnp.zeros((8, 4 * ELEMENTS), F32)

    fetched.wait()
    for step in range(STEPS_DG):
        state = solid

        def store_first(block, value):
            ddt[:, block] = value
        directional(state, dcat, True, store_first)

        def store_second(block, value):
            integral[:, block] = step_solid * state[:, block] - first_factor * ddt[:, block] + second_factor * value
        directional(ddt, dcat, True, store_second)

        if step == 0:
            one_hot_face_sends()
        for g in range(FIELDS):
            trace = mm(tcat[...], triple(integral[g].reshape(BASIS, ELEMENTS)))
            for face in range(4):
                table[3 * g:3 * g + 3, :, face * ELEMENTS:(face + 1) * ELEMENTS] = (
                    trace[face * 24:(face + 1) * 24].reshape(3, 8, ELEMENTS))
        for tile in range(ROWS // 16):
            high, low = halves(table[2 * tile:2 * tile + 2].reshape(16, 4 * ELEMENTS))
            tsplit[32 * tile:32 * tile + 16] = high
            tsplit[32 * tile + 16:32 * tile + 32] = low

        low_side = low_lanes((HALF, 128))
        picked = mm(tsplit[...], hot_send[...]).reshape(ROWS // 16, 2, 16, 512)
        picked = (picked[:, 0] + picked[:, 1]).reshape(ROWS, 512)
        for pair in range(4):
            block = picked[:, pair * 128:(pair + 1) * 128]
            top, bot = block[0:HALF], block[HALF:ROWS]
            msg[step, 2 * pair] = jnp.where(low_side, top, swap_lanes(bot))
            msg[step, 2 * pair + 1] = jnp.where(low_side, swap_lanes(top), bot)
        if step == 0:
            pl.semaphore_wait(barrier, len(peers))
        for k in range(8):
            face_copy(step, k).start()

        if step == 0:
            slot_code = send_inputs()
            for face in range(4):
                code = partner[face:face + 1, :]
                cols = slice(face * ELEMENTS, (face + 1) * ELEMENTS)
                hot_local[:, cols] = one_hot(code, 4 * ELEMENTS)
                hot_remote[:, cols] = one_hot(code - 4 * ELEMENTS, 8 * 64)
            later_matrices()
        else:
            hot_slot[...] = one_hot(slot_code, 4 * ELEMENTS)
        for face in range(4):
            cols = slice(face * ELEMENTS, (face + 1) * ELEMENTS)
            local = mm(tsplit[...], hot_local[:, cols])
            local = local.reshape(ROWS // 16, 2, 16, ELEMENTS)
            outer[:, :, cols] = (local[:, 0] + local[:, 1]).reshape(ROWS // 8, 8, ELEMENTS)

        def store_volume(block, value):
            volume[:, block] = value
        directional(integral, scat, False, store_volume)
        if step == 1:
            position_tables()

        for k in range(8):
            face_arrival(step, k).wait_recv()
        for pair in range(4):
            a, b = got[step, 2 * pair], got[step, 2 * pair + 1]
            top = jnp.where(low_side, a, swap_lanes(b))
            bot = jnp.where(low_side, swap_lanes(a), b)
            cols = slice(pair * 128, (pair + 1) * 128)
            for begin, part in ((0, top), (HALF, bot)):
                for tile in range(HALF // 16):
                    high, low = halves(part[16 * tile:16 * tile + 16])
                    row = 2 * (begin + 16 * tile)
                    tsplit[row:row + 16, cols] = high
                    tsplit[row + 16:row + 32, cols] = low
        for face in range(4):
            cols = slice(face * ELEMENTS, (face + 1) * ELEMENTS)
            remote = mm(tsplit[:, 0:512], hot_remote[:, cols])
            remote = remote.reshape(ROWS // 16, 2, 16, ELEMENTS)
            outer[:, :, cols] = outer[:, :, cols] + (remote[:, 0] + remote[:, 1]).reshape(ROWS // 8, 8, ELEMENTS)
        for face in range(4):
            cols = slice(face * ELEMENTS, (face + 1) * ELEMENTS)
            normal = [0.5 * nrm[c, face:face + 1, :] for c in range(3)]
            speed = 0.5 * spd[...]
            for block in range(3):
                ids = [3 * g + block for g in range(FIELDS)]
                total = jnp.concatenate([table[i, :, cols] + outer[i, :, cols] for i in ids], axis=0)
                high = total.astype(BF16).astype(F32)
                both = jnp.concatenate([high, total - high], axis=0).astype(BF16)
                turned = mm(rotate1[...], both) + mm(rotate2[...], both[0:104])
                for g in range(FIELDS):
                    value = speed * (table[ids[g], :, cols] - outer[ids[g], :, cols])
                    for c in range(3):
                        value = value + normal[c] * turned[24 * g + 8 * c:24 * g + 8 * c + 8]
                    flux[g, face, block] = value
        for g in range(FIELDS):
            f = flux[g].reshape(96, ELEMENTS)
            high = f.astype(BF16).astype(F32)
            both = jnp.concatenate([high, f - high], axis=0).astype(BF16)
            lifted = mm(lift1[...], both) + mm(lift2[...], both[0:96])
            solid[g] = state[g] + volume[g] - lifted.reshape(7, 8, ELEMENTS)

    point = mm(vcat[...], triple(solid[vertical_field].reshape(BASIS, ELEMENTS)))
    points = jnp.concatenate([point[16 * f:16 * f + 16] for f in range(4)], axis=1)
    high = points.astype(BF16).astype(F32)
    both = jnp.concatenate([high, points - high], axis=0).astype(BF16)
    rates = mm(both, hot_slot[...])
    rates = rates[0:16] + rates[16:32]
    for pair in range(n_gy // 2):
        a = rates[0:8, pair * 128:(pair + 1) * 128]
        b = rates[8:16, pair * 128:(pair + 1) * 128]
        rate_msg[2 * pair] = jnp.where(side8, a, swap_lanes(b))
        rate_msg[2 * pair + 1] = jnp.where(side8, swap_lanes(a), b)
    for off in range(1, n_gy):
        row_copy(rate_msg, rate_got, rate_send, rate_recv, off).start()
    rate_got[gy] = rate_msg[gy]
    saved = pltpu.make_async_copy(solid, solid_out, store_sem.at[0])
    saved.start()

    ocean_first_step()

    for off in range(1, n_gy):
        row_arrival(rate_msg, rate_got, rate_send, rate_recv, off).wait_recv()
    edge_row = jnp.where(iota2((16, 128), 0) < 8, iota2((16, 128), 0), iota2((16, 128), 0) + (SIDE - 16))
    edge_col = jnp.where(iota2((8, 128), 0) < 4, iota2((8, 128), 0), iota2((8, 128), 0) + (SIDE - 8))
    pairs = []
    for pair in range(n_gy // 2):
        corner = jnp.where(side8, corner_got[2 * pair], swap_lanes(corner_got[2 * pair + 1])).astype(jnp.int32)
        a, b = rate_got[2 * pair], rate_got[2 * pair + 1]
        first = jnp.where(side8, a, swap_lanes(b))
        second = jnp.where(side8, swap_lanes(a), b)
        rate = [[first[j:j + 1] for j in range(4)], [first[4 + j:5 + j] for j in range(4)],
                [second[j:j + 1] for j in range(4)], [second[4 + j:5 + j] for j in range(4)]]
        pairs.append((corner, rate))

    def chosen(masks, values):
        return jnp.where(masks[0], values[0], jnp.where(masks[1], values[1], jnp.where(
            masks[2], values[2], jnp.where(masks[3], values[3], 0.0))))

    row_parts = [[None] * len(pairs) for _ in range(4)]
    col_parts = [[None] * len(pairs) for _ in range(4)]
    for index, (corner, rate) in enumerate(pairs):
        apart_x = edge_row + 1 - corner[1:2, :]
        apart_y = edge_col + 1 - corner[2:3, :]
        masks_x = [apart_x == i for i in range(4)]
        masks_y = [apart_y == i for i in range(4)]
        for j in range(4):
            row_parts[j][index] = chosen(masks_x, [rate[i][j] for i in range(4)])
            col_parts[j][index] = chosen(masks_y, [rate[j][i] for i in range(4)])

    def summed(parts, table_ref):
        whole = jnp.concatenate([row[pair] for pair in range(n_gy // 2) for row in parts], axis=1)
        high = whole.astype(BF16).astype(F32)
        stacked = jnp.concatenate([high, whole - high], axis=0).astype(BF16)
        width = 2 * slots
        result = mm_nt(stacked[:, 0:width], table_ref[:, 0:width]) + mm_nt(stacked[:, width:], table_ref[:, width:])
        return result[0:whole.shape[0]] + result[whole.shape[0]:]

    edge_rows = summed(row_parts, hot_y)
    f_top[0] = edge_rows[0:8]
    f_bot[0] = edge_rows[8:16]
    f_strip[0] = summed(col_parts, hot_x)
    fh = halo_copies(f_top, f_bot, f_strip, f_row_got, f_strip_got, f_corner_got, fh_send, fh_recv)
    for copy in fh:
        copy.start()

    force_ext[8:8 + SIDE, 0:SIDE] = jnp.zeros((SIDE, SIDE), F32)

    @pl.loop(0, n_gy // 2, unroll=2)
    def _(pair):
        corner = jnp.where(side8, corner_got[2 * pair], swap_lanes(corner_got[2 * pair + 1])).astype(jnp.int32)
        a, b = rate_got[2 * pair], rate_got[2 * pair + 1]
        first = jnp.where(side8, a, swap_lanes(b))
        second = jnp.where(side8, swap_lanes(a), b)
        wide = []
        for line in [first[i:i + 1] for i in range(8)] + [second[i:i + 1] for i in range(8)]:
            wide.append(halves(jnp.broadcast_to(line, (16, 128))))
        apart = jnp.broadcast_to(corner[1:2, :] - 1, (16, 128)).astype(jnp.int16) - iota16
        columns = [[] for _ in range(4)]
        for tile in range(SIDE // 16):
            masks = [apart == jnp.int16(16 * tile - i) for i in range(4)]
            for j in range(4):
                for part in range(2):
                    value = zero16
                    for i in range(4):
                        value = jnp.where(masks[i], wide[4 * i + j][part], value)
                    columns[j].append(value)
        total = jnp.zeros((2 * SIDE, SIDE), F32)
        for half in range(2):
            table_part = hot_y[:, pl.ds(pl.multiple_of(pair * 512 + half * 256, 256), 256)]
            left = jnp.concatenate([jnp.concatenate(columns[2 * half + j], axis=0) for j in range(2)], axis=1)
            total = total + mm_nt(left, table_part)
        total = total.reshape(SIDE // 16, 2, 16, SIDE)
        total = (total[:, 0] + total[:, 1]).reshape(SIDE, SIDE)
        force_ext[8:8 + SIDE, 0:SIDE] = force_ext[8:8 + SIDE, 0:SIDE] + total

    for copy in fh:
        copy.wait_recv()
    place_halo(force_ext, f_row_got, f_strip_got, f_corner_got, 0)

    stores = []
    for piece in range(SIDE // SLAB):
        begin = piece * SLAB
        span = slice(begin, begin + SLAB + 16)
        inner = slice(begin, begin + SLAB)
        lift = force_ext[span, :]
        depth_0 = wave[0, span, :]
        slope_x, slope_y = slopes(lift)
        scale = 0.5 * step_ocean * step_ocean
        mom_x = wave[3, span, :] - scale * (depth_0 * slope_x)
        mom_y = wave[4, span, :] - scale * (depth_0 * slope_y)
        b = wave[1, span, :] + (2 * step_ocean) * lift
        result = shallow_update(wave[2, span, :], mom_x, mom_y, b)
        for i in range(3):
            ocean[i, inner, :] = result[i][8:SLAB + 8, 0:SIDE]
        bed[inner, :] = b[8:SLAB + 8, 0:SIDE]
        stores.append(pltpu.make_async_copy(ocean.at[:, inner], ocean_out.at[:, inner], ocean_sem.at[0, piece]))
        stores.append(pltpu.make_async_copy(bed.at[inner], bed_out.at[inner], ocean_sem.at[1, piece]))
        for copy in stores[-2:]:
            copy.start()

    saved.wait()
    for copy in stores:
        copy.wait()
    for copy in uh + fh:
        copy.wait_send()
    for off in range(1, n_gy):
        row_copy(corner_msg, corner_got, corner_send, corner_recv, off).wait_send()
        row_copy(rate_msg, rate_got, rate_send, rate_recv, off).wait_send()
    for step in range(STEPS_DG):
        for k in range(8):
            face_copy(step, k).wait_send()


SLAB = 64


def hand_over(solid_in, ocean_in, bed_in, solid_out, ocean_out, bed_out, solid, ocean, bed, in_sems, out_sems):
    parts = [(solid_in.at[g:g + 4], solid.at[g:g + 4], solid_out.at[g:g + 4]) for g in range(0, 12, 4)]
    parts += [(solid_in.at[12:13], solid.at[12:13], solid_out.at[12:13])]
    parts += [(ocean_in.at[i], ocean.at[i], ocean_out.at[i]) for i in range(3)]
    parts += [(bed_in, bed, bed_out)]
    fetches = [pltpu.make_async_copy(part[0], part[1], in_sems.at[n]) for n, part in enumerate(parts)]
    stores = [pltpu.make_async_copy(part[1], part[2], out_sems.at[n]) for n, part in enumerate(parts)]
    for copy in fetches:
        copy.start()
    for fetch, store in zip(fetches, stores):
        fetch.wait()
        store.start()
    for copy in stores:
        copy.wait()


def per_device(
    n_gx, n_gy,
    coefficients, jacobian, face_normals, wave_speed, star_mats, deriv_mats, stiff_mats, source_mat,
    trace_mats, lift_mats, face_partner, send_faces, sea_face, sea_row, sea_base, interp_mat,
    water_depth, momentum, bottom,
):
    vm = pl.BlockSpec(memory_space=pltpu.VMEM)
    anywhere = pl.BlockSpec(memory_space=pl.ANY)
    slots = n_gy * CAP
    whole = (FIELDS, 7, 8, ELEMENTS)
    floats = lambda *shape: pltpu.VMEM(shape, F32)
    shorts = lambda *shape: pltpu.VMEM(shape, BF16)
    dma = pltpu.SemaphoreType.DMA
    scratch = [
        floats(*whole),
        floats(7, EXT_X, EXT_Y),
        floats(EXT_X, EXT_Y),
        floats(3, SIDE, SIDE),
        floats(SIDE, SIDE),
        floats(4, SIDE, SIDE),
        floats(4, 24, BASIS),
        floats(4, 24, BASIS),
        floats(16, 24),
        floats(4, 16, 16),
        shorts(168, 168),
        shorts(168, 168),
        shorts(96, 168),
        shorts(64, 168),
        shorts(56, 192),
        shorts(56, 96),
        shorts(208, 416),
        shorts(104, 416),
        shorts(312, 208),
        shorts(312, 104),
        floats(*whole),
        floats(*whole),
        floats(7, 4 * FIELDS, 8, ELEMENTS),
        floats(ROWS // 8, 8, 4 * ELEMENTS),
        shorts(2 * ROWS, 4 * ELEMENTS),
        floats(ROWS // 8, 8, 4 * ELEMENTS),
        floats(FIELDS, 4, 3, 8, ELEMENTS),
        floats(*whole),
        shorts(4 * ELEMENTS, 512),
        shorts(4 * ELEMENTS, 4 * ELEMENTS),
        shorts(512, 4 * ELEMENTS),
        shorts(4 * ELEMENTS, slots),
        shorts(SIDE, 4 * slots),
        shorts(SIDE, 4 * slots),
        floats(STEPS_DG, 8, HALF, 128),
        floats(STEPS_DG, 8, HALF, 128),
        floats(n_gy, 8, 128),
        floats(n_gy, 8, 128),
        floats(n_gy, 8, 128),
        floats(n_gy, 8, 128),
        floats(4, 8, SIDE),
        floats(4, 8, SIDE),
        floats(4, 8, SIDE),
        floats(2, 4, 8, SIDE),
        floats(2, 4, 8, SIDE),
        floats(4, 4, 8, 128),
        floats(1, 8, SIDE),
        floats(1, 8, SIDE),
        floats(1, 8, SIDE),
        floats(2, 1, 8, SIDE),
        floats(2, 1, 8, SIDE),
        floats(4, 1, 8, 128),
        dma((4,)), dma((2,)), dma((2, SIDE // SLAB)),
        dma((STEPS_DG, 8)), dma((STEPS_DG, 8)),
        dma((n_gy - 1,)), dma((n_gy - 1,)), dma((n_gy - 1,)), dma((n_gy - 1,)),
        dma((8,)), dma((8,)), dma((8,)), dma((8,)),
    ]
    results = (
        jax.ShapeDtypeStruct(whole, F32),
        jax.ShapeDtypeStruct((3, SIDE, SIDE), F32),
        jax.ShapeDtypeStruct((SIDE, SIDE), F32))
    made = pl.pallas_call(
        functools.partial(solid_kernel, n_gx, n_gy),
        out_shape=results,
        in_specs=[anywhere] + [vm] * 15 + [anywhere] * 3,
        out_specs=(anywhere,) * 3,
        scratch_shapes=scratch,
        compiler_params=pltpu.CompilerParams(
            collective_id=0, has_side_effects=True, vmem_limit_bytes=60 * 1024 * 1024),
        name="solid",
    )(
        coefficients.reshape(whole), jacobian, face_normals.transpose(1, 0, 2), wave_speed.reshape(1, ELEMENTS),
        deriv_mats, stiff_mats, trace_mats.transpose(1, 0, 2), lift_mats.transpose(2, 0, 1), interp_mat, star_mats, source_mat, face_partner, send_faces,
        sea_face.reshape(1, ELEMENTS), sea_row.reshape(1, ELEMENTS), sea_base.T,
        water_depth, momentum, bottom)
    solid, ocean, bed = pl.pallas_call(
        hand_over,
        out_shape=results,
        in_specs=[anywhere] * 3,
        out_specs=(anywhere,) * 3,
        scratch_shapes=[floats(*whole), floats(3, SIDE, SIDE), floats(SIDE, SIDE), dma((8,)), dma((8,))],
        name="hand_over",
    )(*made)
    return solid.reshape(FIELDS, BASIS, ELEMENTS), ocean, bed


def solution(mesh):
    in_specs = (
        P(None, None, ("gx", "gy")),
        P(None, None, ("gx", "gy")),
        P(None, None, ("gx", "gy")),
        P(("gx", "gy")),
        P(),
        P(),
        P(),
        P(),
        P(),
        P(),
        P(None, ("gx", "gy")),
        P(None, ("gx", "gy")),
        P(("gx", "gy")),
        P(("gx", "gy"), None),
        P(("gx", "gy"), None),
        P(),
        P("gx", "gy"),
        P(None, "gx", "gy"),
        P("gx", "gy"),
    )
    out_specs = (P(None, None, ("gx", "gy")), P(None, "gx", "gy"), P("gx", "gy"))
    return jax.shard_map(
        functools.partial(per_device, mesh.shape["gx"], mesh.shape["gy"]),
        mesh=mesh, in_specs=in_specs, out_specs=out_specs, check_vma=False,
    )
```

```python
import functools

import jax
import jax.numpy as jnp
from jax import lax
from jax.experimental import pallas as pl
from jax.experimental.pallas import tpu as pltpu
from jax.sharding import PartitionSpec as P

MESH = pl.DeviceIdType.MESH
F32 = jnp.float32
BF16 = jnp.bfloat16

FIELDS = 13
BASIS = 56
FACE_BASIS = 21
CAP = 64
ELEMENTS = 256
SIDE = 256
STEPS_DG = 2

step_solid = 0.4
step_ocean = 0.2
depth_floor = 0.5
vertical_field = 6

OFFSETS = [(-1, -1), (-1, 0), (-1, 1), (0, -1), (0, 1), (1, -1), (1, 0), (1, 1)]
ROWS = 320
HALF = ROWS // 2
EXT_X = SIDE + 16
EXT_Y = SIDE + 128


def mm(a, b):
    return jnp.dot(a, b, preferred_element_type=F32)


def mm_nt(a, b):
    return lax.dot_general(a, b, (((1,), (1,)), ((), ())), preferred_element_type=F32)


def halves(x):
    high = x.astype(BF16)
    return high, (x - high.astype(F32)).astype(BF16)


def triple(x):
    high = x.astype(BF16).astype(F32)
    return jnp.concatenate([high, x - high, high], axis=0).astype(BF16)


def one_hot(index_row, rows):
    width = index_row.shape[1]
    index = jnp.broadcast_to(index_row, (16, width)).astype(jnp.int16)
    iota = lax.broadcasted_iota(jnp.int32, (16, width), 0).astype(jnp.int16)
    apart = index - iota
    one, zero = jnp.ones((16, width), BF16), jnp.zeros((16, width), BF16)
    return jnp.concatenate(
        [jnp.where(apart == jnp.int16(16 * tile), one, zero) for tile in range(rows // 16)], axis=0)


def low_lanes(shape):
    return lax.broadcasted_iota(jnp.int32, shape, len(shape) - 1) < 64


def swap_lanes(x):
    return pltpu.roll(x, 64, x.ndim - 1)


def iota2(shape, axis):
    return lax.broadcasted_iota(jnp.int32, shape, axis)


def bits(condition):
    return jnp.where(condition, 1.0, 0.0).astype(BF16)


def lane_triple(w):
    high, low = halves(w)
    k, n = iota2((BASIS, 3 * BASIS), 0), iota2((BASIS, 3 * BASIS), 1)
    return (mm(high, bits((n == k) | (n == k + BASIS))) + mm(low, bits(n == k + 2 * BASIS))).astype(BF16)


def shallow_update(height, mom_x, mom_y, b, extra=None):
    safe = jnp.maximum(height, depth_floor)
    root = lax.rsqrt(safe)
    inv = root * root
    vel_x = mom_x * inv
    vel_y = mom_y * inv
    celerity = safe * root
    cross = mom_x * vel_y
    press = 0.5 * height * height
    n, m = height.shape
    fluxes = (
        (0, n, (mom_x, mom_x * vel_x + press, cross), jnp.abs(vel_x) + celerity),
        (1, m, (mom_y, cross, mom_y * vel_y + press), jnp.abs(vel_y) + celerity))
    state = (height, mom_x, mom_y)
    change = [0.0, 0.0, 0.0]
    for axis, size, flux, speed in fluxes:
        wave = jnp.maximum(speed, pltpu.roll(speed, size - 1, axis))
        for i in range(3):
            face = (flux[i] + pltpu.roll(flux[i], size - 1, axis)) - wave * (
                pltpu.roll(state[i], size - 1, axis) - state[i])
            change[i] = change[i] + (face - pltpu.roll(face, 1, axis))
    half = 0.5 * step_ocean
    slope_x, slope_y = slopes(b)
    return (
        height - half * change[0],
        mom_x - half * (change[1] + height * slope_x),
        mom_y - half * (change[2] + height * slope_y))


def slopes(b):
    n, m = b.shape
    return (
        pltpu.roll(b, n - 1, 0) - pltpu.roll(b, 1, 0),
        pltpu.roll(b, m - 1, 1) - pltpu.roll(b, 1, 1))


def solid_kernel(
    n_gx, n_gy,
    coef, jac, nrm, spd, deriv, stiff, trace_in, lift_in, interp, stars, source, partner, send,
    sea_face, sea_row, sea_base, depth, mom, bottom,
    solid_out, ocean_out, bed_out,
    solid, wave, force_ext, ocean, bed, sea0, tpad, lpad, ipad, spad, dcat, scat, tcat, vcat, lift1, lift2, kron, kron_high, rotate1, rotate2,
    ddt, integral, mixed, table, tsplit, outer, flux, volume, arrived, slot_side,
    hot_send, hot_local, hot_remote, hot_slot, hot_x, hot_y,
    msg, got, corner_msg, corner_got, rate_msg, rate_got,
    u_top, u_bot, u_strip, u_row_got, u_strip_got, u_corner_got,
    f_top, f_bot, f_strip, f_row_got, f_strip_got, f_corner_got,
    load_sem, store_sem, ocean_sem,
    face_send, face_recv, corner_send, corner_recv, rate_send, rate_recv,
    uh_send, uh_recv, fh_send, fh_recv,
):
    gx = lax.axis_index("gx")
    gy = lax.axis_index("gy")
    slots = n_gy * CAP

    def at(dx, dy):
        return (lax.rem(gx + dx + n_gx, n_gx), lax.rem(gy + dy + n_gy, n_gy))

    barrier = pltpu.get_barrier_semaphore()
    peers = [at(dx, dy) for dx, dy in OFFSETS] + [at(0, off) for off in range(2, n_gy - 1)]
    for peer in peers:
        pl.semaphore_signal(barrier, inc=1, device_id=peer, device_id_type=MESH)

    fetched = pltpu.make_async_copy(coef, solid, load_sem.at[3])
    fetched.start()
    loads = [
        pltpu.make_async_copy(depth, sea0.at[0], load_sem.at[0]),
        pltpu.make_async_copy(mom, sea0.at[1:3], load_sem.at[1]),
        pltpu.make_async_copy(bottom, sea0.at[3], load_sem.at[2])]
    for copy in loads:
        copy.start()

    def face_copy(step, k):
        return pltpu.make_async_remote_copy(
            src_ref=msg.at[step, k], dst_ref=got.at[step, 7 - k],
            send_sem=face_send.at[step, k], recv_sem=face_recv.at[step, 7 - k],
            device_id=at(*OFFSETS[k]), device_id_type=MESH)

    def face_arrival(step, k):
        return pltpu.make_async_remote_copy(
            src_ref=msg.at[step, k], dst_ref=got.at[step, k],
            send_sem=face_send.at[step, k], recv_sem=face_recv.at[step, k],
            device_id=at(*OFFSETS[k]), device_id_type=MESH)

    def row_copy(source_ref, target_ref, sends, recvs, off):
        there = lax.rem(gy + off, n_gy)
        return pltpu.make_async_remote_copy(
            src_ref=source_ref.at[there], dst_ref=target_ref.at[gy],
            send_sem=sends.at[off - 1], recv_sem=recvs.at[off - 1],
            device_id=(gx, there), device_id_type=MESH)

    def row_arrival(source_ref, target_ref, sends, recvs, off):
        origin = lax.rem(gy - off + n_gy, n_gy)
        return pltpu.make_async_remote_copy(
            src_ref=source_ref.at[origin], dst_ref=target_ref.at[origin],
            send_sem=sends.at[off - 1], recv_sem=recvs.at[off - 1],
            device_id=(gx, origin), device_id_type=MESH)

    def halo_copies(top, bot, strip, rows_got, strips_got, corners_got, sends, recvs):
        sources = [
            top.at[:, :, 0:128], top, top.at[:, :, 128:256], strip, strip,
            bot.at[:, :, 0:128], bot, bot.at[:, :, 128:256]]
        targets = [
            corners_got.at[0], rows_got.at[0], corners_got.at[1], strips_got.at[0],
            strips_got.at[1], corners_got.at[2], rows_got.at[1], corners_got.at[3]]
        return [
            pltpu.make_async_remote_copy(
                src_ref=sources[k], dst_ref=targets[k],
                send_sem=sends.at[k], recv_sem=recvs.at[k],
                device_id=at(*OFFSETS[k]), device_id_type=MESH)
            for k in range(8)]

    def by_block(ref):
        tiles = ref[...].reshape(3, 7, 8, BASIS)
        return jnp.concatenate([tiles[d, block] for block in range(7) for d in range(3)], axis=0)

    dcat[...] = lane_triple(by_block(deriv))
    scat[...] = lane_triple(by_block(stiff))
    tpad[...] = jnp.zeros(tpad.shape, F32)
    lpad[...] = jnp.zeros(lpad.shape, F32)
    ipad[...] = jnp.zeros(ipad.shape, F32)
    spad[...] = jnp.zeros(spad.shape, F32)
    ipad[:, 0:FACE_BASIS] = interp[...]
    for face in range(4):
        tpad[face, 0:FACE_BASIS, :] = trace_in[:, face, :]
        lpad[face, 0:FACE_BASIS, :] = lift_in[:, face, :]
    for c in range(3):
        spad[c, 0:FIELDS, 0:FIELDS] = stars[c]
    spad[3, 0:FIELDS, 0:FIELDS] = source[...]
    tcat[...] = lane_triple(tpad[...].reshape(96, BASIS))

    repeat = bits(jnp.right_shift(iota2((104, 16), 0), 3) == iota2((104, 16), 1))
    tall = [[mm(repeat, part).astype(BF16) for part in halves(spad[c])] for c in range(4)]

    def spread(part, columns, starts):
        total = jnp.zeros((104, columns), F32)
        k = iota2((16, columns), 0)
        n = jnp.right_shift(iota2((16, columns), 1), 3)
        for c, start in starts:
            total = total + mm(tall[c][part], bits((n == k + start) & (k < FIELDS)))
        same = jnp.bitwise_and(iota2((104, columns), 0), 7) == jnp.bitwise_and(iota2((104, columns), 1), 7)
        return jnp.where(same, total, 0.0)

    every = [(c, c * FIELDS) for c in range(4)]
    def woven(parts):
        return jnp.concatenate([part[8 * g:8 * g + 8] for g in range(FIELDS) for part in parts], axis=0).astype(BF16)

    kron_parts = [spread(0, 416, every), spread(1, 416, every)]
    kron[...] = woven(kron_parts)
    kron_high[...] = kron_parts[0].astype(BF16)

    def one_hot_face_sends():
        for pair in range(4):
            index = jnp.concatenate([send[2 * pair:2 * pair + 1, :], send[2 * pair + 1:2 * pair + 2, :]], axis=1)
            hot_send[:, pair * 128:(pair + 1) * 128] = one_hot(index, 4 * ELEMENTS)

    def star(x, groups):
        high, low = halves(x)
        both = mm(kron[:, 0:8 * groups], high).reshape(FIELDS, 2, 8, ELEMENTS)
        return both[:, 0] + both[:, 1] + mm(kron_high[:, 0:8 * groups], low).reshape(FIELDS, 8, ELEMENTS)

    def turn(total):
        high = total.astype(BF16).astype(F32)
        both = jnp.concatenate([high, total - high], axis=0).astype(BF16)
        return mm(rotate1[...], both) + mm(rotate2[...], both[0:104])

    def directional(source_ref, weights, with_source, store):
        for h in range(FIELDS):
            q = source_ref[h].reshape(BASIS, ELEMENTS)
            spatial = mm(weights[...], triple(q))
            for block in range(7):
                parts = [spatial[24 * block + 8 * d:24 * block + 8 * d + 8] for d in range(3)]
                for c in range(3):
                    mixed[block, c * FIELDS + h] = (
                        jac[0, c:c + 1, :] * parts[0] + jac[1, c:c + 1, :] * parts[1] + jac[2, c:c + 1, :] * parts[2])
            if with_source:
                mixed[:, 3 * FIELDS + h] = source_ref[h]
        groups = 4 * FIELDS if with_source else 3 * FIELDS
        for block in range(7):
            result = star(mixed[block, 0:groups].reshape(8 * groups, ELEMENTS), groups)
            store(block, result)

    def later_matrices():
        rotate1[...] = woven([spread(0, 208, [(c, 0), (c, FIELDS)]) for c in range(3)])
        rotate2[...] = woven([spread(1, 104, [(c, 0)]) for c in range(3)])
        across = [jnp.concatenate([0.5 * nrm[c, face:face + 1, :] for face in range(4)], axis=1) for c in range(3)]
        across += [jnp.concatenate([0.5 * spd[...]] * 4, axis=1)] * 5
        sides = jnp.concatenate([jnp.broadcast_to(row, (1, 4 * ELEMENTS)) for row in across], axis=0)
        high = sides.astype(BF16).astype(F32)
        found = mm(jnp.concatenate([high, sides - high], axis=0).astype(BF16), hot_send[...])
        slot_side[...] = found[0:8] + found[8:16]
        first = jnp.zeros((BASIS, 192), F32)
        second = jnp.zeros((BASIS, 96), F32)
        for face in range(4):
            same = bits(iota2((BASIS, BASIS), 0) == iota2((BASIS, BASIS), 1))
            high, low = [mm_nt(same, part).astype(BF16) for part in halves(lpad[face])]
            k, n = iota2((24, 192), 0) + 24 * face, iota2((24, 192), 1)
            first = first + mm(high, bits((n == k) | (n == k + 96)))
            second = second + mm(low, bits(iota2((24, 96), 1) == iota2((24, 96), 0) + 24 * face))
        lift1[...] = first.astype(BF16)
        lift2[...] = second.astype(BF16)
        i_high, i_low = halves(ipad[...])
        points = []
        for face in range(4):
            t_high, t_low = halves(tpad[face])
            points.append(mm(i_high, t_high) + mm(i_high, t_low) + mm(i_low, t_high))
        vcat[...] = lane_triple(jnp.concatenate(points, axis=0))

    pick_row = iota2((8, SIDE), 0)
    edge = bits(iota2((8, SIDE), 1) == jnp.where(pick_row < 4, pick_row, pick_row + (SIDE - 8)))

    def strip_of(x):
        high, low = halves(x)
        rest = (x - high.astype(F32) - low.astype(F32)).astype(BF16)
        return mm_nt(edge, high) + mm_nt(edge, low) + mm_nt(edge, rest)

    uh = halo_copies(u_top, u_bot, u_strip, u_row_got, u_strip_got, u_corner_got, uh_send, uh_recv)

    def send_inputs():
        for copy in loads:
            copy.wait()
        for field in range(4):
            u_top[field] = sea0[field, 0:8, :]
            u_bot[field] = sea0[field, SIDE - 8:SIDE, :]
            u_strip[field] = strip_of(sea0[field])
        rows = sea_row[...]
        hits = jnp.where(iota2((n_gy, ELEMENTS), 0) == rows, 1.0, 0.0)
        tri = bits(iota2((ELEMENTS, ELEMENTS), 0) < iota2((ELEMENTS, ELEMENTS), 1))
        before = mm(hits.astype(BF16), tri)
        slot = jnp.sum(before * hits, axis=0, keepdims=True).astype(jnp.int32)
        placed = one_hot(rows * CAP + slot, slots)
        line = iota2((8, ELEMENTS), 0)
        values = jnp.where(line == 0, sea_face[...], jnp.where(
            line == 1, sea_base[0:1, :], sea_base[1:2, :])).astype(F32) + 1.0
        high, low = halves(values)
        found = mm_nt(high, placed) + mm_nt(low, placed)
        for pair in range(n_gy // 2):
            block = found[:, pair * 128:(pair + 1) * 128]
            corner_msg[2 * pair] = block
            corner_msg[2 * pair + 1] = swap_lanes(block)
        for copy in uh:
            copy.start()
        for off in range(1, n_gy):
            row_copy(corner_msg, corner_got, corner_send, corner_recv, off).start()
        corner_got[gy] = corner_msg[gy]
        return found[0:1, :].astype(jnp.int32) - 1

    side8 = low_lanes((8, 128))

    iota16 = iota2((16, 128), 0).astype(jnp.int16)
    one16, zero16 = jnp.ones((16, 128), BF16), jnp.zeros((16, 128), BF16)

    def position_tables():
        for off in range(1, n_gy):
            row_arrival(corner_msg, corner_got, corner_send, corner_recv, off).wait_recv()
        for pair in range(n_gy // 2):
            corner = jnp.where(side8, corner_got[2 * pair], swap_lanes(corner_got[2 * pair + 1])).astype(jnp.int32)
            for hot, line in ((hot_x, 1), (hot_y, 2)):
                apart = jnp.broadcast_to(corner[line:line + 1, :] - 1, (16, 128)).astype(jnp.int16) - iota16
                for tile in range(SIDE // 16):
                    for j in range(4):
                        base = pair * 512 + j * 128
                        hot[16 * tile:16 * tile + 16, base:base + 128] = jnp.where(
                            apart == jnp.int16(16 * tile - j), one16, zero16)

    up_in = gx > 0
    down_in = gx < n_gx - 1
    left_in = gy > 0
    right_in = gy < n_gy - 1

    def place_halo(target, rows_got, strips_got, corners_got, field):
        target[0:8, 0:SIDE] = jnp.where(up_in, rows_got[1, field], 0.0)
        target[8 + SIDE:EXT_X, 0:SIDE] = jnp.where(down_in, rows_got[0, field], 0.0)
        strip = jnp.concatenate([
            jnp.where(right_in, strips_got[0, field], 0.0), jnp.zeros((112, SIDE), F32),
            jnp.where(left_in, strips_got[1, field], 0.0)], axis=0)
        target[8:8 + SIDE, SIDE:EXT_Y] = jnp.transpose(strip)
        target[0:8, SIDE:EXT_Y] = jnp.where(
            side8, jnp.where(up_in & right_in, corners_got[2, field], 0.0),
            jnp.where(up_in & left_in, corners_got[3, field], 0.0))
        target[8 + SIDE:EXT_X, SIDE:EXT_Y] = jnp.where(
            side8, jnp.where(down_in & right_in, corners_got[0, field], 0.0),
            jnp.where(down_in & left_in, corners_got[1, field], 0.0))

    def ocean_first_step():
        for copy in uh:
            copy.wait_recv()
        for field in range(4):
            row = (0, 5, 6, 1)[field]
            wave[row, 8:8 + SIDE, 0:SIDE] = sea0[field]
            place_halo(wave.at[row], u_row_got, u_strip_got, u_corner_got, field)

        def part(begin, rows, inner_from, inner_to):
            span = pl.ds(begin, rows)
            result = shallow_update(wave[0, span, :], wave[5, span, :], wave[6, span, :], wave[1, span, :])
            x = begin + iota2((rows, EXT_Y), 0)
            y = iota2((rows, EXT_Y), 1)
            out = ((x < 8) & (gx == 0)) | ((x >= 8 + SIDE) & (gx == n_gx - 1))
            out = out | ((y >= SIDE) & (y < SIDE + 64) & (gy == n_gy - 1)) | ((y >= SIDE + 64) & (gy == 0))
            for i in range(3):
                wave[2 + i, pl.ds(begin + inner_from, inner_to - inner_from), :] = jnp.where(
                    out, 0.0, result[i])[inner_from:inner_to]

        @pl.loop(0, SIDE // SLAB)
        def _(s):
            part(pl.multiple_of(s * SLAB, 8), SLAB + 16, 8, SLAB + 8)
        part(0, 16, 0, 8)
        part(EXT_X - 16, 16, 8, 16)

    first_factor = step_solid * step_solid / 2
    second_factor = first_factor * step_solid / 3
    table[ROWS // 8 - 1] = jnp.zeros((8, 4 * ELEMENTS), F32)

    fetched.wait()
    for step in range(STEPS_DG):
        state = solid

        def store_first(block, value):
            ddt[:, block] = value
        directional(state, dcat, True, store_first)

        def store_second(block, value):
            integral[:, block] = step_solid * state[:, block] - first_factor * ddt[:, block] + second_factor * value
        directional(ddt, dcat, True, store_second)

        if step == 0:
            one_hot_face_sends()
        for g in range(FIELDS):
            trace = mm(tcat[...], triple(integral[g].reshape(BASIS, ELEMENTS)))
            for face in range(4):
                table[3 * g:3 * g + 3, :, face * ELEMENTS:(face + 1) * ELEMENTS] = (
                    trace[face * 24:(face + 1) * 24].reshape(3, 8, ELEMENTS))
        for tile in range(ROWS // 16):
            high, low = halves(table[2 * tile:2 * tile + 2].reshape(16, 4 * ELEMENTS))
            tsplit[32 * tile:32 * tile + 16] = high
            tsplit[32 * tile + 16:32 * tile + 32] = low

        low_side = low_lanes((HALF, 128))
        middle = 2 * ELEMENTS
        for half in range(2):
            lanes = slice(half * 256, half * 256 + 256)
            picked = (
                mm(tsplit[:, 0:middle], hot_send[0:middle, lanes]) + mm(tsplit[:, middle:], hot_send[middle:, lanes])
            ).reshape(ROWS // 16, 2, 16, 256)
            picked = (picked[:, 0] + picked[:, 1]).reshape(ROWS, 256)
            for pair in range(2):
                block = picked[:, pair * 128:(pair + 1) * 128]
                top, bot = block[0:HALF], block[HALF:ROWS]
                k = 4 * half + 2 * pair
                msg[step, k] = jnp.where(low_side, top, swap_lanes(bot))
                msg[step, k + 1] = jnp.where(low_side, swap_lanes(top), bot)
            if step == 0 and half == 0:
                pl.semaphore_wait(barrier, len(peers))
            for k in range(4 * half, 4 * half + 4):
                face_copy(step, k).start()

        if step == 0:
            slot_code = send_inputs()
            for face in range(4):
                code = partner[face:face + 1, :]
                cols = slice(face * ELEMENTS, (face + 1) * ELEMENTS)
                hot_local[:, cols] = one_hot(code, 4 * ELEMENTS)
                hot_remote[:, cols] = one_hot(code - 4 * ELEMENTS, 8 * 64)
            later_matrices()
        else:
            hot_slot[...] = one_hot(slot_code, 4 * ELEMENTS)
        for face in range(4):
            cols = slice(face * ELEMENTS, (face + 1) * ELEMENTS)
            local = mm(tsplit[...], hot_local[:, cols])
            local = local.reshape(ROWS // 16, 2, 16, ELEMENTS)
            outer[:, :, cols] = (local[:, 0] + local[:, 1]).reshape(ROWS // 8, 8, ELEMENTS)

        for face in range(4):
            cols = slice(face * ELEMENTS, (face + 1) * ELEMENTS)
            normal = [0.5 * nrm[c, face:face + 1, :] for c in range(3)]
            speed = 0.5 * spd[...]
            for block in range(3):
                ids = [3 * g + block for g in range(FIELDS)]
                turned = turn(jnp.concatenate([table[n, :, cols] + outer[n, :, cols] for n in ids], axis=0))
                for g in range(FIELDS):
                    value = speed * (table[ids[g], :, cols] - outer[ids[g], :, cols])
                    for c in range(3):
                        value = value + normal[c] * turned[24 * g + 8 * c:24 * g + 8 * c + 8]
                    flux[g, face, block] = value

        def store_volume(block, value):
            volume[:, block] = value
        directional(integral, scat, False, store_volume)
        if step == 1:
            position_tables()

        for k in range(8):
            face_arrival(step, k).wait_recv()
        for pair in range(4):
            a, b = got[step, 2 * pair], got[step, 2 * pair + 1]
            cols = slice(pair * 128, (pair + 1) * 128)
            arrived[0:HALF // 8, :, cols] = jnp.where(low_side, a, swap_lanes(b)).reshape(HALF // 8, 8, 128)
            arrived[HALF // 8:, :, cols] = jnp.where(low_side, swap_lanes(a), b).reshape(HALF // 8, 8, 128)
        for side in range(2):
            lanes = slice(side * 256, side * 256 + 256)
            normal = [slot_side[c:c + 1, lanes] for c in range(3)]
            speed = slot_side[3:4, lanes]
            for block in range(3):
                ids = [3 * g + block for g in range(FIELDS)]
                turned = turn(jnp.concatenate([arrived[n, :, lanes] for n in ids], axis=0))
                for g in range(FIELDS):
                    value = -speed * arrived[ids[g], :, lanes]
                    for c in range(3):
                        value = value + normal[c] * turned[24 * g + 8 * c:24 * g + 8 * c + 8]
                    arrived[ids[g], :, lanes] = value
        for tile in range(ROWS // 16):
            high, low = halves(arrived[2 * tile:2 * tile + 2].reshape(16, 512))
            tsplit[32 * tile:32 * tile + 16, 0:512] = high
            tsplit[32 * tile + 16:32 * tile + 32, 0:512] = low
        for face in range(4):
            cols = slice(face * ELEMENTS, (face + 1) * ELEMENTS)
            remote = mm(tsplit[:, 0:512], hot_remote[:, cols]).reshape(ROWS // 16, 2, 16, ELEMENTS)
            remote = (remote[:, 0] + remote[:, 1]).reshape(ROWS // 8, 8, ELEMENTS)
            for g in range(FIELDS):
                for block in range(3):
                    flux[g, face, block] = flux[g, face, block] + remote[3 * g + block]
        for g in range(FIELDS):
            f = flux[g].reshape(96, ELEMENTS)
            high = f.astype(BF16).astype(F32)
            both = jnp.concatenate([high, f - high], axis=0).astype(BF16)
            lifted = mm(lift1[...], both) + mm(lift2[...], both[0:96])
            solid[g] = state[g] + volume[g] - lifted.reshape(7, 8, ELEMENTS)

    point = mm(vcat[...], triple(solid[vertical_field].reshape(BASIS, ELEMENTS)))
    points = jnp.concatenate([point[16 * f:16 * f + 16] for f in range(4)], axis=1)
    high = points.astype(BF16).astype(F32)
    both = jnp.concatenate([high, points - high], axis=0).astype(BF16)
    rates = mm(both, hot_slot[...])
    rates = rates[0:16] + rates[16:32]
    for pair in range(n_gy // 2):
        a = rates[0:8, pair * 128:(pair + 1) * 128]
        b = rates[8:16, pair * 128:(pair + 1) * 128]
        rate_msg[2 * pair] = jnp.where(side8, a, swap_lanes(b))
        rate_msg[2 * pair + 1] = jnp.where(side8, swap_lanes(a), b)
    for off in range(1, n_gy):
        row_copy(rate_msg, rate_got, rate_send, rate_recv, off).start()
    rate_got[gy] = rate_msg[gy]
    saved = pltpu.make_async_copy(solid, solid_out, store_sem.at[0])
    saved.start()

    ocean_first_step()

    for off in range(1, n_gy):
        row_arrival(rate_msg, rate_got, rate_send, rate_recv, off).wait_recv()
    edge_row = jnp.where(iota2((16, 128), 0) < 8, iota2((16, 128), 0), iota2((16, 128), 0) + (SIDE - 16))
    edge_col = jnp.where(iota2((8, 128), 0) < 4, iota2((8, 128), 0), iota2((8, 128), 0) + (SIDE - 8))
    pairs = []
    for pair in range(n_gy // 2):
        corner = jnp.where(side8, corner_got[2 * pair], swap_lanes(corner_got[2 * pair + 1])).astype(jnp.int32)
        a, b = rate_got[2 * pair], rate_got[2 * pair + 1]
        first = jnp.where(side8, a, swap_lanes(b))
        second = jnp.where(side8, swap_lanes(a), b)
        rate = [[first[j:j + 1] for j in range(4)], [first[4 + j:5 + j] for j in range(4)],
                [second[j:j + 1] for j in range(4)], [second[4 + j:5 + j] for j in range(4)]]
        pairs.append((corner, rate))

    def chosen(masks, values):
        return jnp.where(masks[0], values[0], jnp.where(masks[1], values[1], jnp.where(
            masks[2], values[2], jnp.where(masks[3], values[3], 0.0))))

    row_parts = [[None] * len(pairs) for _ in range(4)]
    col_parts = [[None] * len(pairs) for _ in range(4)]
    for index, (corner, rate) in enumerate(pairs):
        apart_x = edge_row + 1 - corner[1:2, :]
        apart_y = edge_col + 1 - corner[2:3, :]
        masks_x = [apart_x == i for i in range(4)]
        masks_y = [apart_y == i for i in range(4)]
        for j in range(4):
            row_parts[j][index] = chosen(masks_x, [rate[i][j] for i in range(4)])
            col_parts[j][index] = chosen(masks_y, [rate[j][i] for i in range(4)])

    def summed(parts, table_ref):
        stacked = []
        for row in parts:
            whole = jnp.concatenate(row, axis=1)
            high = whole.astype(BF16).astype(F32)
            stacked += [high, whole - high]
        stacked = jnp.concatenate(stacked, axis=0).astype(BF16)
        places = jnp.concatenate([table_ref[:, pair * 512:pair * 512 + 128] for pair in range(n_gy // 2)], axis=1)
        result = mm_nt(stacked, places)
        count = parts[0][0].shape[0]
        total = result[0:count] + result[count:2 * count]
        for shift in range(1, 4):
            begin = 2 * count * shift
            moved = result[begin:begin + count] + result[begin + count:begin + 2 * count]
            total = total + pltpu.roll(moved, shift, 1)
        return total

    edge_rows = summed(row_parts, hot_y)
    f_top[0] = edge_rows[0:8]
    f_bot[0] = edge_rows[8:16]
    f_strip[0] = summed(col_parts, hot_x)
    fh = halo_copies(f_top, f_bot, f_strip, f_row_got, f_strip_got, f_corner_got, fh_send, fh_recv)
    for copy in fh:
        copy.start()

    force_ext[8:8 + SIDE, 0:SIDE] = jnp.zeros((SIDE, SIDE), F32)

    @pl.loop(0, n_gy // 2, unroll=2)
    def _(pair):
        corner = jnp.where(side8, corner_got[2 * pair], swap_lanes(corner_got[2 * pair + 1])).astype(jnp.int32)
        a, b = rate_got[2 * pair], rate_got[2 * pair + 1]
        first = jnp.where(side8, a, swap_lanes(b))
        second = jnp.where(side8, swap_lanes(a), b)
        wide = []
        for line in [first[i:i + 1] for i in range(8)] + [second[i:i + 1] for i in range(8)]:
            wide.append(halves(jnp.broadcast_to(line, (16, 128))))
        apart = jnp.broadcast_to(corner[1:2, :] - 1, (16, 128)).astype(jnp.int16) - iota16
        columns = [[] for _ in range(4)]
        for tile in range(SIDE // 16):
            masks = [apart == jnp.int16(16 * tile - i) for i in range(4)]
            for j in range(4):
                for part in range(2):
                    value = zero16
                    for i in range(4):
                        value = jnp.where(masks[i], wide[4 * i + j][part], value)
                    columns[j].append(value)
        total = jnp.zeros((2 * SIDE, SIDE), F32)
        for half in range(2):
            table_part = hot_y[:, pl.ds(pl.multiple_of(pair * 512 + half * 256, 256), 256)]
            left = jnp.concatenate([jnp.concatenate(columns[2 * half + j], axis=0) for j in range(2)], axis=1)
            total = total + mm_nt(left, table_part)
        total = total.reshape(SIDE // 16, 2, 16, SIDE)
        total = (total[:, 0] + total[:, 1]).reshape(SIDE, SIDE)
        force_ext[8:8 + SIDE, 0:SIDE] = force_ext[8:8 + SIDE, 0:SIDE] + total

    for copy in fh:
        copy.wait_recv()
    place_halo(force_ext, f_row_got, f_strip_got, f_corner_got, 0)

    stores = []
    for piece in range(SIDE // SLAB):
        begin = piece * SLAB
        span = slice(begin, begin + SLAB + 16)
        inner = slice(begin, begin + SLAB)
        lift = force_ext[span, :]
        depth_0 = wave[0, span, :]
        slope_x, slope_y = slopes(lift)
        scale = 0.5 * step_ocean * step_ocean
        mom_x = wave[3, span, :] - scale * (depth_0 * slope_x)
        mom_y = wave[4, span, :] - scale * (depth_0 * slope_y)
        b = wave[1, span, :] + (2 * step_ocean) * lift
        result = shallow_update(wave[2, span, :], mom_x, mom_y, b)
        for i in range(3):
            ocean[i, inner, :] = result[i][8:SLAB + 8, 0:SIDE]
        bed[inner, :] = b[8:SLAB + 8, 0:SIDE]
        stores.append(pltpu.make_async_copy(ocean.at[:, inner], ocean_out.at[:, inner], ocean_sem.at[0, piece]))
        stores.append(pltpu.make_async_copy(bed.at[inner], bed_out.at[inner], ocean_sem.at[1, piece]))
        for copy in stores[-2:]:
            copy.start()

    saved.wait()
    for copy in stores:
        copy.wait()
    for copy in uh + fh:
        copy.wait_send()
    for off in range(1, n_gy):
        row_copy(corner_msg, corner_got, corner_send, corner_recv, off).wait_send()
        row_copy(rate_msg, rate_got, rate_send, rate_recv, off).wait_send()
    for step in range(STEPS_DG):
        for k in range(8):
            face_copy(step, k).wait_send()


SLAB = 64


def hand_over(solid_in, ocean_in, bed_in, solid_out, ocean_out, bed_out, solid, ocean, bed, in_sems, out_sems):
    parts = [(solid_in.at[g:g + 4], solid.at[g:g + 4], solid_out.at[g:g + 4]) for g in range(0, 12, 4)]
    parts += [(solid_in.at[12:13], solid.at[12:13], solid_out.at[12:13])]
    parts += [(ocean_in.at[i], ocean.at[i], ocean_out.at[i]) for i in range(3)]
    parts += [(bed_in, bed, bed_out)]
    fetches = [pltpu.make_async_copy(part[0], part[1], in_sems.at[n]) for n, part in enumerate(parts)]
    stores = [pltpu.make_async_copy(part[1], part[2], out_sems.at[n]) for n, part in enumerate(parts)]
    for copy in fetches:
        copy.start()
    for fetch, store in zip(fetches, stores):
        fetch.wait()
        store.start()
    for copy in stores:
        copy.wait()


def per_device(
    n_gx, n_gy,
    coefficients, jacobian, face_normals, wave_speed, star_mats, deriv_mats, stiff_mats, source_mat,
    trace_mats, lift_mats, face_partner, send_faces, sea_face, sea_row, sea_base, interp_mat,
    water_depth, momentum, bottom,
):
    vm = pl.BlockSpec(memory_space=pltpu.VMEM)
    anywhere = pl.BlockSpec(memory_space=pl.ANY)
    slots = n_gy * CAP
    whole = (FIELDS, 7, 8, ELEMENTS)
    floats = lambda *shape: pltpu.VMEM(shape, F32)
    shorts = lambda *shape: pltpu.VMEM(shape, BF16)
    dma = pltpu.SemaphoreType.DMA
    scratch = [
        floats(*whole),
        floats(7, EXT_X, EXT_Y),
        floats(EXT_X, EXT_Y),
        floats(3, SIDE, SIDE),
        floats(SIDE, SIDE),
        floats(4, SIDE, SIDE),
        floats(4, 24, BASIS),
        floats(4, 24, BASIS),
        floats(16, 24),
        floats(4, 16, 16),
        shorts(168, 168),
        shorts(168, 168),
        shorts(96, 168),
        shorts(64, 168),
        shorts(56, 192),
        shorts(56, 96),
        shorts(208, 416),
        shorts(104, 416),
        shorts(312, 208),
        shorts(312, 104),
        floats(*whole),
        floats(*whole),
        floats(7, 4 * FIELDS, 8, ELEMENTS),
        floats(ROWS // 8, 8, 4 * ELEMENTS),
        shorts(2 * ROWS, 4 * ELEMENTS),
        floats(ROWS // 8, 8, 4 * ELEMENTS),
        floats(FIELDS, 4, 3, 8, ELEMENTS),
        floats(*whole),
        floats(ROWS // 8, 8, 512),
        floats(8, 512),
        shorts(4 * ELEMENTS, 512),
        shorts(4 * ELEMENTS, 4 * ELEMENTS),
        shorts(512, 4 * ELEMENTS),
        shorts(4 * ELEMENTS, slots),
        shorts(SIDE, 4 * slots),
        shorts(SIDE, 4 * slots),
        floats(STEPS_DG, 8, HALF, 128),
        floats(STEPS_DG, 8, HALF, 128),
        floats(n_gy, 8, 128),
        floats(n_gy, 8, 128),
        floats(n_gy, 8, 128),
        floats(n_gy, 8, 128),
        floats(4, 8, SIDE),
        floats(4, 8, SIDE),
        floats(4, 8, SIDE),
        floats(2, 4, 8, SIDE),
        floats(2, 4, 8, SIDE),
        floats(4, 4, 8, 128),
        floats(1, 8, SIDE),
        floats(1, 8, SIDE),
        floats(1, 8, SIDE),
        floats(2, 1, 8, SIDE),
        floats(2, 1, 8, SIDE),
        floats(4, 1, 8, 128),
        dma((4,)), dma((2,)), dma((2, SIDE // SLAB)),
        dma((STEPS_DG, 8)), dma((STEPS_DG, 8)),
        dma((n_gy - 1,)), dma((n_gy - 1,)), dma((n_gy - 1,)), dma((n_gy - 1,)),
        dma((8,)), dma((8,)), dma((8,)), dma((8,)),
    ]
    results = (
        jax.ShapeDtypeStruct(whole, F32),
        jax.ShapeDtypeStruct((3, SIDE, SIDE), F32),
        jax.ShapeDtypeStruct((SIDE, SIDE), F32))
    made = pl.pallas_call(
        functools.partial(solid_kernel, n_gx, n_gy),
        out_shape=results,
        in_specs=[anywhere] + [vm] * 15 + [anywhere] * 3,
        out_specs=(anywhere,) * 3,
        scratch_shapes=scratch,
        compiler_params=pltpu.CompilerParams(
            collective_id=0, has_side_effects=True, vmem_limit_bytes=60 * 1024 * 1024),
        name="solid",
    )(
        coefficients.reshape(whole), jacobian, face_normals.transpose(1, 0, 2), wave_speed.reshape(1, ELEMENTS),
        deriv_mats, stiff_mats, trace_mats.transpose(1, 0, 2), lift_mats.transpose(2, 0, 1), interp_mat, star_mats, source_mat, face_partner, send_faces,
        sea_face.reshape(1, ELEMENTS), sea_row.reshape(1, ELEMENTS), sea_base.T,
        water_depth, momentum, bottom)
    solid, ocean, bed = pl.pallas_call(
        hand_over,
        out_shape=results,
        in_specs=[anywhere] * 3,
        out_specs=(anywhere,) * 3,
        scratch_shapes=[floats(*whole), floats(3, SIDE, SIDE), floats(SIDE, SIDE), dma((8,)), dma((8,))],
        name="hand_over",
    )(*made)
    return solid.reshape(FIELDS, BASIS, ELEMENTS), ocean, bed


def solution(mesh):
    in_specs = (
        P(None, None, ("gx", "gy")),
        P(None, None, ("gx", "gy")),
        P(None, None, ("gx", "gy")),
        P(("gx", "gy")),
        P(),
        P(),
        P(),
        P(),
        P(),
        P(),
        P(None, ("gx", "gy")),
        P(None, ("gx", "gy")),
        P(("gx", "gy")),
        P(("gx", "gy"), None),
        P(("gx", "gy"), None),
        P(),
        P("gx", "gy"),
        P(None, "gx", "gy"),
        P("gx", "gy"),
    )
    out_specs = (P(None, None, ("gx", "gy")), P(None, "gx", "gy"), P("gx", "gy"))
    return jax.shard_map(
        functools.partial(per_device, mesh.shape["gx"], mesh.shape["gy"]),
        mesh=mesh, in_specs=in_specs, out_specs=out_specs, check_vma=False,
    )
```

```python
import functools

import jax
import jax.numpy as jnp
from jax import lax
from jax.experimental import pallas as pl
from jax.experimental.pallas import tpu as pltpu
from jax.sharding import PartitionSpec as P

MESH = pl.DeviceIdType.MESH
F32 = jnp.float32
BF16 = jnp.bfloat16

FIELDS = 13
BASIS = 56
FACE_BASIS = 21
CAP = 64
ELEMENTS = 256
SIDE = 256
STEPS_DG = 2

step_solid = 0.4
step_ocean = 0.2
depth_floor = 0.5
vertical_field = 6

OFFSETS = [(-1, -1), (-1, 0), (-1, 1), (0, -1), (0, 1), (1, -1), (1, 0), (1, 1)]
ROWS = 320
HALF = ROWS // 2
EXT_X = SIDE + 16
EXT_Y = SIDE + 128


def mm(a, b):
    return jnp.dot(a, b, preferred_element_type=F32)


def mm_nt(a, b):
    return lax.dot_general(a, b, (((1,), (1,)), ((), ())), preferred_element_type=F32)


def halves(x):
    high = x.astype(BF16)
    return high, (x - high.astype(F32)).astype(BF16)


def triple(x):
    high = x.astype(BF16).astype(F32)
    return jnp.concatenate([high, x - high, high], axis=0).astype(BF16)


def one_hot(index_row, rows):
    width = index_row.shape[1]
    index = jnp.broadcast_to(index_row, (16, width)).astype(jnp.int16)
    iota = lax.broadcasted_iota(jnp.int32, (16, width), 0).astype(jnp.int16)
    apart = index - iota
    one, zero = jnp.ones((16, width), BF16), jnp.zeros((16, width), BF16)
    return jnp.concatenate(
        [jnp.where(apart == jnp.int16(16 * tile), one, zero) for tile in range(rows // 16)], axis=0)


def low_lanes(shape):
    return lax.broadcasted_iota(jnp.int32, shape, len(shape) - 1) < 64


def swap_lanes(x):
    return pltpu.roll(x, 64, x.ndim - 1)


def iota2(shape, axis):
    return lax.broadcasted_iota(jnp.int32, shape, axis)


def bits(condition):
    return jnp.where(condition, 1.0, 0.0).astype(BF16)


def lane_triple(w):
    high, low = halves(w)
    k, n = iota2((BASIS, 3 * BASIS), 0), iota2((BASIS, 3 * BASIS), 1)
    return (mm(high, bits((n == k) | (n == k + BASIS))) + mm(low, bits(n == k + 2 * BASIS))).astype(BF16)


def shallow_update(height, mom_x, mom_y, b, extra=None):
    safe = jnp.maximum(height, depth_floor)
    root = lax.rsqrt(safe)
    inv = root * root
    vel_x = mom_x * inv
    vel_y = mom_y * inv
    celerity = safe * root
    cross = mom_x * vel_y
    press = 0.5 * height * height
    n, m = height.shape
    fluxes = (
        (0, n, (mom_x, mom_x * vel_x + press, cross), jnp.abs(vel_x) + celerity),
        (1, m, (mom_y, cross, mom_y * vel_y + press), jnp.abs(vel_y) + celerity))
    state = (height, mom_x, mom_y)
    change = [0.0, 0.0, 0.0]
    for axis, size, flux, speed in fluxes:
        wave = jnp.maximum(speed, pltpu.roll(speed, size - 1, axis))
        for i in range(3):
            face = (flux[i] + pltpu.roll(flux[i], size - 1, axis)) - wave * (
                pltpu.roll(state[i], size - 1, axis) - state[i])
            change[i] = change[i] + (face - pltpu.roll(face, 1, axis))
    half = 0.5 * step_ocean
    slope_x, slope_y = slopes(b)
    return (
        height - half * change[0],
        mom_x - half * (change[1] + height * slope_x),
        mom_y - half * (change[2] + height * slope_y))


def slopes(b):
    n, m = b.shape
    return (
        pltpu.roll(b, n - 1, 0) - pltpu.roll(b, 1, 0),
        pltpu.roll(b, m - 1, 1) - pltpu.roll(b, 1, 1))


def solid_kernel(
    n_gx, n_gy,
    coef, jac, nrm, spd, deriv, stiff, trace_in, lift_in, interp, stars, source, partner, send,
    sea_face, sea_row, sea_base, depth, mom, bottom,
    solid_out, ocean_out, bed_out,
    solid, wave, force_ext, ocean, bed, sea0, tpad, lpad, ipad, spad, dcat, scat, tcat, vcat, lift1, lift2, kron, kron_high, rotate1, rotate2,
    ddt, integral, mixed, table, tsplit, outer, flux, volume, arrived, slot_side,
    hot_send, hot_local, hot_remote, hot_slot, hot_x, hot_y,
    msg, got, corner_msg, corner_got, rate_msg, rate_got,
    u_top, u_bot, u_strip, u_row_got, u_strip_got, u_corner_got,
    f_top, f_bot, f_strip, f_row_got, f_strip_got, f_corner_got,
    load_sem, store_sem, ocean_sem,
    face_send, face_recv, corner_send, corner_recv, rate_send, rate_recv,
    uh_send, uh_recv, fh_send, fh_recv,
):
    gx = lax.axis_index("gx")
    gy = lax.axis_index("gy")
    slots = n_gy * CAP

    def at(dx, dy):
        return (lax.rem(gx + dx + n_gx, n_gx), lax.rem(gy + dy + n_gy, n_gy))

    barrier = pltpu.get_barrier_semaphore()
    peers = [at(dx, dy) for dx, dy in OFFSETS] + [at(0, off) for off in range(2, n_gy - 1)]
    for peer in peers:
        pl.semaphore_signal(barrier, inc=1, device_id=peer, device_id_type=MESH)

    fetched = pltpu.make_async_copy(coef, solid, load_sem.at[3])
    fetched.start()
    loads = [
        pltpu.make_async_copy(depth, sea0.at[0], load_sem.at[0]),
        pltpu.make_async_copy(mom, sea0.at[1:3], load_sem.at[1]),
        pltpu.make_async_copy(bottom, sea0.at[3], load_sem.at[2])]
    for copy in loads:
        copy.start()

    def face_copy(step, k):
        return pltpu.make_async_remote_copy(
            src_ref=msg.at[step, k], dst_ref=got.at[step, 7 - k],
            send_sem=face_send.at[step, k], recv_sem=face_recv.at[step, 7 - k],
            device_id=at(*OFFSETS[k]), device_id_type=MESH)

    def face_arrival(step, k):
        return pltpu.make_async_remote_copy(
            src_ref=msg.at[step, k], dst_ref=got.at[step, k],
            send_sem=face_send.at[step, k], recv_sem=face_recv.at[step, k],
            device_id=at(*OFFSETS[k]), device_id_type=MESH)

    def row_copy(source_ref, target_ref, sends, recvs, off):
        there = lax.rem(gy + off, n_gy)
        return pltpu.make_async_remote_copy(
            src_ref=source_ref.at[there], dst_ref=target_ref.at[gy],
            send_sem=sends.at[off - 1], recv_sem=recvs.at[off - 1],
            device_id=(gx, there), device_id_type=MESH)

    def row_arrival(source_ref, target_ref, sends, recvs, off):
        origin = lax.rem(gy - off + n_gy, n_gy)
        return pltpu.make_async_remote_copy(
            src_ref=source_ref.at[origin], dst_ref=target_ref.at[origin],
            send_sem=sends.at[off - 1], recv_sem=recvs.at[off - 1],
            device_id=(gx, origin), device_id_type=MESH)

    def halo_copies(top, bot, strip, rows_got, strips_got, corners_got, sends, recvs):
        sources = [
            top.at[:, :, 0:128], top, top.at[:, :, 128:256], strip, strip,
            bot.at[:, :, 0:128], bot, bot.at[:, :, 128:256]]
        targets = [
            corners_got.at[0], rows_got.at[0], corners_got.at[1], strips_got.at[0],
            strips_got.at[1], corners_got.at[2], rows_got.at[1], corners_got.at[3]]
        return [
            pltpu.make_async_remote_copy(
                src_ref=sources[k], dst_ref=targets[k],
                send_sem=sends.at[k], recv_sem=recvs.at[k],
                device_id=at(*OFFSETS[k]), device_id_type=MESH)
            for k in range(8)]

    def by_block(ref):
        tiles = ref[...].reshape(3, 7, 8, BASIS)
        return jnp.concatenate([tiles[d, block] for block in range(7) for d in range(3)], axis=0)

    dcat[...] = lane_triple(by_block(deriv))
    scat[...] = lane_triple(by_block(stiff))
    tpad[...] = jnp.zeros(tpad.shape, F32)
    lpad[...] = jnp.zeros(lpad.shape, F32)
    ipad[...] = jnp.zeros(ipad.shape, F32)
    spad[...] = jnp.zeros(spad.shape, F32)
    ipad[:, 0:FACE_BASIS] = interp[...]
    for face in range(4):
        tpad[face, 0:FACE_BASIS, :] = trace_in[:, face, :]
        lpad[face, 0:FACE_BASIS, :] = lift_in[:, face, :]
    for c in range(3):
        spad[c, 0:FIELDS, 0:FIELDS] = stars[c]
    spad[3, 0:FIELDS, 0:FIELDS] = source[...]
    tcat[...] = lane_triple(tpad[...].reshape(96, BASIS))

    repeat = bits(jnp.right_shift(iota2((104, 16), 0), 3) == iota2((104, 16), 1))
    tall = [[mm(repeat, part).astype(BF16) for part in halves(spad[c])] for c in range(4)]

    def spread(part, columns, starts):
        total = jnp.zeros((104, columns), F32)
        k = iota2((16, columns), 0)
        n = jnp.right_shift(iota2((16, columns), 1), 3)
        for c, start in starts:
            total = total + mm(tall[c][part], bits((n == k + start) & (k < FIELDS)))
        same = jnp.bitwise_and(iota2((104, columns), 0), 7) == jnp.bitwise_and(iota2((104, columns), 1), 7)
        return jnp.where(same, total, 0.0)

    every = [(c, c * FIELDS) for c in range(4)]
    def woven(parts):
        return jnp.concatenate([part[8 * g:8 * g + 8] for g in range(FIELDS) for part in parts], axis=0).astype(BF16)

    kron_parts = [spread(0, 416, every), spread(1, 416, every)]
    kron[...] = woven(kron_parts)
    kron_high[...] = kron_parts[0].astype(BF16)

    def one_hot_face_sends():
        for pair in range(4):
            index = jnp.concatenate([send[2 * pair:2 * pair + 1, :], send[2 * pair + 1:2 * pair + 2, :]], axis=1)
            hot_send[:, pair * 128:(pair + 1) * 128] = one_hot(index, 4 * ELEMENTS)

    def star(x, groups):
        high, low = halves(x)
        both = mm(kron[:, 0:8 * groups], high).reshape(FIELDS, 2, 8, ELEMENTS)
        return both[:, 0] + both[:, 1] + mm(kron_high[:, 0:8 * groups], low).reshape(FIELDS, 8, ELEMENTS)

    def turn(total):
        high = total.astype(BF16).astype(F32)
        both = jnp.concatenate([high, total - high], axis=0).astype(BF16)
        return mm(rotate1[...], both) + mm(rotate2[...], both[0:104])

    def directional(source_ref, weights, with_source, store):
        for h in range(FIELDS):
            q = source_ref[h].reshape(BASIS, ELEMENTS)
            spatial = mm(weights[...], triple(q))
            for block in range(7):
                parts = [spatial[24 * block + 8 * d:24 * block + 8 * d + 8] for d in range(3)]
                for c in range(3):
                    mixed[block, c * FIELDS + h] = (
                        jac[0, c:c + 1, :] * parts[0] + jac[1, c:c + 1, :] * parts[1] + jac[2, c:c + 1, :] * parts[2])
            if with_source:
                mixed[:, 3 * FIELDS + h] = source_ref[h]
        groups = 4 * FIELDS if with_source else 3 * FIELDS
        for block in range(7):
            result = star(mixed[block, 0:groups].reshape(8 * groups, ELEMENTS), groups)
            store(block, result)

    def later_matrices():
        rotate1[...] = woven([spread(0, 208, [(c, 0), (c, FIELDS)]) for c in range(3)])
        rotate2[...] = woven([spread(1, 104, [(c, 0)]) for c in range(3)])
        across = [jnp.concatenate([0.5 * nrm[c, face:face + 1, :] for face in range(4)], axis=1) for c in range(3)]
        across += [jnp.concatenate([0.5 * spd[...]] * 4, axis=1)] * 5
        sides = jnp.concatenate([jnp.broadcast_to(row, (1, 4 * ELEMENTS)) for row in across], axis=0)
        high = sides.astype(BF16).astype(F32)
        found = mm(jnp.concatenate([high, sides - high], axis=0).astype(BF16), hot_send[...])
        slot_side[...] = found[0:8] + found[8:16]
        first = jnp.zeros((BASIS, 192), F32)
        second = jnp.zeros((BASIS, 96), F32)
        for face in range(4):
            same = bits(iota2((BASIS, BASIS), 0) == iota2((BASIS, BASIS), 1))
            high, low = [mm_nt(same, part).astype(BF16) for part in halves(lpad[face])]
            k, n = iota2((24, 192), 0) + 24 * face, iota2((24, 192), 1)
            first = first + mm(high, bits((n == k) | (n == k + 96)))
            second = second + mm(low, bits(iota2((24, 96), 1) == iota2((24, 96), 0) + 24 * face))
        lift1[...] = first.astype(BF16)
        lift2[...] = second.astype(BF16)
        i_high, i_low = halves(ipad[...])
        points = []
        for face in range(4):
            t_high, t_low = halves(tpad[face])
            points.append(mm(i_high, t_high) + mm(i_high, t_low) + mm(i_low, t_high))
        vcat[...] = lane_triple(jnp.concatenate(points, axis=0))

    pick_row = iota2((8, SIDE), 0)
    edge = bits(iota2((8, SIDE), 1) == jnp.where(pick_row < 4, pick_row, pick_row + (SIDE - 8)))

    def strip_of(x):
        high, low = halves(x)
        rest = (x - high.astype(F32) - low.astype(F32)).astype(BF16)
        return mm_nt(edge, high) + mm_nt(edge, low) + mm_nt(edge, rest)

    uh = halo_copies(u_top, u_bot, u_strip, u_row_got, u_strip_got, u_corner_got, uh_send, uh_recv)

    def send_inputs():
        for copy in loads:
            copy.wait()
        for field in range(4):
            u_top[field] = sea0[field, 0:8, :]
            u_bot[field] = sea0[field, SIDE - 8:SIDE, :]
            u_strip[field] = strip_of(sea0[field])
        rows = sea_row[...]
        hits = jnp.where(iota2((n_gy, ELEMENTS), 0) == rows, 1.0, 0.0)
        tri = bits(iota2((ELEMENTS, ELEMENTS), 0) < iota2((ELEMENTS, ELEMENTS), 1))
        before = mm(hits.astype(BF16), tri)
        slot = jnp.sum(before * hits, axis=0, keepdims=True).astype(jnp.int32)
        placed = one_hot(rows * CAP + slot, slots)
        line = iota2((8, ELEMENTS), 0)
        values = jnp.where(line == 0, sea_face[...], jnp.where(
            line == 1, sea_base[0:1, :], sea_base[1:2, :])).astype(F32) + 1.0
        high, low = halves(values)
        found = mm_nt(high, placed) + mm_nt(low, placed)
        for pair in range(n_gy // 2):
            block = found[:, pair * 128:(pair + 1) * 128]
            corner_msg[2 * pair] = block
            corner_msg[2 * pair + 1] = swap_lanes(block)
        for copy in uh:
            copy.start()
        for off in range(1, n_gy):
            row_copy(corner_msg, corner_got, corner_send, corner_recv, off).start()
        corner_got[gy] = corner_msg[gy]
        return found[0:1, :].astype(jnp.int32) - 1

    side8 = low_lanes((8, 128))

    iota16 = iota2((16, 128), 0).astype(jnp.int16)
    one16, zero16 = jnp.ones((16, 128), BF16), jnp.zeros((16, 128), BF16)

    def position_tables():
        for off in range(1, n_gy):
            row_arrival(corner_msg, corner_got, corner_send, corner_recv, off).wait_recv()
        for pair in range(n_gy // 2):
            corner = jnp.where(side8, corner_got[2 * pair], swap_lanes(corner_got[2 * pair + 1])).astype(jnp.int32)
            for hot, line in ((hot_x, 1), (hot_y, 2)):
                apart = jnp.broadcast_to(corner[line:line + 1, :] - 1, (16, 128)).astype(jnp.int16) - iota16
                for tile in range(SIDE // 16):
                    for j in range(4):
                        base = pair * 512 + j * 128
                        hot[16 * tile:16 * tile + 16, base:base + 128] = jnp.where(
                            apart == jnp.int16(16 * tile - j), one16, zero16)

    up_in = gx > 0
    down_in = gx < n_gx - 1
    left_in = gy > 0
    right_in = gy < n_gy - 1

    def place_halo(target, rows_got, strips_got, corners_got, field):
        target[0:8, 0:SIDE] = jnp.where(up_in, rows_got[1, field], 0.0)
        target[8 + SIDE:EXT_X, 0:SIDE] = jnp.where(down_in, rows_got[0, field], 0.0)
        strip = jnp.concatenate([
            jnp.where(right_in, strips_got[0, field], 0.0), jnp.zeros((112, SIDE), F32),
            jnp.where(left_in, strips_got[1, field], 0.0)], axis=0)
        target[8:8 + SIDE, SIDE:EXT_Y] = jnp.transpose(strip)
        target[0:8, SIDE:EXT_Y] = jnp.where(
            side8, jnp.where(up_in & right_in, corners_got[2, field], 0.0),
            jnp.where(up_in & left_in, corners_got[3, field], 0.0))
        target[8 + SIDE:EXT_X, SIDE:EXT_Y] = jnp.where(
            side8, jnp.where(down_in & right_in, corners_got[0, field], 0.0),
            jnp.where(down_in & left_in, corners_got[1, field], 0.0))

    def ocean_first_step():
        for copy in uh:
            copy.wait_recv()
        for field in range(4):
            row = (0, 5, 6, 1)[field]
            wave[row, 8:8 + SIDE, 0:SIDE] = sea0[field]
            place_halo(wave.at[row], u_row_got, u_strip_got, u_corner_got, field)

        def part(begin, rows, inner_from, inner_to):
            span = pl.ds(begin, rows)
            result = shallow_update(wave[0, span, :], wave[5, span, :], wave[6, span, :], wave[1, span, :])
            x = begin + iota2((rows, EXT_Y), 0)
            y = iota2((rows, EXT_Y), 1)
            out = ((x < 8) & (gx == 0)) | ((x >= 8 + SIDE) & (gx == n_gx - 1))
            out = out | ((y >= SIDE) & (y < SIDE + 64) & (gy == n_gy - 1)) | ((y >= SIDE + 64) & (gy == 0))
            for i in range(3):
                wave[2 + i, pl.ds(begin + inner_from, inner_to - inner_from), :] = jnp.where(
                    out, 0.0, result[i])[inner_from:inner_to]

        @pl.loop(0, SIDE // SLAB)
        def _(s):
            part(pl.multiple_of(s * SLAB, 8), SLAB + 16, 8, SLAB + 8)
        part(0, 16, 0, 8)
        part(EXT_X - 16, 16, 8, 16)

    first_factor = step_solid * step_solid / 2
    second_factor = first_factor * step_solid / 3
    table[ROWS // 8 - 1] = jnp.zeros((8, 4 * ELEMENTS), F32)

    one_hot_face_sends()
    later_matrices()
    fetched.wait()
    for step in range(STEPS_DG):
        state = solid

        def store_first(block, value):
            ddt[:, block] = value
        directional(state, dcat, True, store_first)

        def store_second(block, value):
            integral[:, block] = step_solid * state[:, block] - first_factor * ddt[:, block] + second_factor * value
        directional(ddt, dcat, True, store_second)

        for g in range(FIELDS):
            trace = mm(tcat[...], triple(integral[g].reshape(BASIS, ELEMENTS)))
            for face in range(4):
                table[3 * g:3 * g + 3, :, face * ELEMENTS:(face + 1) * ELEMENTS] = (
                    trace[face * 24:(face + 1) * 24].reshape(3, 8, ELEMENTS))
        for tile in range(ROWS // 16):
            high, low = halves(table[2 * tile:2 * tile + 2].reshape(16, 4 * ELEMENTS))
            tsplit[32 * tile:32 * tile + 16] = high
            tsplit[32 * tile + 16:32 * tile + 32] = low

        low_side = low_lanes((HALF, 128))
        middle = 2 * ELEMENTS
        for half in range(2):
            lanes = slice(half * 256, half * 256 + 256)
            picked = (
                mm(tsplit[:, 0:middle], hot_send[0:middle, lanes]) + mm(tsplit[:, middle:], hot_send[middle:, lanes])
            ).reshape(ROWS // 16, 2, 16, 256)
            picked = (picked[:, 0] + picked[:, 1]).reshape(ROWS, 256)
            for pair in range(2):
                block = picked[:, pair * 128:(pair + 1) * 128]
                top, bot = block[0:HALF], block[HALF:ROWS]
                k = 4 * half + 2 * pair
                msg[step, k] = jnp.where(low_side, top, swap_lanes(bot))
                msg[step, k + 1] = jnp.where(low_side, swap_lanes(top), bot)
            if step == 0 and half == 0:
                pl.semaphore_wait(barrier, len(peers))
            for k in range(4 * half, 4 * half + 4):
                face_copy(step, k).start()

        if step == 0:
            slot_code = send_inputs()
            for face in range(4):
                code = partner[face:face + 1, :]
                cols = slice(face * ELEMENTS, (face + 1) * ELEMENTS)
                hot_local[:, cols] = one_hot(code, 4 * ELEMENTS)
                hot_remote[:, cols] = one_hot(code - 4 * ELEMENTS, 8 * 64)
        else:
            hot_slot[...] = one_hot(slot_code, 4 * ELEMENTS)
        for face in range(4):
            cols = slice(face * ELEMENTS, (face + 1) * ELEMENTS)
            local = mm(tsplit[...], hot_local[:, cols])
            local = local.reshape(ROWS // 16, 2, 16, ELEMENTS)
            outer[:, :, cols] = (local[:, 0] + local[:, 1]).reshape(ROWS // 8, 8, ELEMENTS)

        for face in range(4):
            cols = slice(face * ELEMENTS, (face + 1) * ELEMENTS)
            normal = [0.5 * nrm[c, face:face + 1, :] for c in range(3)]
            speed = 0.5 * spd[...]
            for block in range(3):
                ids = [3 * g + block for g in range(FIELDS)]
                turned = turn(jnp.concatenate([table[n, :, cols] + outer[n, :, cols] for n in ids], axis=0))
                for g in range(FIELDS):
                    value = speed * (table[ids[g], :, cols] - outer[ids[g], :, cols])
                    for c in range(3):
                        value = value + normal[c] * turned[24 * g + 8 * c:24 * g + 8 * c + 8]
                    flux[g, face, block] = value

        def store_volume(block, value):
            volume[:, block] = value
        directional(integral, scat, False, store_volume)
        if step == 1:
            position_tables()

        for k in range(8):
            face_arrival(step, k).wait_recv()
        for pair in range(4):
            a, b = got[step, 2 * pair], got[step, 2 * pair + 1]
            cols = slice(pair * 128, (pair + 1) * 128)
            arrived[0:HALF // 8, :, cols] = jnp.where(low_side, a, swap_lanes(b)).reshape(HALF // 8, 8, 128)
            arrived[HALF // 8:, :, cols] = jnp.where(low_side, swap_lanes(a), b).reshape(HALF // 8, 8, 128)
        for side in range(2):
            lanes = slice(side * 256, side * 256 + 256)
            normal = [slot_side[c:c + 1, lanes] for c in range(3)]
            speed = slot_side[3:4, lanes]
            for block in range(3):
                ids = [3 * g + block for g in range(FIELDS)]
                turned = turn(jnp.concatenate([arrived[n, :, lanes] for n in ids], axis=0))
                for g in range(FIELDS):
                    value = -speed * arrived[ids[g], :, lanes]
                    for c in range(3):
                        value = value + normal[c] * turned[24 * g + 8 * c:24 * g + 8 * c + 8]
                    arrived[ids[g], :, lanes] = value
        for tile in range(ROWS // 16):
            high, low = halves(arrived[2 * tile:2 * tile + 2].reshape(16, 512))
            tsplit[32 * tile:32 * tile + 16, 0:512] = high
            tsplit[32 * tile + 16:32 * tile + 32, 0:512] = low
        for face in range(4):
            cols = slice(face * ELEMENTS, (face + 1) * ELEMENTS)
            remote = mm(tsplit[:, 0:512], hot_remote[:, cols]).reshape(ROWS // 16, 2, 16, ELEMENTS)
            remote = (remote[:, 0] + remote[:, 1]).reshape(ROWS // 8, 8, ELEMENTS)
            for g in range(FIELDS):
                for block in range(3):
                    flux[g, face, block] = flux[g, face, block] + remote[3 * g + block]
        for g in range(FIELDS):
            f = flux[g].reshape(96, ELEMENTS)
            high = f.astype(BF16).astype(F32)
            both = jnp.concatenate([high, f - high], axis=0).astype(BF16)
            lifted = mm(lift1[...], both) + mm(lift2[...], both[0:96])
            solid[g] = state[g] + volume[g] - lifted.reshape(7, 8, ELEMENTS)

    point = mm(vcat[...], triple(solid[vertical_field].reshape(BASIS, ELEMENTS)))
    points = jnp.concatenate([point[16 * f:16 * f + 16] for f in range(4)], axis=1)
    high = points.astype(BF16).astype(F32)
    both = jnp.concatenate([high, points - high], axis=0).astype(BF16)
    rates = mm(both, hot_slot[...])
    rates = rates[0:16] + rates[16:32]
    for pair in range(n_gy // 2):
        a = rates[0:8, pair * 128:(pair + 1) * 128]
        b = rates[8:16, pair * 128:(pair + 1) * 128]
        rate_msg[2 * pair] = jnp.where(side8, a, swap_lanes(b))
        rate_msg[2 * pair + 1] = jnp.where(side8, swap_lanes(a), b)
    for off in range(1, n_gy):
        row_copy(rate_msg, rate_got, rate_send, rate_recv, off).start()
    rate_got[gy] = rate_msg[gy]
    saved = pltpu.make_async_copy(solid, solid_out, store_sem.at[0])
    saved.start()

    ocean_first_step()

    for off in range(1, n_gy):
        row_arrival(rate_msg, rate_got, rate_send, rate_recv, off).wait_recv()
    edge_row = jnp.where(iota2((16, 128), 0) < 8, iota2((16, 128), 0), iota2((16, 128), 0) + (SIDE - 16))
    edge_col = jnp.where(iota2((8, 128), 0) < 4, iota2((8, 128), 0), iota2((8, 128), 0) + (SIDE - 8))
    pairs = []
    for pair in range(n_gy // 2):
        corner = jnp.where(side8, corner_got[2 * pair], swap_lanes(corner_got[2 * pair + 1])).astype(jnp.int32)
        a, b = rate_got[2 * pair], rate_got[2 * pair + 1]
        first = jnp.where(side8, a, swap_lanes(b))
        second = jnp.where(side8, swap_lanes(a), b)
        rate = [[first[j:j + 1] for j in range(4)], [first[4 + j:5 + j] for j in range(4)],
                [second[j:j + 1] for j in range(4)], [second[4 + j:5 + j] for j in range(4)]]
        pairs.append((corner, rate))

    def chosen(masks, values):
        return jnp.where(masks[0], values[0], jnp.where(masks[1], values[1], jnp.where(
            masks[2], values[2], jnp.where(masks[3], values[3], 0.0))))

    row_parts = [[None] * len(pairs) for _ in range(4)]
    col_parts = [[None] * len(pairs) for _ in range(4)]
    for index, (corner, rate) in enumerate(pairs):
        apart_x = edge_row + 1 - corner[1:2, :]
        apart_y = edge_col + 1 - corner[2:3, :]
        masks_x = [apart_x == i for i in range(4)]
        masks_y = [apart_y == i for i in range(4)]
        for j in range(4):
            row_parts[j][index] = chosen(masks_x, [rate[i][j] for i in range(4)])
            col_parts[j][index] = chosen(masks_y, [rate[j][i] for i in range(4)])

    def summed(parts, table_ref):
        stacked = []
        for row in parts:
            whole = jnp.concatenate(row, axis=1)
            high = whole.astype(BF16).astype(F32)
            stacked += [high, whole - high]
        stacked = jnp.concatenate(stacked, axis=0).astype(BF16)
        places = jnp.concatenate([table_ref[:, pair * 512:pair * 512 + 128] for pair in range(n_gy // 2)], axis=1)
        result = mm_nt(stacked, places)
        count = parts[0][0].shape[0]
        total = result[0:count] + result[count:2 * count]
        for shift in range(1, 4):
            begin = 2 * count * shift
            moved = result[begin:begin + count] + result[begin + count:begin + 2 * count]
            total = total + pltpu.roll(moved, shift, 1)
        return total

    edge_rows = summed(row_parts, hot_y)
    f_top[0] = edge_rows[0:8]
    f_bot[0] = edge_rows[8:16]
    f_strip[0] = summed(col_parts, hot_x)
    fh = halo_copies(f_top, f_bot, f_strip, f_row_got, f_strip_got, f_corner_got, fh_send, fh_recv)
    for copy in fh:
        copy.start()

    force_ext[8:8 + SIDE, 0:SIDE] = jnp.zeros((SIDE, SIDE), F32)

    @pl.loop(0, n_gy // 2, unroll=2)
    def _(pair):
        corner = jnp.where(side8, corner_got[2 * pair], swap_lanes(corner_got[2 * pair + 1])).astype(jnp.int32)
        a, b = rate_got[2 * pair], rate_got[2 * pair + 1]
        first = jnp.where(side8, a, swap_lanes(b))
        second = jnp.where(side8, swap_lanes(a), b)
        wide = []
        for line in [first[i:i + 1] for i in range(8)] + [second[i:i + 1] for i in range(8)]:
            wide.append(halves(jnp.broadcast_to(line, (16, 128))))
        apart = jnp.broadcast_to(corner[1:2, :] - 1, (16, 128)).astype(jnp.int16) - iota16
        columns = [[] for _ in range(4)]
        for tile in range(SIDE // 16):
            masks = [apart == jnp.int16(16 * tile - i) for i in range(4)]
            for j in range(4):
                for part in range(2):
                    value = zero16
                    for i in range(4):
                        value = jnp.where(masks[i], wide[4 * i + j][part], value)
                    columns[j].append(value)
        total = jnp.zeros((2 * SIDE, SIDE), F32)
        for half in range(2):
            table_part = hot_y[:, pl.ds(pl.multiple_of(pair * 512 + half * 256, 256), 256)]
            left = jnp.concatenate([jnp.concatenate(columns[2 * half + j], axis=0) for j in range(2)], axis=1)
            total = total + mm_nt(left, table_part)
        total = total.reshape(SIDE // 16, 2, 16, SIDE)
        total = (total[:, 0] + total[:, 1]).reshape(SIDE, SIDE)
        force_ext[8:8 + SIDE, 0:SIDE] = force_ext[8:8 + SIDE, 0:SIDE] + total

    for copy in fh:
        copy.wait_recv()
    place_halo(force_ext, f_row_got, f_strip_got, f_corner_got, 0)

    stores = []
    for piece in range(SIDE // SLAB):
        begin = piece * SLAB
        span = slice(begin, begin + SLAB + 16)
        inner = slice(begin, begin + SLAB)
        lift = force_ext[span, :]
        depth_0 = wave[0, span, :]
        slope_x, slope_y = slopes(lift)
        scale = 0.5 * step_ocean * step_ocean
        mom_x = wave[3, span, :] - scale * (depth_0 * slope_x)
        mom_y = wave[4, span, :] - scale * (depth_0 * slope_y)
        b = wave[1, span, :] + (2 * step_ocean) * lift
        result = shallow_update(wave[2, span, :], mom_x, mom_y, b)
        for i in range(3):
            ocean[i, inner, :] = result[i][8:SLAB + 8, 0:SIDE]
        bed[inner, :] = b[8:SLAB + 8, 0:SIDE]
        stores.append(pltpu.make_async_copy(ocean.at[:, inner], ocean_out.at[:, inner], ocean_sem.at[0, piece]))
        stores.append(pltpu.make_async_copy(bed.at[inner], bed_out.at[inner], ocean_sem.at[1, piece]))
        for copy in stores[-2:]:
            copy.start()

    saved.wait()
    for copy in stores:
        copy.wait()
    for copy in uh + fh:
        copy.wait_send()
    for off in range(1, n_gy):
        row_copy(corner_msg, corner_got, corner_send, corner_recv, off).wait_send()
        row_copy(rate_msg, rate_got, rate_send, rate_recv, off).wait_send()
    for step in range(STEPS_DG):
        for k in range(8):
            face_copy(step, k).wait_send()


SLAB = 64


def hand_over(solid_in, ocean_in, bed_in, solid_out, ocean_out, bed_out, solid, ocean, bed, in_sems, out_sems):
    parts = [(solid_in.at[g:g + 4], solid.at[g:g + 4], solid_out.at[g:g + 4]) for g in range(0, 12, 4)]
    parts += [(solid_in.at[12:13], solid.at[12:13], solid_out.at[12:13])]
    parts += [(ocean_in.at[i], ocean.at[i], ocean_out.at[i]) for i in range(3)]
    parts += [(bed_in, bed, bed_out)]
    fetches = [pltpu.make_async_copy(part[0], part[1], in_sems.at[n]) for n, part in enumerate(parts)]
    stores = [pltpu.make_async_copy(part[1], part[2], out_sems.at[n]) for n, part in enumerate(parts)]
    for copy in fetches:
        copy.start()
    for fetch, store in zip(fetches, stores):
        fetch.wait()
        store.start()
    for copy in stores:
        copy.wait()


def per_device(
    n_gx, n_gy,
    coefficients, jacobian, face_normals, wave_speed, star_mats, deriv_mats, stiff_mats, source_mat,
    trace_mats, lift_mats, face_partner, send_faces, sea_face, sea_row, sea_base, interp_mat,
    water_depth, momentum, bottom,
):
    vm = pl.BlockSpec(memory_space=pltpu.VMEM)
    anywhere = pl.BlockSpec(memory_space=pl.ANY)
    slots = n_gy * CAP
    whole = (FIELDS, 7, 8, ELEMENTS)
    floats = lambda *shape: pltpu.VMEM(shape, F32)
    shorts = lambda *shape: pltpu.VMEM(shape, BF16)
    dma = pltpu.SemaphoreType.DMA
    scratch = [
        floats(*whole),
        floats(7, EXT_X, EXT_Y),
        floats(EXT_X, EXT_Y),
        floats(3, SIDE, SIDE),
        floats(SIDE, SIDE),
        floats(4, SIDE, SIDE),
        floats(4, 24, BASIS),
        floats(4, 24, BASIS),
        floats(16, 24),
        floats(4, 16, 16),
        shorts(168, 168),
        shorts(168, 168),
        shorts(96, 168),
        shorts(64, 168),
        shorts(56, 192),
        shorts(56, 96),
        shorts(208, 416),
        shorts(104, 416),
        shorts(312, 208),
        shorts(312, 104),
        floats(*whole),
        floats(*whole),
        floats(7, 4 * FIELDS, 8, ELEMENTS),
        floats(ROWS // 8, 8, 4 * ELEMENTS),
        shorts(2 * ROWS, 4 * ELEMENTS),
        floats(ROWS // 8, 8, 4 * ELEMENTS),
        floats(FIELDS, 4, 3, 8, ELEMENTS),
        floats(*whole),
        floats(ROWS // 8, 8, 512),
        floats(8, 512),
        shorts(4 * ELEMENTS, 512),
        shorts(4 * ELEMENTS, 4 * ELEMENTS),
        shorts(512, 4 * ELEMENTS),
        shorts(4 * ELEMENTS, slots),
        shorts(SIDE, 4 * slots),
        shorts(SIDE, 4 * slots),
        floats(STEPS_DG, 8, HALF, 128),
        floats(STEPS_DG, 8, HALF, 128),
        floats(n_gy, 8, 128),
        floats(n_gy, 8, 128),
        floats(n_gy, 8, 128),
        floats(n_gy, 8, 128),
        floats(4, 8, SIDE),
        floats(4, 8, SIDE),
        floats(4, 8, SIDE),
        floats(2, 4, 8, SIDE),
        floats(2, 4, 8, SIDE),
        floats(4, 4, 8, 128),
        floats(1, 8, SIDE),
        floats(1, 8, SIDE),
        floats(1, 8, SIDE),
        floats(2, 1, 8, SIDE),
        floats(2, 1, 8, SIDE),
        floats(4, 1, 8, 128),
        dma((4,)), dma((2,)), dma((2, SIDE // SLAB)),
        dma((STEPS_DG, 8)), dma((STEPS_DG, 8)),
        dma((n_gy - 1,)), dma((n_gy - 1,)), dma((n_gy - 1,)), dma((n_gy - 1,)),
        dma((8,)), dma((8,)), dma((8,)), dma((8,)),
    ]
    results = (
        jax.ShapeDtypeStruct(whole, F32),
        jax.ShapeDtypeStruct((3, SIDE, SIDE), F32),
        jax.ShapeDtypeStruct((SIDE, SIDE), F32))
    made = pl.pallas_call(
        functools.partial(solid_kernel, n_gx, n_gy),
        out_shape=results,
        in_specs=[anywhere] + [vm] * 15 + [anywhere] * 3,
        out_specs=(anywhere,) * 3,
        scratch_shapes=scratch,
        compiler_params=pltpu.CompilerParams(
            collective_id=0, has_side_effects=True, vmem_limit_bytes=60 * 1024 * 1024),
        name="solid",
    )(
        coefficients.reshape(whole), jacobian, face_normals.transpose(1, 0, 2), wave_speed.reshape(1, ELEMENTS),
        deriv_mats, stiff_mats, trace_mats.transpose(1, 0, 2), lift_mats.transpose(2, 0, 1), interp_mat, star_mats, source_mat, face_partner, send_faces,
        sea_face.reshape(1, ELEMENTS), sea_row.reshape(1, ELEMENTS), sea_base.T,
        water_depth, momentum, bottom)
    solid, ocean, bed = pl.pallas_call(
        hand_over,
        out_shape=results,
        in_specs=[anywhere] * 3,
        out_specs=(anywhere,) * 3,
        scratch_shapes=[floats(*whole), floats(3, SIDE, SIDE), floats(SIDE, SIDE), dma((8,)), dma((8,))],
        name="hand_over",
    )(*made)
    return solid.reshape(FIELDS, BASIS, ELEMENTS), ocean, bed


def solution(mesh):
    in_specs = (
        P(None, None, ("gx", "gy")),
        P(None, None, ("gx", "gy")),
        P(None, None, ("gx", "gy")),
        P(("gx", "gy")),
        P(),
        P(),
        P(),
        P(),
        P(),
        P(),
        P(None, ("gx", "gy")),
        P(None, ("gx", "gy")),
        P(("gx", "gy")),
        P(("gx", "gy"), None),
        P(("gx", "gy"), None),
        P(),
        P("gx", "gy"),
        P(None, "gx", "gy"),
        P("gx", "gy"),
    )
    out_specs = (P(None, None, ("gx", "gy")), P(None, "gx", "gy"), P("gx", "gy"))
    return jax.shard_map(
        functools.partial(per_device, mesh.shape["gx"], mesh.shape["gy"]),
        mesh=mesh, in_specs=in_specs, out_specs=out_specs, check_vma=False,
    )
```
